128 devices in a mesh: cells: 32 (over y, z, core), tiles: 4 (over x).
Axes of the slice: x: 4, y: 4, z: 4, core: 2. Of those that a mesh axis runs over, the one named last changes fastest.
Arguments:
- embeddings: bfloat16 [3, 32768, 256], P(None, 'cells'), may hold values from -6 to 6
- log_mass: float32 [3, 32768], P(None, 'cells'), may hold values from -1 to 1
- signatures: bfloat16 [32768, 256], P('cells'), may hold values from -6 to 6
- tile_list: int32 [2, 2, 4096], P(None, None, ('cells', 'tiles')), may hold values from -1 to 255, as said below
Outputs:
- early_fates: bfloat16 [32768, 256], P('cells')
- late_fates: bfloat16 [32768, 256], P('cells')
The draws below stay inside these ranges and needn't reach their ends.
Inputs may be any that keep to these rules, and one draw needn't show every extreme that they name: `tile_list`: for each coupling, slots c * 128 to c * 128 + 127 belong to owner c (an index of cells). A live slot holds a source block of owner c (blocks c * 8 to c * 8 + 7) and a target block of owner c - 1, c or c + 1; an empty slot holds -1 in both rows. Within the slots of each device the live ones come first. No pair of blocks appears twice in a coupling, every source block and every target block appears in some live slot, and one owner in each coupling has all 128 slots live.
All inputs are finite; a program needn't handle non-finite values.
Results may differ from the reference program's by a relative error of at most 0.006.
Values may be sent and summed in bfloat16 or wider, within the bound.
No kernel may reach another device: no remote copies, remote signals or barrier semaphores. Data moves between devices by JAX's collectives and lax.ppermute only.
A program may use at most 64 MiB of HBM per device.

```python
import jax
import jax.numpy as jnp
from jax import lax

EMB = 256
FATE = 256
BLOCK = 128
SWEEPS = 2
NBLK = 8
TILE_CAP = 128
CELLS = 32768
BLOCKS = 256
N_CELLS = 32
N_TILES = 4


def owner_slots(owner_key, owner_index, live_count):
    pair_index = jnp.arange(NBLK * 3 * NBLK, dtype=jnp.int32)
    source_local = pair_index // (3 * NBLK)
    window_block = pair_index % (3 * NBLK)
    target_owner = owner_index - 1 + window_block // NBLK
    inside = (target_owner >= 0) & (target_owner < N_CELLS)
    diagonal = window_block == NBLK + source_local
    noise = jax.random.randint(owner_key, pair_index.shape, 0, 65536, dtype=jnp.int32)
    scores = noise * (3 * NBLK * NBLK) + pair_index
    scores = jnp.where(diagonal, scores + 536870912, scores)
    scores = jnp.where(inside, scores, -1 - pair_index)
    ranked = jnp.argsort(-scores)[:TILE_CAP]
    rank_index = jnp.arange(TILE_CAP, dtype=jnp.int32)
    live_mask = rank_index < live_count
    sources = jnp.where(live_mask, owner_index * NBLK + source_local[ranked], -1)
    targets = jnp.where(live_mask, (owner_index - 1) * NBLK + window_block[ranked], -1)
    share = TILE_CAP // N_TILES
    placed = rank_index % share * N_TILES + rank_index // share
    return jnp.stack([sources[placed], targets[placed]])


def draw_tile_list(key, part):
    listings = []
    for coupling in range(2):
        coupling_key = jax.random.fold_in(key, coupling + 11)
        busy_key, count_key, order_key = jax.random.split(coupling_key, 3)
        busiest = jax.random.randint(busy_key, (), 0, N_CELLS, dtype=jnp.int32)
        counts = jax.random.randint(count_key, (N_CELLS,), NBLK, 3 * TILE_CAP // 4 + 1, dtype=jnp.int32)
        owners = jnp.arange(N_CELLS, dtype=jnp.int32)
        counts = jnp.where(owners == busiest, TILE_CAP, counts)
        owner_keys = jax.random.split(order_key, N_CELLS)
        slots = jax.vmap(owner_slots)(owner_keys, owners, counts)
        listings.append(jnp.transpose(slots, (1, 0, 2)).reshape(2, N_CELLS * TILE_CAP))
    return jnp.stack(listings)


def block_scale(own_key, shape, pieces, low, largest):
    factor_of, own = 1.0, jax.random.fold_in(own_key, 6)
    for position, parts in pieces:
        steps = jnp.exp(jax.random.uniform(jax.random.fold_in(own, position), (parts,), jnp.float32, low / len(pieces), largest / len(pieces)))
        factor_of = factor_of * jnp.repeat(steps, shape[position] // parts).reshape([-1 if axis == position else 1 for axis in range(len(shape))])
    return factor_of


def scatter_about(stream_key, extent, scale, reach, pieces=(), held_as=jnp.bfloat16):
    gain = block_scale(stream_key, extent, pieces, -0.22, 0.18) if pieces else 1.0
    values = jax.random.normal(stream_key, extent, jnp.float32) * scale * gain
    return jnp.minimum(jnp.maximum(values, -reach), reach).astype(held_as)


def setup_inputs(seed: int = 0) -> dict:
    streams_of = jax.random.split(jax.random.key(seed), 5)
    return {
        "embeddings": scatter_about(streams_of[0], (3, CELLS, EMB), 1.0, 6.0, ((1, 32),)),
        "log_mass": jnp.clip(jax.random.uniform(streams_of[1], (3, CELLS), jnp.float32, -1.0, 1.0) * block_scale(streams_of[1], (3, CELLS), ((1, 32),), -0.4, 0.0), -1.0, 1.0),
        "signatures": scatter_about(streams_of[2], (CELLS, FATE), 1.0, 6.0, ((0, 32),)),
        "tile_list": draw_tile_list(jax.random.fold_in(streams_of[4], 71), 0),
    }


EPS = 0.01
RHO = 1.0
NEG = -1.0e30


def block_cost(source_rows, target_rows, source_norm, target_norm):
    crossed = jnp.dot(source_rows, target_rows.T, preferred_element_type=jnp.float32)
    return (source_norm[:, None] + target_norm[None, :] - 2.0 * crossed) / EMB


def merge_pair(first_pair, second_pair):
    highest = jnp.maximum(first_pair[0], second_pair[0])
    summed = first_pair[1] * jnp.exp(first_pair[0] - highest) + second_pair[1] * jnp.exp(second_pair[0] - highest)
    return highest, summed


def unchanged(carried, entry):
    return carried


def row_lse(sources, source_norm, targets, target_norm, target_terms, listing):
    def active_tile(carried, entry):
        highest, summed = carried
        costs = block_cost(sources[entry[0]], targets[entry[1]], source_norm[entry[0]], target_norm[entry[1]])
        scores = target_terms[entry[1]][None, :] - costs / EPS
        maxima = jnp.max(scores, axis=1)
        masses = jnp.sum(jnp.exp(scores - maxima[:, None]), axis=1)
        merged = merge_pair((highest[entry[0]], summed[entry[0]]), (maxima, masses))
        return highest.at[entry[0]].set(merged[0]), summed.at[entry[0]].set(merged[1])

    def advance(carried, entry):
        return lax.cond(entry[0] >= 0, active_tile, unchanged, carried, entry), None

    starting = (jnp.full(source_norm.shape, NEG, jnp.float32), jnp.zeros(source_norm.shape, jnp.float32))
    (highest, summed), ignored = lax.scan(advance, starting, listing.T)
    return highest + jnp.log(summed)


def col_lse(sources, source_norm, targets, target_norm, source_terms, listing):
    def active_tile(carried, entry):
        highest, summed = carried
        costs = block_cost(sources[entry[0]], targets[entry[1]], source_norm[entry[0]], target_norm[entry[1]])
        scores = source_terms[entry[0]][:, None] - costs / EPS
        maxima = jnp.max(scores, axis=0)
        masses = jnp.sum(jnp.exp(scores - maxima[None, :]), axis=0)
        merged = merge_pair((highest[entry[1]], summed[entry[1]]), (maxima, masses))
        return highest.at[entry[1]].set(merged[0]), summed.at[entry[1]].set(merged[1])

    def advance(carried, entry):
        return lax.cond(entry[0] >= 0, active_tile, unchanged, carried, entry), None

    starting = (jnp.full(target_norm.shape, NEG, jnp.float32), jnp.zeros(target_norm.shape, jnp.float32))
    (highest, summed), ignored = lax.scan(advance, starting, listing.T)
    return highest + jnp.log(summed)


def potentials(sources, targets, log_source, log_target, listing):
    source_norm = jnp.sum(sources * sources, axis=2)
    target_norm = jnp.sum(targets * targets, axis=2)
    damping = RHO / (RHO + EPS)
    potential = jnp.zeros(log_target.shape, jnp.float32)
    for sweep_index in range(SWEEPS):
        target_terms = potential / EPS + log_target
        log_total = row_lse(sources, source_norm, targets, target_norm, target_terms, listing)
        source_terms = (-damping * EPS * log_total) / EPS + log_source
        potential = -damping * EPS * col_lse(sources, source_norm, targets, target_norm, source_terms, listing)
    target_terms = potential / EPS + log_target
    log_total = row_lse(sources, source_norm, targets, target_norm, target_terms, listing)
    return target_terms, log_total


def pull(sources, targets, target_terms, log_total, listing, fate_blocks):
    source_norm = jnp.sum(sources * sources, axis=2)
    target_norm = jnp.sum(targets * targets, axis=2)

    def active_tile(carried, entry):
        costs = block_cost(sources[entry[0]], targets[entry[1]], source_norm[entry[0]], target_norm[entry[1]])
        scores = target_terms[entry[1]][None, :] - costs / EPS
        weights = jnp.exp(scores - log_total[entry[0]][:, None]).astype(jnp.bfloat16)
        product_part = jnp.dot(weights, fate_blocks[entry[1]], preferred_element_type=jnp.float32)
        return carried.at[entry[0]].add(product_part)

    def advance(carried, entry):
        return lax.cond(entry[0] >= 0, active_tile, unchanged, carried, entry), None

    starting = jnp.zeros((BLOCKS, BLOCK, fate_blocks.shape[2]), jnp.float32)
    accumulated, ignored = lax.scan(advance, starting, listing.T)
    return accumulated.reshape(-1, fate_blocks.shape[2]).astype(jnp.bfloat16)


def reference(embeddings, log_mass, signatures, tile_list):
    moments = [embeddings[moment].astype(jnp.float32).reshape(BLOCKS, BLOCK, EMB) for moment in range(3)]
    log_blocks = [log_mass[moment].reshape(BLOCKS, BLOCK) for moment in range(3)]
    states = [potentials(moments[coupling], moments[coupling + 1], log_blocks[coupling], log_blocks[coupling + 1], tile_list[coupling]) for coupling in range(2)]
    late = pull(moments[1], moments[2], states[1][0], states[1][1], tile_list[1], signatures.reshape(BLOCKS, BLOCK, FATE))
    early = pull(moments[0], moments[1], states[0][0], states[0][1], tile_list[0], late.reshape(BLOCKS, BLOCK, FATE))
    return early, late
```

```python
import jax
import jax.numpy as jnp
from jax import lax
from jax.experimental import pallas as pl
from jax.experimental.pallas import tpu as pltpu
from jax.sharding import PartitionSpec as P

EMB = 256
BLOCK = 128
NBLK = 8
WIN = 3 * NBLK
CELLS = NBLK * BLOCK
EPS = 0.01
RHO = 1.0
LAM = RHO / (RHO + EPS)
INV = 1.0 / (EMB * EPS)
BIG = 1e30

ROW_LIST = 0
COL_LIST = 384
ROW_COUNT = 768
COL_COUNT = 784
TABLE = 1024

VMEM = pl.BlockSpec(memory_space=pltpu.VMEM)
SMEM = pl.BlockSpec(memory_space=pltpu.SMEM)


def sibling(value):
    return lax.ppermute(value, "cells", [(c, c ^ 1) for c in range(lax.axis_size("cells"))])


def outward(value):
    count = lax.axis_size("cells")
    pairs = [(c, (c + 1 if c % 2 else c - 1) % count) for c in range(count)]
    return lax.ppermute(value, "cells", pairs)


def mirrored(value):
    count = lax.axis_size("tiles")
    return lax.ppermute(value, "tiles", [(t, count - 1 - t) for t in range(count)])


def call(kernel, outs, out_specs, in_specs, scratch=(), flops=10**9, mib=40):
    return pl.pallas_call(
        kernel,
        out_shape=outs,
        in_specs=in_specs,
        out_specs=out_specs,
        scratch_shapes=list(scratch),
        compiler_params=pltpu.CompilerParams(vmem_limit_bytes=mib << 20),
        cost_estimate=pl.CostEstimate(flops=flops, bytes_accessed=4 << 20, transcendentals=1 << 21),
    )


def table_kernel(owner_ref, slots_ref, table_ref):
    owner = owner_ref[0]
    for coupling in range(2):

        @pl.loop(0, NBLK)
        def _(i):
            table_ref[ROW_COUNT + coupling * NBLK + i] = 0

        @pl.loop(0, WIN)
        def _(i):
            table_ref[COL_COUNT + coupling * WIN + i] = 0

        @pl.loop(0, 128)
        def _(slot):
            part, rest = slot // 32, slot % 32
            at = part * 128 + coupling * 64 + rest
            source = slots_ref[at]

            @pl.when(source >= 0)
            def _():
                target = slots_ref[at + 32]
                s = source - owner * NBLK
                away = target // NBLK
                region = jnp.where(away == owner, 0, jnp.where(away == (owner ^ 1), 1, 2))
                t = region * NBLK + target % NBLK
                row = ROW_COUNT + coupling * NBLK + s
                col = COL_COUNT + coupling * WIN + t
                n = table_ref[row]
                table_ref[ROW_LIST + (coupling * NBLK + s) * WIN + n] = t
                table_ref[row] = n + 1
                k = table_ref[col]
                table_ref[COL_LIST + (coupling * WIN + t) * NBLK + k] = s
                table_ref[col] = k + 1


def products(source_ref, target_refs, g_ref):
    for region, target_ref in enumerate(target_refs):

        @pl.loop(0, NBLK // 2)
        def _(pair):
            rows = target_ref[pl.ds(pl.multiple_of(pair * 256, 256), 256), :]
            g = lax.dot_general(
                source_ref[...], rows, (((1,), (1,)), ((), ())), preferred_element_type=jnp.float32
            ) * (2.0 * INV)
            g_ref[region * NBLK + 2 * pair] = g[:, :BLOCK]
            g_ref[region * NBLK + 2 * pair + 1] = g[:, BLOCK:]


def row_of(ref, index):
    return ref[pl.ds(index, 1), :]


def row_maximum(table_ref, coupling, s, hh_ref, g_ref):
    rows = pl.ds(pl.multiple_of(s * BLOCK, BLOCK), BLOCK)
    count = table_ref[ROW_COUNT + coupling * NBLK + s]
    base = ROW_LIST + (coupling * NBLK + s) * WIN

    def step(p, highest):
        t = table_ref[base + p]
        return jnp.maximum(highest, g_ref[t, rows, :] + row_of(hh_ref, t))

    highest = lax.fori_loop(0, count, step, jnp.full((BLOCK, BLOCK), -BIG, jnp.float32))
    return rows, count, base, jnp.max(highest, axis=1, keepdims=True)


def scale_kernel(table_ref, coupling, hh_ref, kc_ref, g_ref, part_ref, uu_ref):
    @pl.loop(0, NBLK)
    def _(s):
        rows, count, base, m = row_maximum(table_ref, coupling, s, hh_ref, g_ref)

        def step(p, acc):
            t = table_ref[base + p]
            return acc + jnp.exp(g_ref[t, rows, :] + row_of(hh_ref, t) - m)

        acc = lax.fori_loop(0, count, step, jnp.zeros((BLOCK, BLOCK), jnp.float32))
        total = m + jnp.log(jnp.sum(acc, axis=1, keepdims=True))
        kc = jnp.broadcast_to(row_of(kc_ref, s), (BLOCK, BLOCK)).T
        uu_ref[s] = kc - LAM * total

    @pl.loop(0, WIN)
    def _(t):
        count = table_ref[COL_COUNT + coupling * WIN + t]
        base = COL_LIST + (coupling * WIN + t) * NBLK

        def score(p):
            s = table_ref[base + p]
            return g_ref[t, pl.ds(pl.multiple_of(s * BLOCK, BLOCK), BLOCK), :] + uu_ref[s]

        def highest_step(p, highest):
            return jnp.maximum(highest, jnp.max(score(p).reshape(16, 8, BLOCK), axis=0))

        highest = lax.fori_loop(0, count, highest_step, jnp.full((8, BLOCK), -BIG, jnp.float32))
        m = jnp.max(highest, axis=0, keepdims=True)

        def step(p, acc):
            return acc + jnp.sum(jnp.exp(score(p) - m).reshape(16, 8, BLOCK), axis=0)

        acc = lax.fori_loop(0, count, step, jnp.zeros((8, BLOCK), jnp.float32))
        part_ref[0, pl.ds(t, 1), :] = m
        part_ref[1, pl.ds(t, 1), :] = jnp.sum(acc, axis=0, keepdims=True)


def weigh(table_ref, coupling, hh_ref, g_ref, w_ref, sum_ref):
    @pl.loop(0, NBLK)
    def _(s):
        rows, count, base, m = row_maximum(table_ref, coupling, s, hh_ref, g_ref)
        w_ref[rows, :] = jnp.zeros((BLOCK, WIN * BLOCK), jnp.bfloat16)

        def step(p, acc):
            t = table_ref[base + p]
            e = jnp.exp(g_ref[t, rows, :] + row_of(hh_ref, t) - m)
            w_ref[rows, pl.ds(pl.multiple_of(t * BLOCK, BLOCK), BLOCK)] = e.astype(jnp.bfloat16)
            return acc + e

        acc = lax.fori_loop(0, count, step, jnp.zeros((BLOCK, BLOCK), jnp.float32))
        sum_ref[rows, :] = jnp.broadcast_to(jnp.sum(acc, axis=1, keepdims=True), (BLOCK, BLOCK))


def pull(w_ref, sum_ref, fate_refs, out_ref):
    @pl.loop(0, 4)
    def _(chunk):
        rows = pl.ds(pl.multiple_of(chunk * 256, 256), 256)
        total = jnp.zeros((256, out_ref.shape[1]), jnp.float32)
        for region, fate_ref in enumerate(fate_refs):
            total += jnp.dot(
                w_ref[rows, region * CELLS : (region + 1) * CELLS],
                fate_ref[...],
                preferred_element_type=jnp.float32,
            )
        inverse = 1.0 / sum_ref[rows, :]
        out_ref[rows, :] = (total * jnp.concatenate([inverse, inverse], axis=1)).astype(jnp.bfloat16)


def first_kernel(group_ref, table_ref, source_ref, own_ref, sib_ref, out_ref, hh_ref, kc_ref, g_ref, part_ref, uu_ref):
    products(source_ref, (own_ref, sib_ref, out_ref), g_ref)
    scale_kernel(table_ref, group_ref[0], hh_ref, kc_ref, g_ref, part_ref, uu_ref)


def second_kernel(group_ref, table_ref, hh_ref, kc_ref, g_ref, part_ref, uu_ref):
    scale_kernel(table_ref, group_ref[0], hh_ref, kc_ref, g_ref, part_ref, uu_ref)


def products_kernel(source_ref, own_ref, sib_ref, out_ref, g_ref):
    products(source_ref, (own_ref, sib_ref, out_ref), g_ref)


def late_kernel(group_ref, table_ref, hh_ref, g_ref, other_ref, own_ref, sib_ref, out_ref, late_ref, w_ref, sum_ref):
    @pl.when(group_ref[0] == 1)
    def _():
        weigh(table_ref, 1, hh_ref, g_ref, w_ref, sum_ref)

    @pl.when(group_ref[0] == 0)
    def _():
        weigh(table_ref, 1, hh_ref, other_ref, w_ref, sum_ref)

    pull(w_ref, sum_ref, (own_ref, sib_ref, out_ref), late_ref)


def early_weights_kernel(group_ref, table_ref, hh_ref, g_ref, other_ref, w_ref, sum_ref):
    @pl.when(group_ref[0] == 0)
    def _():
        weigh(table_ref, 0, hh_ref, g_ref, w_ref, sum_ref)

    @pl.when(group_ref[0] == 1)
    def _():
        weigh(table_ref, 0, hh_ref, other_ref, w_ref, sum_ref)


def early_kernel(w_ref, sum_ref, own_ref, sib_ref, out_ref, early_ref):
    pull(w_ref, sum_ref, (own_ref, sib_ref, out_ref), early_ref)


def merged(first, second):
    highest = jnp.maximum(first[0], second[0])
    return jnp.stack(
        [
            highest,
            first[1] * jnp.exp(first[0] - highest) + second[1] * jnp.exp(second[0] - highest),
        ]
    )


def folded(part):
    own = merged(part[:, :NBLK], sibling(part[:, NBLK : 2 * NBLK]))
    beyond = part[:, 2 * NBLK :]
    arrived = outward(jnp.concatenate([own, beyond], axis=1))
    own = merged(own, arrived[:, NBLK:])
    out = merged(arrived[:, :NBLK], beyond)
    own_total = own[0] + jnp.log(own[1])
    out_total = out[0] + jnp.log(out[1])
    return jnp.concatenate([own_total, sibling(own_total), out_total], axis=0)


def on_device(embeddings, log_mass, signatures, tile_list):
    owner = lax.axis_index("cells").astype(jnp.int32)
    group = (lax.axis_index("tiles") >= 2).astype(jnp.int32)
    owner_arg, group_arg = owner.reshape(1), group.reshape(1)

    def moment(array, index):
        return lax.dynamic_index_in_dim(array, index, 0, keepdims=False)

    target = moment(embeddings, group + 1)
    target_out = outward(target)
    target_sib = sibling(target)
    slots = lax.all_gather(tile_list, "tiles").reshape(-1)
    widened = embeddings.astype(jnp.float32)
    norms = (jnp.sum(widened * widened, axis=2) * INV).reshape(3, NBLK, BLOCK)
    masses = log_mass.reshape(3, NBLK, BLOCK)
    small = jnp.stack([masses, norms], axis=1)
    small_sib, small_out = sibling(small), outward(small)
    window = jnp.concatenate(
        [moment(small, group + 1), moment(small_sib, group + 1), moment(small_out, group + 1)], axis=1
    )
    start = window[0] - window[1]
    kt = (LAM - 1.0) * window[1] + window[0]
    at_source = moment(small, group)
    kc = (LAM - 1.0) * at_source[1] + at_source[0]

    table = call(
        table_kernel, jax.ShapeDtypeStruct((TABLE,), jnp.int32), SMEM, [SMEM, SMEM], mib=16
    )(owner_arg, slots)

    g_shape = jax.ShapeDtypeStruct((WIN, CELLS, BLOCK), jnp.float32)
    part_shape = jax.ShapeDtypeStruct((2, WIN, BLOCK), jnp.float32)
    uu = pltpu.VMEM((NBLK, BLOCK, BLOCK), jnp.float32)
    g, part = call(
        first_kernel, (g_shape, part_shape), (VMEM, VMEM), [SMEM, SMEM] + [VMEM] * 6, [uu]
    )(group_arg, table, moment(embeddings, group), target, target_sib, target_out, start, kc)

    other, _ = lax.optimization_barrier((moment(embeddings, 2 - group), target_out))
    other_out, other_sib = outward(other), sibling(other)

    hh = kt - LAM * folded(part)
    part = call(second_kernel, part_shape, VMEM, [SMEM, SMEM] + [VMEM] * 3, [uu])(
        group_arg, table, hh, kc, g
    )
    fates, _ = lax.optimization_barrier((signatures, hh))
    fates_out, fates_sib = outward(fates), sibling(fates)

    g_other = call(products_kernel, g_shape, VMEM, [VMEM] * 4)(
        moment(embeddings, 1 - group), other, other_sib, other_out
    )
    hh = kt - LAM * folded(part)
    hh_other = mirrored(hh)
    hh_late = jnp.where(group == 1, hh, hh_other)
    hh_early = jnp.where(group == 1, hh_other, hh)

    out_shape = jax.ShapeDtypeStruct((CELLS, signatures.shape[1]), jnp.bfloat16)
    w = jax.ShapeDtypeStruct((CELLS, WIN * BLOCK), jnp.bfloat16)
    sums = jax.ShapeDtypeStruct((CELLS, BLOCK), jnp.float32)
    late = call(
        late_kernel,
        out_shape,
        VMEM,
        [SMEM, SMEM] + [VMEM] * 6,
        [pltpu.VMEM(w.shape, w.dtype), pltpu.VMEM(sums.shape, sums.dtype)],
    )(group_arg, table, hh_late, g, g_other, signatures, fates_sib, fates_out)
    late_out, late_sib = outward(late), sibling(late)
    weights, weight_sums = call(
        early_weights_kernel, (w, sums), (VMEM, VMEM), [SMEM, SMEM] + [VMEM] * 3
    )(group_arg, table, hh_early, g, g_other)
    early = call(early_kernel, out_shape, VMEM, [VMEM] * 5)(
        weights, weight_sums, late, late_sib, late_out
    )
    return early, late


def solution(mesh):
    in_specs = (
        P(None, "cells", None),
        P(None, "cells"),
        P("cells", None),
        P(None, None, ("cells", "tiles")),
    )
    out_specs = (P("cells", None), P("cells", None))
    return jax.shard_map(
        on_device, mesh=mesh, in_specs=in_specs, out_specs=out_specs, check_vma=False
    )
```

```python
import jax
import jax.numpy as jnp
from jax import lax
from jax.experimental import pallas as pl
from jax.experimental.pallas import tpu as pltpu
from jax.sharding import PartitionSpec as P

EMB = 256
BLOCK = 128
NBLK = 8
WIN = 3 * NBLK
CELLS = NBLK * BLOCK
EPS = 0.01
RHO = 1.0
LAM = RHO / (RHO + EPS)
BIG = 1e30

LOG2E = 1.4426950408889634
SCALE = LOG2E / (EMB * EPS)

QUAD = 4
STRIDE = WIN + QUAD
GROUPS = 2 * NBLK * STRIDE
TABLE = 512

VMEM = pl.BlockSpec(memory_space=pltpu.VMEM)
SMEM = pl.BlockSpec(memory_space=pltpu.SMEM)


def sibling(value):
    return lax.ppermute(value, "cells", [(c, c ^ 1) for c in range(lax.axis_size("cells"))])


def outward(value):
    count = lax.axis_size("cells")
    pairs = [(c, (c + 1 if c % 2 else c - 1) % count) for c in range(count)]
    return lax.ppermute(value, "cells", pairs)


def mirrored(value):
    count = lax.axis_size("tiles")
    return lax.ppermute(value, "tiles", [(t, count - 1 - t) for t in range(count)])


def call(kernel, outs, out_specs, in_specs, scratch=(), flops=10**9, mib=16):
    return pl.pallas_call(
        kernel,
        out_shape=outs,
        in_specs=in_specs,
        out_specs=out_specs,
        scratch_shapes=list(scratch),
        compiler_params=pltpu.CompilerParams(vmem_limit_bytes=mib << 20),
        cost_estimate=pl.CostEstimate(flops=flops, bytes_accessed=4 << 20, transcendentals=1 << 21),
    )


def slot_codes(tile_list, owner):
    source, target = tile_list[:, 0], tile_list[:, 1]
    away = target >> 3
    region = jnp.where(away == owner, 0, jnp.where(away == (owner ^ 1), 1, 2))
    code = (source - owner * NBLK) * 32 + region * NBLK + (target & 7)
    return jnp.where(source >= 0, code, -1)


def table_kernel(*refs):
    *code_refs, table_ref = refs
    for coupling in range(2):
        for s in range(NBLK):
            table_ref[GROUPS + coupling * NBLK + s] = 0

        @pl.loop(0, code_refs[0].shape[1])
        def _(slot):
            for code_ref in code_refs:
                code = code_ref[coupling, slot]

                @pl.when(code >= 0)
                def _():
                    row = coupling * NBLK + (code >> 5)
                    count = table_ref[GROUPS + row]
                    table_ref[row * STRIDE + count] = code & 31
                    table_ref[GROUPS + row] = count + 1

        for s in range(NBLK):
            row = coupling * NBLK + s
            count = table_ref[GROUPS + row]
            for extra in range(QUAD - 1):
                table_ref[row * STRIDE + count + extra] = WIN
            table_ref[GROUPS + row] = (count + QUAD - 1) >> 2


def products(source_ref, target_refs, g_ref):
    for region, target_ref in enumerate(target_refs):

        @pl.loop(0, NBLK // 2)
        def _(pair):
            rows = target_ref[pl.ds(pl.multiple_of(pair * 256, 256), 256), :]
            g = lax.dot_general(
                source_ref[...], rows, (((1,), (1,)), ((), ())), preferred_element_type=jnp.float32
            ) * (2.0 * SCALE)
            g_ref[region * NBLK + 2 * pair] = g[:, :BLOCK]
            g_ref[region * NBLK + 2 * pair + 1] = g[:, BLOCK:]

    g_ref[WIN] = jnp.zeros((CELLS, BLOCK), jnp.float32)


def extended(hh_ref, terms_ref):
    terms_ref[:WIN, :] = hh_ref[...]
    terms_ref[WIN:, :] = jnp.full((8, BLOCK), -BIG, jnp.float32)


def row_parts(table_ref, coupling, s):
    row = coupling * NBLK + s
    base = row * STRIDE

    def targets(q):
        return [table_ref[base + q * QUAD + k] for k in range(QUAD)]

    rows = pl.ds(pl.multiple_of(s * BLOCK, BLOCK), BLOCK)
    return rows, table_ref[GROUPS + row], targets


def row_maximum(rows, groups, targets, terms_ref, g_ref):
    def step(q, highest):
        v = [g_ref[t, rows, :] + terms_ref[pl.ds(t, 1), :] for t in targets(q)]
        return jnp.maximum(highest, jnp.maximum(jnp.maximum(v[0], v[1]), jnp.maximum(v[2], v[3])))

    highest = lax.fori_loop(0, groups, step, jnp.full((BLOCK, BLOCK), -BIG, jnp.float32))
    return jnp.max(highest, axis=1, keepdims=True)


def scale_rows(table_ref, coupling, hh_ref, kc_ref, g_ref, part_ref, terms_ref, top_ref, mass_ref):
    extended(hh_ref, terms_ref)
    top_ref[...] = jnp.full(top_ref.shape, -BIG, jnp.float32)
    mass_ref[...] = jnp.zeros(mass_ref.shape, jnp.float32)

    @pl.loop(0, NBLK)
    def _(s):
        rows, groups, targets = row_parts(table_ref, coupling, s)
        m = row_maximum(rows, groups, targets, terms_ref, g_ref)

        def step(q, acc):
            v = [jnp.exp2(g_ref[t, rows, :] + terms_ref[pl.ds(t, 1), :] - m) for t in targets(q)]
            return acc + ((v[0] + v[1]) + (v[2] + v[3]))

        acc = lax.fori_loop(0, groups, step, jnp.zeros((BLOCK, BLOCK), jnp.float32))
        total = m + LOG2E * jnp.log(jnp.sum(acc, axis=1, keepdims=True))
        kc = jnp.broadcast_to(kc_ref[pl.ds(s, 1), :], (BLOCK, BLOCK)).T
        uu = kc - LAM * total

        @pl.loop(0, groups)
        def _(q):
            ts = targets(q)
            tops = [top_ref[t] for t in ts]
            masses = [mass_ref[t] for t in ts]
            for t, top, mass in zip(ts, tops, masses):
                v = (g_ref[t, rows, :] + uu).reshape(BLOCK // 8, 8, BLOCK)
                high = jnp.maximum(top, jnp.max(v, axis=0))
                mass_ref[t] = mass * jnp.exp2(top - high) + jnp.sum(jnp.exp2(v - high), axis=0)
                top_ref[t] = high

    top = top_ref[:WIN]
    high = jnp.max(top, axis=1, keepdims=True)
    part_ref[0] = high[:, 0, :]
    part_ref[1] = jnp.sum(mass_ref[:WIN] * jnp.exp2(top - high), axis=1)


def weigh(table_ref, coupling, hh_ref, g_ref, w_ref, sum_ref, terms_ref):
    extended(hh_ref, terms_ref)

    @pl.loop(0, NBLK)
    def _(s):
        rows, groups, targets = row_parts(table_ref, coupling, s)
        m = row_maximum(rows, groups, targets, terms_ref, g_ref)
        w_ref[rows, :] = jnp.zeros((BLOCK, (WIN + 1) * BLOCK), jnp.bfloat16)

        def step(q, acc):
            for t in targets(q):
                e = jnp.exp2(g_ref[t, rows, :] + terms_ref[pl.ds(t, 1), :] - m)
                w_ref[rows, pl.ds(pl.multiple_of(t * BLOCK, BLOCK), BLOCK)] = e.astype(jnp.bfloat16)
                acc = acc + e
            return acc

        acc = lax.fori_loop(0, groups, step, jnp.zeros((BLOCK, BLOCK), jnp.float32))
        sum_ref[rows, :] = jnp.broadcast_to(jnp.sum(acc, axis=1, keepdims=True), (BLOCK, BLOCK))


def pull(w_ref, sum_ref, fate_refs, out_ref):
    @pl.loop(0, 4)
    def _(chunk):
        rows = pl.ds(pl.multiple_of(chunk * 256, 256), 256)
        total = jnp.zeros((256, out_ref.shape[1]), jnp.float32)
        for region, fate_ref in enumerate(fate_refs):
            total += jnp.dot(
                w_ref[rows, region * CELLS : (region + 1) * CELLS],
                fate_ref[...],
                preferred_element_type=jnp.float32,
            )
        inverse = 1.0 / sum_ref[rows, :]
        out_ref[rows, :] = (total * jnp.concatenate([inverse, inverse], axis=1)).astype(jnp.bfloat16)


def first_kernel(group_ref, table_ref, source_ref, own_ref, sib_ref, out_ref, hh_ref, kc_ref, g_ref, part_ref, *scratch):
    products(source_ref, (own_ref, sib_ref, out_ref), g_ref)
    scale_rows(table_ref, group_ref[0], hh_ref, kc_ref, g_ref, part_ref, *scratch)


def second_kernel(group_ref, table_ref, hh_ref, kc_ref, g_ref, part_ref, *scratch):
    scale_rows(table_ref, group_ref[0], hh_ref, kc_ref, g_ref, part_ref, *scratch)


def products_kernel(source_ref, own_ref, sib_ref, out_ref, g_ref):
    products(source_ref, (own_ref, sib_ref, out_ref), g_ref)


def weigh_one(coupling, group_ref, table_ref, hh_ref, g_ref, other_ref, *outs):
    @pl.when(group_ref[0] == coupling)
    def _():
        weigh(table_ref, coupling, hh_ref, g_ref, *outs)

    @pl.when(group_ref[0] != coupling)
    def _():
        weigh(table_ref, coupling, hh_ref, other_ref, *outs)


def late_kernel(group_ref, table_ref, hh_ref, g_ref, other_ref, own_ref, sib_ref, out_ref, late_ref, w_ref, sum_ref, terms_ref):
    weigh_one(1, group_ref, table_ref, hh_ref, g_ref, other_ref, w_ref, sum_ref, terms_ref)
    pull(w_ref, sum_ref, (own_ref, sib_ref, out_ref), late_ref)


def early_weights_kernel(group_ref, table_ref, hh_ref, g_ref, other_ref, w_ref, sum_ref, terms_ref):
    weigh_one(0, group_ref, table_ref, hh_ref, g_ref, other_ref, w_ref, sum_ref, terms_ref)


def early_kernel(w_ref, sum_ref, own_ref, sib_ref, out_ref, early_ref):
    pull(w_ref, sum_ref, (own_ref, sib_ref, out_ref), early_ref)


G_SHAPE = jax.ShapeDtypeStruct((WIN + 1, CELLS, BLOCK), jnp.float32)
PART_SHAPE = jax.ShapeDtypeStruct((2, WIN, BLOCK), jnp.float32)
W_SHAPE = jax.ShapeDtypeStruct((CELLS, (WIN + 1) * BLOCK), jnp.bfloat16)
SUM_SHAPE = jax.ShapeDtypeStruct((CELLS, BLOCK), jnp.float32)
FATE_SHAPE = jax.ShapeDtypeStruct((CELLS, EMB), jnp.bfloat16)
TERMS = pltpu.VMEM((WIN + 8, BLOCK), jnp.float32)
SWEEP_SCRATCH = [TERMS] + [pltpu.VMEM((WIN + 1, 8, BLOCK), jnp.float32)] * 2
HOLD = [pltpu.VMEM(W_SHAPE.shape, W_SHAPE.dtype), pltpu.VMEM(SUM_SHAPE.shape, SUM_SHAPE.dtype)]


def build_table(codes):
    specs = [SMEM] * len(codes)
    return call(table_kernel, jax.ShapeDtypeStruct((TABLE,), jnp.int32), SMEM, specs)(*codes)


def first_sweep(*args):
    return call(first_kernel, (G_SHAPE, PART_SHAPE), (VMEM, VMEM), [SMEM, SMEM] + [VMEM] * 6, SWEEP_SCRATCH)(*args)


def next_sweep(*args):
    return call(second_kernel, PART_SHAPE, VMEM, [SMEM, SMEM] + [VMEM] * 3, SWEEP_SCRATCH)(*args)


def other_products(*args):
    return call(products_kernel, G_SHAPE, VMEM, [VMEM] * 4)(*args)


def late_fates(*args):
    return call(late_kernel, FATE_SHAPE, VMEM, [SMEM, SMEM] + [VMEM] * 6, HOLD + [TERMS])(*args)


def early_weights(*args):
    return call(
        early_weights_kernel, (W_SHAPE, SUM_SHAPE), (VMEM, VMEM), [SMEM, SMEM] + [VMEM] * 3, [TERMS]
    )(*args)


def early_fates(*args):
    return call(early_kernel, FATE_SHAPE, VMEM, [VMEM] * 5)(*args)


def merged(first, second):
    highest = jnp.maximum(first[0], second[0])
    return jnp.stack(
        [
            highest,
            first[1] * jnp.exp2(first[0] - highest) + second[1] * jnp.exp2(second[0] - highest),
        ]
    )


def folded(part):
    own = merged(part[:, :NBLK], sibling(part[:, NBLK : 2 * NBLK]))
    beyond = part[:, 2 * NBLK :]
    arrived = outward(jnp.concatenate([own, beyond], axis=1))
    own = merged(own, arrived[:, NBLK:])
    out = merged(arrived[:, :NBLK], beyond)
    own_total = own[0] + jnp.log2(own[1])
    out_total = out[0] + jnp.log2(out[1])
    return jnp.concatenate([own_total, sibling(own_total), out_total], axis=0)


def shifted(value, steps):
    count = lax.axis_size("tiles")
    return lax.ppermute(value, "tiles", [(t, (t + steps) % count) for t in range(count)])


def on_device(embeddings, log_mass, signatures, tile_list):
    owner = lax.axis_index("cells").astype(jnp.int32)
    group = (lax.axis_index("tiles") >= 2).astype(jnp.int32)
    group_arg = group.reshape(1)

    def moment(array, index):
        return lax.dynamic_index_in_dim(array, index, 0, keepdims=False)

    target = moment(embeddings, group + 1)
    target_out, target_sib = outward(target), sibling(target)
    codes = slot_codes(tile_list, owner)
    table = build_table([codes] + [shifted(codes, k) for k in range(1, lax.axis_size("tiles"))])

    widened = embeddings.astype(jnp.float32)
    norms = (jnp.sum(widened * widened, axis=2) * SCALE).reshape(3, NBLK, BLOCK)
    masses = log_mass.reshape(3, NBLK, BLOCK) * LOG2E
    small = jnp.stack([masses - norms, masses + (LAM - 1.0) * norms], axis=1)
    window = jnp.concatenate(
        [moment(part, group + 1) for part in (small, sibling(small), outward(small))], axis=1
    )
    kc = moment(small, group)[1]

    g, part = first_sweep(
        group_arg, table, moment(embeddings, group), target, target_sib, target_out, window[0], kc
    )

    other, _ = lax.optimization_barrier((moment(embeddings, 2 - group), target_out))
    other_out, other_sib = outward(other), sibling(other)

    hh = window[1] - LAM * folded(part)
    part = next_sweep(group_arg, table, hh, kc, g)
    fates, _ = lax.optimization_barrier((signatures, hh))
    fates_out, fates_sib = outward(fates), sibling(fates)

    g_other = other_products(moment(embeddings, 1 - group), other, other_sib, other_out)
    hh = window[1] - LAM * folded(part)
    hh_other = mirrored(hh)
    hh_late = jnp.where(group == 1, hh, hh_other)
    hh_early = jnp.where(group == 1, hh_other, hh)

    late = late_fates(group_arg, table, hh_late, g, g_other, signatures, fates_sib, fates_out)
    late_out, late_sib = outward(late), sibling(late)
    weights, sums = early_weights(group_arg, table, hh_early, g, g_other)
    early = early_fates(weights, sums, late, late_sib, late_out)
    return early, late


def solution(mesh):
    in_specs = (
        P(None, "cells", None),
        P(None, "cells"),
        P("cells", None),
        P(None, None, ("cells", "tiles")),
    )
    out_specs = (P("cells", None), P("cells", None))
    return jax.shard_map(
        on_device, mesh=mesh, in_specs=in_specs, out_specs=out_specs, check_vma=False
    )
```

```python
import jax
import jax.numpy as jnp
from jax import lax
from jax.experimental import pallas as pl
from jax.experimental.pallas import tpu as pltpu
from jax.sharding import PartitionSpec as P

EMB = 256
BLOCK = 128
NBLK = 8
WIN = 3 * NBLK
CELLS = NBLK * BLOCK
EPS = 0.01
RHO = 1.0
LAM = RHO / (RHO + EPS)
BIG = 1e30

LOG2E = 1.4426950408889634
SCALE = LOG2E / (EMB * EPS)

QUAD = 4
STRIDE = WIN + QUAD
GROUPS = NBLK * STRIDE
TABLE = 256

FLOPS, BYTES, MIB = 3 * 10**9, 10**4, 6
VMEM = pl.BlockSpec(memory_space=pltpu.VMEM)
SMEM = pl.BlockSpec(memory_space=pltpu.SMEM)


def sibling(value):
    return lax.ppermute(value, "cells", [(c, c ^ 1) for c in range(lax.axis_size("cells"))])


def outward(value):
    count = lax.axis_size("cells")
    pairs = [(c, (c + 1 if c % 2 else c - 1) % count) for c in range(count)]
    return lax.ppermute(value, "cells", pairs)


def mirrored(value):
    count = lax.axis_size("tiles")
    return lax.ppermute(value, "tiles", [(t, count - 1 - t) for t in range(count)])


def call(kernel, outs, out_specs, in_specs, scratch=(), aliases=None, flops=FLOPS, mib=MIB):
    return pl.pallas_call(
        kernel,
        out_shape=outs,
        in_specs=in_specs,
        out_specs=out_specs,
        scratch_shapes=list(scratch),
        input_output_aliases=aliases or {},
        compiler_params=pltpu.CompilerParams(vmem_limit_bytes=mib << 20),
        cost_estimate=pl.CostEstimate(flops=flops, bytes_accessed=BYTES, transcendentals=0),
    )


def table_kernel(place_ref, *refs):
    *slot_refs, table_ref = refs
    owner, coupling = place_ref[0], place_ref[1]
    for s in range(NBLK):
        table_ref[GROUPS + s] = 0

    @pl.loop(0, slot_refs[0].shape[2])
    def _(slot):
        for slot_ref in slot_refs:
            source = slot_ref[coupling, 0, slot]

            @pl.when(source >= 0)
            def _():
                target = slot_ref[coupling, 1, slot]
                away = target >> 3
                region = jnp.where(away == owner, 0, jnp.where(away == (owner ^ 1), 1, 2))
                s = source & 7
                count = table_ref[GROUPS + s]
                table_ref[s * STRIDE + count] = region * NBLK + (target & 7)
                table_ref[GROUPS + s] = count + 1

    for s in range(NBLK):
        count = table_ref[GROUPS + s]
        for extra in range(QUAD - 1):
            table_ref[s * STRIDE + count + extra] = WIN
        table_ref[GROUPS + s] = (count + QUAD - 1) >> 2


def products(source_ref, target_refs, g_ref, first):
    for region, target_ref in enumerate(target_refs, first):

        @pl.loop(0, NBLK // 2)
        def _(pair):
            rows = target_ref[pl.ds(pl.multiple_of(pair * 256, 256), 256), :]
            g = lax.dot_general(
                source_ref[...], rows, (((1,), (1,)), ((), ())), preferred_element_type=jnp.float32
            ) * (2.0 * SCALE)
            g_ref[region * NBLK + 2 * pair] = g[:, :BLOCK]
            g_ref[region * NBLK + 2 * pair + 1] = g[:, BLOCK:]


def target_constants(target_ref, mass_row, window_ref, region):
    ones = jnp.ones((8, EMB), jnp.bfloat16)
    for pair in range(NBLK // 2):
        y = target_ref[pair * 256 : (pair + 1) * 256, :].astype(jnp.float32)
        square = y * y
        high = square.astype(jnp.bfloat16)
        low = (square - high.astype(jnp.float32)).astype(jnp.bfloat16)
        norm = sum(
            lax.dot_general(ones, part, (((1,), (1,)), ((), ())), preferred_element_type=jnp.float32)
            for part in (high, low)
        )
        for half in range(2):
            block = 2 * pair + half
            scaled = norm[:1, half * BLOCK : (half + 1) * BLOCK] * SCALE
            mass = mass_row(block) * LOG2E
            at = region * NBLK + block
            window_ref[0, at : at + 1, :] = mass - scaled
            window_ref[1, at : at + 1, :] = mass + (LAM - 1.0) * scaled


def mass_rows(mass_ref, group, first):
    def row(block):
        lanes = slice(block * BLOCK, (block + 1) * BLOCK)
        low, high = mass_ref[first : first + 1, lanes], mass_ref[first + 1 : first + 2, lanes]
        return jnp.where(group == 0, low, high)

    return row


def extended(hh_ref, terms_ref):
    terms_ref[:WIN, :] = hh_ref[...]
    terms_ref[WIN:, :] = jnp.full((8, BLOCK), -BIG, jnp.float32)


def row_parts(table_ref, s):
    base = s * STRIDE

    def targets(q):
        return [table_ref[base + q * QUAD + k] for k in range(QUAD)]

    rows = pl.ds(pl.multiple_of(s * BLOCK, BLOCK), BLOCK)
    return rows, table_ref[GROUPS + s], targets


def row_maximum(rows, groups, targets, terms_ref, g_ref):
    def step(q, highest):
        v = [g_ref[t, rows, :] + terms_ref[pl.ds(t, 1), :] for t in targets(q)]
        return jnp.maximum(highest, jnp.maximum(jnp.maximum(v[0], v[1]), jnp.maximum(v[2], v[3])))

    highest = lax.fori_loop(0, groups, step, jnp.full((BLOCK, BLOCK), -BIG, jnp.float32))
    return jnp.max(highest, axis=1, keepdims=True)


def sweep_kernel(table_ref, hh_ref, kc_ref, g_ref, part_ref, terms_ref, top_ref, mass_ref):
    extended(hh_ref, terms_ref)
    top_ref[...] = jnp.full(top_ref.shape, -BIG, jnp.float32)
    mass_ref[...] = jnp.zeros(mass_ref.shape, jnp.float32)

    @pl.loop(0, NBLK)
    def _(s):
        rows, groups, targets = row_parts(table_ref, s)
        m = row_maximum(rows, groups, targets, terms_ref, g_ref)

        def step(q, acc):
            v = [jnp.exp2(g_ref[t, rows, :] + terms_ref[pl.ds(t, 1), :] - m) for t in targets(q)]
            return acc + ((v[0] + v[1]) + (v[2] + v[3]))

        acc = lax.fori_loop(0, groups, step, jnp.zeros((BLOCK, BLOCK), jnp.float32))
        total = m + LOG2E * jnp.log(jnp.sum(acc, axis=1, keepdims=True))
        uu = kc_ref[rows, :] - LAM * total

        @pl.loop(0, groups)
        def _(q):
            ts = targets(q)
            tops = [top_ref[t] for t in ts]
            masses = [mass_ref[t] for t in ts]
            for t, top, mass in zip(ts, tops, masses):
                v = (g_ref[t, rows, :] + uu).reshape(BLOCK // 8, 8, BLOCK)
                high = jnp.maximum(top, jnp.max(v, axis=0))
                mass_ref[t] = mass * jnp.exp2(top - high) + jnp.sum(jnp.exp2(v - high), axis=0)
                top_ref[t] = high

    top = top_ref[:WIN]
    high = jnp.max(top, axis=1, keepdims=True)
    part_ref[0] = high[:, 0, :]
    part_ref[1] = jnp.sum(mass_ref[:WIN] * jnp.exp2(top - high), axis=1)


def weigh(table_ref, hh_ref, g_ref, w_ref, sum_ref, terms_ref):
    extended(hh_ref, terms_ref)

    @pl.loop(0, NBLK)
    def _(s):
        rows, groups, targets = row_parts(table_ref, s)
        m = row_maximum(rows, groups, targets, terms_ref, g_ref)
        w_ref[rows, :] = jnp.zeros((BLOCK, (WIN + 1) * BLOCK), jnp.bfloat16)

        def step(q, acc):
            for t in targets(q):
                e = jnp.exp2(g_ref[t, rows, :] + terms_ref[pl.ds(t, 1), :] - m)
                w_ref[rows, pl.ds(pl.multiple_of(t * BLOCK, BLOCK), BLOCK)] = e.astype(jnp.bfloat16)
                acc = acc + e
            return acc

        acc = lax.fori_loop(0, groups, step, jnp.zeros((BLOCK, BLOCK), jnp.float32))
        sum_ref[rows, :] = jnp.broadcast_to(jnp.sum(acc, axis=1, keepdims=True), (BLOCK, BLOCK))


def pulled(w_ref, rows, fate_refs, first):
    total = 0.0
    for region, fate_ref in enumerate(fate_refs, first):
        total += jnp.dot(
            w_ref[rows, region * CELLS : (region + 1) * CELLS],
            fate_ref[...],
            preferred_element_type=jnp.float32,
        )
    return total


def divided(total, sums):
    inverse = 1.0 / sums
    return (total * jnp.concatenate([inverse, inverse], axis=1)).astype(jnp.bfloat16)


def chunks(body):
    @pl.loop(0, 4)
    def _(chunk):
        body(pl.ds(pl.multiple_of(chunk * 256, 256), 256))


def near_kernel(place_ref, cells_ref, mass_ref, sib_mass_ref, sib_ref, g_ref, kc_ref, window_ref):
    group = place_ref[1]
    source_ref, own_ref = cells_ref.at[group], cells_ref.at[group + 1]
    products(source_ref, (own_ref, sib_ref), g_ref, 0)
    g_ref[WIN] = jnp.zeros((CELLS, BLOCK), jnp.float32)
    target_constants(own_ref, mass_rows(mass_ref, group, 1), window_ref, 0)
    target_constants(sib_ref, mass_rows(sib_mass_ref, group, 1), window_ref, 1)
    source_mass = mass_rows(mass_ref, group, 0)
    for s in range(NBLK):
        x = source_ref[s * BLOCK : (s + 1) * BLOCK, :].astype(jnp.float32)
        norm = jnp.sum(x * x, axis=1, keepdims=True) * SCALE
        mass = jnp.broadcast_to(source_mass(s), (BLOCK, BLOCK)).T
        kc_ref[s * BLOCK : (s + 1) * BLOCK, :] = mass * LOG2E + (LAM - 1.0) * norm


def far_kernel(place_ref, cells_ref, out_mass_ref, out_ref, near_ref, near_window_ref, g_ref, window_ref):
    del near_ref
    group = place_ref[1]
    window_ref[:, : 2 * NBLK, :] = near_window_ref[...]
    products(cells_ref.at[group], (out_ref,), g_ref, 2)
    target_constants(out_ref, mass_rows(out_mass_ref, group, 1), window_ref, 2)


def other_kernel(place_ref, cells_ref, sib_ref, out_ref, g_ref):
    group = place_ref[1]
    products(cells_ref.at[1 - group], (cells_ref.at[2 - group], sib_ref, out_ref), g_ref, 0)
    g_ref[WIN] = jnp.zeros((CELLS, BLOCK), jnp.float32)


def weigh_one(coupling, place_ref, mine, others, *outs):
    @pl.when(place_ref[1] == coupling)
    def _():
        weigh(*mine, *outs)

    @pl.when(place_ref[1] != coupling)
    def _():
        weigh(*others, *outs)


def late_kernel(place_ref, table_ref, hh_ref, g_ref, table2_ref, hh2_ref, g2_ref, own_ref, sib_ref, out_ref, late_ref, w_ref, sum_ref, terms_ref):
    weigh_one(1, place_ref, (table_ref, hh_ref, g_ref), (table2_ref, hh2_ref, g2_ref), w_ref, sum_ref, terms_ref)
    fates = (own_ref, sib_ref, out_ref)

    @chunks
    def _(rows):
        late_ref[rows, :] = divided(pulled(w_ref, rows, fates, 0), sum_ref[rows, :])


def early_weights_kernel(place_ref, table_ref, hh_ref, g_ref, table2_ref, hh2_ref, g2_ref, w_ref, sum_ref, terms_ref):
    weigh_one(0, place_ref, (table_ref, hh_ref, g_ref), (table2_ref, hh2_ref, g2_ref), w_ref, sum_ref, terms_ref)


def early_near_kernel(w_ref, own_ref, sib_ref, total_ref):
    @chunks
    def _(rows):
        total_ref[rows, :] = pulled(w_ref, rows, (own_ref, sib_ref), 0)


def early_kernel(w_ref, sum_ref, total_ref, out_ref, early_ref):
    @chunks
    def _(rows):
        total = total_ref[rows, :] + pulled(w_ref, rows, (out_ref,), 2)
        early_ref[rows, :] = divided(total, sum_ref[rows, :])


G_SHAPE = pltpu.VMEM((WIN + 1, CELLS, BLOCK), jnp.float32)
PART_SHAPE = jax.ShapeDtypeStruct((2, WIN, BLOCK), jnp.float32)
W_SHAPE = jax.ShapeDtypeStruct((CELLS, (WIN + 1) * BLOCK), jnp.bfloat16)
COLUMN_SHAPE = jax.ShapeDtypeStruct((CELLS, BLOCK), jnp.float32)
FATE_SHAPE = jax.ShapeDtypeStruct((CELLS, EMB), jnp.bfloat16)
TOTAL_SHAPE = jax.ShapeDtypeStruct((CELLS, EMB), jnp.float32)
TERMS = pltpu.VMEM((WIN + 8, BLOCK), jnp.float32)
SWEEP_SCRATCH = [TERMS] + [pltpu.VMEM((WIN + 1, 8, BLOCK), jnp.float32)] * 2
HOLD = [pltpu.VMEM(W_SHAPE.shape, W_SHAPE.dtype), pltpu.VMEM(COLUMN_SHAPE.shape, COLUMN_SHAPE.dtype)]


WINDOW_SHAPE = jax.ShapeDtypeStruct((2, WIN, BLOCK), jnp.float32)
NEAR_SHAPE = jax.ShapeDtypeStruct((2, 2 * NBLK, BLOCK), jnp.float32)


def build_table(place, slots):
    specs = [SMEM] * (1 + len(slots))
    return call(table_kernel, jax.ShapeDtypeStruct((TABLE,), jnp.int32), SMEM, specs)(place, *slots)


def near_products(*args):
    return call(near_kernel, (G_SHAPE, COLUMN_SHAPE, NEAR_SHAPE), (VMEM,) * 3, [SMEM] + [VMEM] * 4)(*args)


def far_products(*args):
    return call(far_kernel, (G_SHAPE, WINDOW_SHAPE), (VMEM,) * 2, [SMEM] + [VMEM] * 5, aliases={4: 0})(*args)


def sweep(*args):
    return call(sweep_kernel, PART_SHAPE, VMEM, [SMEM] + [VMEM] * 3, SWEEP_SCRATCH)(*args)


def other_products(*args):
    return call(other_kernel, G_SHAPE, VMEM, [SMEM] + [VMEM] * 3)(*args)


COUPLINGS = [SMEM, SMEM, VMEM, VMEM, SMEM, VMEM, VMEM]


def late_fates(*args):
    return call(late_kernel, FATE_SHAPE, VMEM, COUPLINGS + [VMEM] * 3, HOLD + [TERMS], mib=12)(*args)


def early_weights(*args):
    return call(early_weights_kernel, (W_SHAPE, COLUMN_SHAPE), (VMEM, VMEM), COUPLINGS, [TERMS])(*args)


def early_near(*args):
    return call(early_near_kernel, TOTAL_SHAPE, VMEM, [VMEM] * 3)(*args)


def early_fates(*args):
    return call(early_kernel, FATE_SHAPE, VMEM, [VMEM] * 4)(*args)


def merged(first, second):
    highest = jnp.maximum(first[0], second[0])
    return jnp.stack(
        [
            highest,
            first[1] * jnp.exp2(first[0] - highest) + second[1] * jnp.exp2(second[0] - highest),
        ]
    )


def folded(part, beside=lambda message: None):
    own = merged(part[:, :NBLK], sibling(part[:, NBLK : 2 * NBLK]))
    beyond = part[:, 2 * NBLK :]
    message = jnp.concatenate([own, beyond], axis=1)
    arrived, made = lax.optimization_barrier((outward(message), beside(message)))
    own = merged(own, arrived[:, NBLK:])
    out = merged(arrived[:, :NBLK], beyond)
    own_total = own[0] + jnp.log2(own[1])
    out_total = out[0] + jnp.log2(out[1])
    return jnp.concatenate([own_total, sibling(own_total), out_total], axis=0), made


def shifted(value, steps):
    count = lax.axis_size("tiles")
    return lax.ppermute(value, "tiles", [(t, (t + steps) % count) for t in range(count)])


def on_device(embeddings, log_mass, signatures, tile_list):
    owner = lax.axis_index("cells").astype(jnp.int32)
    group = (lax.axis_index("tiles") >= 2).astype(jnp.int32)
    place, place_other = jnp.stack([owner, group]), jnp.stack([owner, 1 - group])

    def moment(index):
        return lax.dynamic_index_in_dim(embeddings, index, 0, keepdims=False)

    def after(values, gate):
        return lax.optimization_barrier((values, gate))[0]

    target = moment(group + 1)
    target_out, target_sib = outward(target), sibling(target)
    masses, slots = after((log_mass, tile_list), target_sib)
    gathered = [slots] + [shifted(slots, k) for k in range(1, lax.axis_size("tiles"))]
    masses_out, masses_sib = outward(masses), sibling(masses)
    g, kc, near = near_products(place, embeddings, masses, masses_sib, target_sib)
    gathered, masses_out = lax.optimization_barrier((gathered, masses_out))
    table = build_table(place, gathered)

    other = after(moment(2 - group), near)
    other_out, other_sib = outward(other), sibling(other)
    g, window = far_products(place, embeddings, masses_out, target_out, g, near)
    part = sweep(table, window[0], kc, g)

    def beside(message):
        (sib, out), lists = after(((other_sib, other_out), gathered), message)
        return other_products(place, embeddings, sib, out), build_table(place_other, lists)

    totals, (g_other, table_other) = folded(part, beside)
    hh = window[1] - LAM * totals
    part = sweep(table, hh, kc, g)
    fates = after(signatures, hh)
    fates_out, fates_sib = outward(fates), sibling(fates)

    hh = window[1] - LAM * folded(part)[0]
    couplings = (place, table, hh, g, table_other, mirrored(hh), g_other)
    late = late_fates(*couplings, signatures, fates_sib, fates_out)
    late_out, late_sib = outward(late), sibling(late)
    weights, sums = early_weights(*couplings)
    total = early_near(weights, late, late_sib)
    early = early_fates(weights, sums, total, late_out)
    return early, late


def solution(mesh):
    in_specs = (
        P(None, "cells", None),
        P(None, "cells"),
        P("cells", None),
        P(None, None, ("cells", "tiles")),
    )
    out_specs = (P("cells", None), P("cells", None))
    return jax.shard_map(
        on_device, mesh=mesh, in_specs=in_specs, out_specs=out_specs, check_vma=False
    )
```

```python
import jax
import jax.numpy as jnp
from jax import lax
from jax.experimental import pallas as pl
from jax.experimental.pallas import tpu as pltpu
from jax.sharding import PartitionSpec as P

EMB = 256
BLOCK = 128
NBLK = 8
WIN = 3 * NBLK
CELLS = NBLK * BLOCK
EPS = 0.01
RHO = 1.0
LAM = RHO / (RHO + EPS)
BIG = 1e30

LOG2E = 1.4426950408889634
SCALE = LOG2E / (EMB * EPS)

QUAD = 4
STRIDE = WIN + QUAD
GROUPS = 384
TABLE = 512

FLOPS, BYTES, MIB = 3 * 10**9, 10**4, 4
VMEM = pl.BlockSpec(memory_space=pltpu.VMEM)
SMEM = pl.BlockSpec(memory_space=pltpu.SMEM)
ANY = pl.BlockSpec(memory_space=pl.ANY)


def sibling(value):
    return lax.ppermute(value, "cells", [(c, c ^ 1) for c in range(lax.axis_size("cells"))])


def outward(value):
    count = lax.axis_size("cells")
    pairs = [(c, (c + 1 if c % 2 else c - 1) % count) for c in range(count)]
    return lax.ppermute(value, "cells", pairs)


def mirrored(value):
    count = lax.axis_size("tiles")
    return lax.ppermute(value, "tiles", [(t, count - 1 - t) for t in range(count)])


def call(kernel, outs, out_specs, in_specs, scratch=(), aliases=None, flops=FLOPS, mib=MIB):
    return pl.pallas_call(
        kernel,
        out_shape=outs,
        in_specs=in_specs,
        out_specs=out_specs,
        scratch_shapes=list(scratch),
        input_output_aliases=aliases or {},
        compiler_params=pltpu.CompilerParams(vmem_limit_bytes=mib << 20),
        cost_estimate=pl.CostEstimate(flops=flops, bytes_accessed=BYTES, transcendentals=0),
    )


def table_kernel(place_ref, behind_ref, *refs):
    del behind_ref
    *slot_refs, table_ref = refs
    owner, coupling = place_ref[0], place_ref[1]
    for s in range(NBLK + 1):
        table_ref[GROUPS + s] = 0

    @pl.loop(0, slot_refs[0].shape[2] // 2)
    def _(pair):
        for slot_ref in slot_refs:
            for half in range(2):
                source = slot_ref[coupling, 0, 2 * pair + half]
                target = slot_ref[coupling, 1, 2 * pair + half]
                away = target >> 3
                region = jnp.where(away == owner, 0, jnp.where(away == (owner ^ 1), NBLK, 2 * NBLK))
                s = jnp.where(source < 0, NBLK, source & 7)
                count = table_ref[GROUPS + s]
                table_ref[GROUPS + s] = count + 1
                table_ref[s * STRIDE + count] = region + (target & 7)

    for s in range(NBLK):
        count = table_ref[GROUPS + s]
        for extra in range(QUAD - 1):
            table_ref[s * STRIDE + count + extra] = WIN
        table_ref[GROUPS + s] = (count + QUAD - 1) >> 2


def products(source_ref, target_refs, g_ref, first):
    for region, target_ref in enumerate(target_refs, first):

        @pl.loop(0, NBLK // 2)
        def _(pair):
            rows = target_ref[pl.ds(pl.multiple_of(pair * 256, 256), 256), :]
            g = lax.dot_general(
                source_ref[...], rows, (((1,), (1,)), ((), ())), preferred_element_type=jnp.float32
            ) * (2.0 * SCALE)
            g_ref[region * NBLK + 2 * pair] = g[:, :BLOCK]
            g_ref[region * NBLK + 2 * pair + 1] = g[:, BLOCK:]


def target_constants(target_ref, mass_row, window_ref, region):
    ones = jnp.ones((8, EMB), jnp.bfloat16)
    for pair in range(NBLK // 2):
        y = target_ref[pair * 256 : (pair + 1) * 256, :].astype(jnp.float32)
        square = y * y
        high = square.astype(jnp.bfloat16)
        low = (square - high.astype(jnp.float32)).astype(jnp.bfloat16)
        norm = sum(
            lax.dot_general(ones, part, (((1,), (1,)), ((), ())), preferred_element_type=jnp.float32)
            for part in (high, low)
        )
        for half in range(2):
            block = 2 * pair + half
            scaled = norm[:1, half * BLOCK : (half + 1) * BLOCK] * SCALE
            mass = mass_row(block) * LOG2E
            at = region * NBLK + block
            window_ref[0, at : at + 1, :] = mass - scaled
            window_ref[1, at : at + 1, :] = mass + (LAM - 1.0) * scaled


def mass_rows(mass_ref, group, first):
    def row(block):
        lanes = slice(block * BLOCK, (block + 1) * BLOCK)
        low, high = mass_ref[first : first + 1, lanes], mass_ref[first + 1 : first + 2, lanes]
        return jnp.where(group == 0, low, high)

    return row


STRIPS = BLOCK // 8


def extended(hh_ref, terms_ref):
    for t in range(WIN):
        terms_ref[t] = jnp.broadcast_to(hh_ref[t : t + 1, :], (8, BLOCK))
    terms_ref[WIN] = jnp.full((8, BLOCK), -BIG, jnp.float32)


def source_rows(s):
    return pl.ds(pl.multiple_of(s * BLOCK, BLOCK), BLOCK)


def group_targets(table_ref, s, q):
    return [table_ref[s * STRIDE + q * QUAD + k] for k in range(QUAD)]


def strips(g_ref, t, s):
    return g_ref[jnp.minimum(t, WIN - 1), source_rows(s), :].reshape(STRIPS, 8, BLOCK)


def row_maxima(table_ref, terms_ref, g_ref, m_ref):
    @pl.loop(0, NBLK)
    def _(s):
        def step(q, highest):
            v = [strips(g_ref, t, s) + terms_ref[t] for t in group_targets(table_ref, s, q)]
            return jnp.maximum(highest, jnp.maximum(jnp.maximum(v[0], v[1]), jnp.maximum(v[2], v[3])))

        start = jnp.full((STRIPS, 8, BLOCK), -BIG, jnp.float32)
        highest = lax.fori_loop(0, table_ref[GROUPS + s], step, start)
        m_ref[source_rows(s), :] = highest.reshape(BLOCK, BLOCK)

    m_ref[...] = jnp.broadcast_to(jnp.max(m_ref[...], axis=1, keepdims=True), m_ref.shape)


def sweep_kernel(table_ref, hh_ref, kc_ref, g_ref, part_ref, terms_ref, top_ref, mass_ref, m_ref, acc_ref):
    extended(hh_ref, terms_ref)
    top_ref[...] = jnp.full(top_ref.shape, -BIG, jnp.float32)
    mass_ref[...] = jnp.zeros(mass_ref.shape, jnp.float32)
    row_maxima(table_ref, terms_ref, g_ref, m_ref)

    @pl.loop(0, NBLK)
    def _(s):
        m = m_ref[source_rows(s), :].reshape(STRIPS, 8, BLOCK)

        def step(q, acc):
            v = [
                jnp.exp2(strips(g_ref, t, s) + terms_ref[t] - m)
                for t in group_targets(table_ref, s, q)
            ]
            return acc + ((v[0] + v[1]) + (v[2] + v[3]))

        start = jnp.zeros((STRIPS, 8, BLOCK), jnp.float32)
        acc = lax.fori_loop(0, table_ref[GROUPS + s], step, start)
        acc_ref[source_rows(s), :] = acc.reshape(BLOCK, BLOCK)

    sums = jnp.broadcast_to(jnp.sum(acc_ref[...], axis=1, keepdims=True), acc_ref.shape)
    acc_ref[...] = kc_ref[...] - LAM * (m_ref[...] + LOG2E * jnp.log(sums))

    @pl.loop(0, NBLK)
    def _(s):
        uu = acc_ref[source_rows(s), :].reshape(STRIPS, 8, BLOCK)

        @pl.loop(0, table_ref[GROUPS + s])
        def _(q):
            ts = group_targets(table_ref, s, q)
            tops = [top_ref[t] for t in ts]
            masses = [mass_ref[t] for t in ts]
            made = []
            for t, top, mass in zip(ts, tops, masses):
                v = strips(g_ref, t, s) + uu
                high = jnp.maximum(top, jnp.max(v, axis=0))
                made.append((high, mass * jnp.exp2(top - high) + jnp.sum(jnp.exp2(v - high), axis=0)))
            for t, (high, mass) in zip(ts, made):
                top_ref[t] = high
                mass_ref[t] = mass

    top = top_ref[:WIN]
    high = jnp.max(top, axis=1, keepdims=True)
    part_ref[0] = high[:, 0, :]
    part_ref[1] = jnp.sum(mass_ref[:WIN] * jnp.exp2(top - high), axis=1)


def weigh(table_ref, hh_ref, g_ref, w_ref, sum_ref, terms_ref, m_ref):
    extended(hh_ref, terms_ref)
    row_maxima(table_ref, terms_ref, g_ref, m_ref)

    @pl.loop(0, NBLK)
    def _(s):
        rows = source_rows(s)
        m = m_ref[rows, :].reshape(STRIPS, 8, BLOCK)
        w_ref[rows, :] = jnp.zeros((BLOCK, (WIN + 1) * BLOCK), jnp.bfloat16)

        def step(q, acc):
            ts = group_targets(table_ref, s, q)
            v = [jnp.exp2(strips(g_ref, t, s) + terms_ref[t] - m) for t in ts]
            for t, e in zip(ts, v):
                lanes = pl.ds(pl.multiple_of(t * BLOCK, BLOCK), BLOCK)
                w_ref[rows, lanes] = e.reshape(BLOCK, BLOCK).astype(jnp.bfloat16)
            return acc + ((v[0] + v[1]) + (v[2] + v[3]))

        start = jnp.zeros((STRIPS, 8, BLOCK), jnp.float32)
        acc = lax.fori_loop(0, table_ref[GROUPS + s], step, start)
        sum_ref[rows, :] = acc.reshape(BLOCK, BLOCK)

    sum_ref[...] = jnp.broadcast_to(jnp.sum(sum_ref[...], axis=1, keepdims=True), sum_ref.shape)


def pulled(w_ref, rows, fate_refs, first):
    total = 0.0
    for region, fate_ref in enumerate(fate_refs, first):
        total += jnp.dot(
            w_ref[rows, region * CELLS : (region + 1) * CELLS],
            fate_ref[...],
            preferred_element_type=jnp.float32,
        )
    return total


def divided(total, sums):
    inverse = 1.0 / sums
    return (total * jnp.concatenate([inverse, inverse], axis=1)).astype(jnp.bfloat16)


def chunks(body):
    @pl.loop(0, 4)
    def _(chunk):
        body(pl.ds(pl.multiple_of(chunk * 256, 256), 256))


def near_kernel(place_ref, source_ref, own_ref, mass_hbm, sib_mass_ref, sib_ref, g_ref, kc_ref, window_ref, mass_ref, sem):
    group = place_ref[1]
    fetched = pltpu.make_async_copy(mass_hbm, mass_ref, sem)
    fetched.start()
    products(source_ref, (own_ref, sib_ref), g_ref, 0)
    target_constants(sib_ref, mass_rows(sib_mass_ref, group, 1), window_ref, 1)
    fetched.wait()
    target_constants(own_ref, mass_rows(mass_ref, group, 1), window_ref, 0)
    source_mass = mass_rows(mass_ref, group, 0)
    for s in range(NBLK):
        x = source_ref[s * BLOCK : (s + 1) * BLOCK, :].astype(jnp.float32)
        norm = jnp.sum(x * x, axis=1, keepdims=True) * SCALE
        mass = jnp.broadcast_to(source_mass(s), (BLOCK, BLOCK)).T
        kc_ref[s * BLOCK : (s + 1) * BLOCK, :] = mass * LOG2E + (LAM - 1.0) * norm


def far_kernel(place_ref, table_ref, source_ref, out_mass_ref, out_ref, near_ref, near_window_ref, g_ref, window_ref):
    del table_ref, near_ref
    window_ref[:, : 2 * NBLK, :] = near_window_ref[...]
    products(source_ref, (out_ref,), g_ref, 2)
    target_constants(out_ref, mass_rows(out_mass_ref, place_ref[1], 1), window_ref, 2)


def other_kernel(behind_ref, source_ref, own_ref, sib_ref, out_ref, g_ref):
    del behind_ref
    products(source_ref, [ref.at[:CELLS] for ref in (own_ref, sib_ref, out_ref)], g_ref, 0)


def weigh_one(coupling, place_ref, mine, others, *outs):
    @pl.when(place_ref[1] == coupling)
    def _():
        weigh(*mine, *outs)

    @pl.when(place_ref[1] != coupling)
    def _():
        weigh(*others, *outs)


def late_kernel(place_ref, table_ref, hh_ref, g_ref, table2_ref, hh2_ref, g2_ref, own_ref, sib_ref, out_ref, late_ref, w_ref, sum_ref, terms_ref, m_ref):
    weigh_one(1, place_ref, (table_ref, hh_ref, g_ref), (table2_ref, hh2_ref, g2_ref), w_ref, sum_ref, terms_ref, m_ref)
    fates = [ref.at[CELLS:] for ref in (own_ref, sib_ref, out_ref)]

    @chunks
    def _(rows):
        late_ref[rows, :] = divided(pulled(w_ref, rows, fates, 0), sum_ref[rows, :])


def early_weights_kernel(place_ref, table_ref, hh_ref, g_ref, table2_ref, hh2_ref, g2_ref, w_ref, sum_ref, terms_ref, m_ref):
    weigh_one(0, place_ref, (table_ref, hh_ref, g_ref), (table2_ref, hh2_ref, g2_ref), w_ref, sum_ref, terms_ref, m_ref)


def early_near_kernel(w_ref, own_ref, sib_ref, total_ref):
    @chunks
    def _(rows):
        total_ref[rows, :] = pulled(w_ref, rows, (own_ref, sib_ref), 0)


def early_kernel(w_ref, sum_ref, total_ref, out_ref, early_ref):
    @chunks
    def _(rows):
        total = total_ref[rows, :] + pulled(w_ref, rows, (out_ref,), 2)
        early_ref[rows, :] = divided(total, sum_ref[rows, :])


G_SHAPE = pltpu.VMEM((WIN, CELLS, BLOCK), jnp.float32)
PART_SHAPE = jax.ShapeDtypeStruct((2, WIN, BLOCK), jnp.float32)
W_SHAPE = jax.ShapeDtypeStruct((CELLS, (WIN + 1) * BLOCK), jnp.bfloat16)
COLUMN_SHAPE = jax.ShapeDtypeStruct((CELLS, BLOCK), jnp.float32)
FATE_SHAPE = jax.ShapeDtypeStruct((CELLS, EMB), jnp.bfloat16)
TOTAL_SHAPE = jax.ShapeDtypeStruct((CELLS, EMB), jnp.float32)
TERMS = pltpu.VMEM((WIN + 1, 8, BLOCK), jnp.float32)
COLUMN = pltpu.VMEM(COLUMN_SHAPE.shape, COLUMN_SHAPE.dtype)
SWEEP_SCRATCH = [TERMS] * 3 + [COLUMN] * 2
HOLD = [pltpu.VMEM(W_SHAPE.shape, W_SHAPE.dtype), COLUMN]


WINDOW_SHAPE = jax.ShapeDtypeStruct((2, WIN, BLOCK), jnp.float32)
NEAR_SHAPE = jax.ShapeDtypeStruct((2, 2 * NBLK, BLOCK), jnp.float32)


def build_table(place, behind, slots):
    specs = [SMEM, ANY] + [SMEM] * len(slots)
    return call(table_kernel, jax.ShapeDtypeStruct((TABLE,), jnp.int32), SMEM, specs)(place, behind, *slots)


def near_products(*args):
    specs = [SMEM, VMEM, VMEM, ANY, VMEM, VMEM]
    scratch = [pltpu.VMEM((3, CELLS), jnp.float32), pltpu.SemaphoreType.DMA]
    return call(near_kernel, (G_SHAPE, COLUMN_SHAPE, NEAR_SHAPE), (VMEM,) * 3, specs, scratch)(*args)


def far_products(*args):
    return call(far_kernel, (G_SHAPE, WINDOW_SHAPE), (VMEM,) * 2, [SMEM, SMEM] + [VMEM] * 5, aliases={5: 0})(*args)


def sweep(*args):
    return call(sweep_kernel, PART_SHAPE, VMEM, [SMEM] + [VMEM] * 3, SWEEP_SCRATCH)(*args)


def other_products(*args):
    return call(other_kernel, G_SHAPE, VMEM, [ANY] + [VMEM] * 4)(*args)


COUPLINGS = [SMEM, SMEM, VMEM, VMEM, SMEM, VMEM, VMEM]


def late_fates(*args):
    return call(late_kernel, FATE_SHAPE, VMEM, COUPLINGS + [VMEM] * 3, HOLD + [TERMS, COLUMN], mib=9)(*args)


def early_weights(*args):
    return call(early_weights_kernel, (W_SHAPE, COLUMN_SHAPE), (VMEM, VMEM), COUPLINGS, [TERMS, COLUMN])(*args)


def early_near(*args):
    return call(early_near_kernel, TOTAL_SHAPE, VMEM, [VMEM] * 3)(*args)


def early_fates(*args):
    return call(early_kernel, FATE_SHAPE, VMEM, [VMEM] * 4)(*args)


def merged(first, second):
    highest = jnp.maximum(first[0], second[0])
    return jnp.stack(
        [
            highest,
            first[1] * jnp.exp2(first[0] - highest) + second[1] * jnp.exp2(second[0] - highest),
        ]
    )


def folded(part, beside):
    own = merged(part[:, :NBLK], sibling(part[:, NBLK : 2 * NBLK]))
    beyond = part[:, 2 * NBLK :]
    message = jnp.concatenate([own, beyond], axis=1)
    arrived, made = lax.optimization_barrier((outward(message), beside(message)))
    own = merged(own, arrived[:, NBLK:])
    out = merged(arrived[:, :NBLK], beyond)
    own_total = own[0] + jnp.log2(own[1])
    out_total = out[0] + jnp.log2(out[1])
    return jnp.concatenate([own_total, sibling(own_total), out_total], axis=0), made


def shifted(value, steps):
    count = lax.axis_size("tiles")
    return lax.ppermute(value, "tiles", [(t, (t + steps) % count) for t in range(count)])


def on_device(embeddings, log_mass, signatures, tile_list):
    owner = lax.axis_index("cells").astype(jnp.int32)
    group = (lax.axis_index("tiles") >= 2).astype(jnp.int32)
    place, place_other = jnp.stack([owner, group]), jnp.stack([owner, 1 - group])

    def moment(array, index):
        return lax.dynamic_index_in_dim(array, index, 0, keepdims=False)

    target = moment(embeddings, group + 1)
    target_out, target_sib = outward(target), sibling(target)
    cells, masses, slots, target_sib = lax.optimization_barrier(
        (embeddings, log_mass, tile_list, target_sib)
    )
    gathered = [slots] + [shifted(slots, k) for k in range(1, lax.axis_size("tiles"))]
    masses_out, masses_sib = outward(masses), sibling(masses)
    source, other_source = moment(cells, group), moment(cells, 1 - group)
    rest = jnp.concatenate([moment(cells, 2 - group), signatures])
    g, kc, near = near_products(place, source, target, log_mass, masses_sib, target_sib)
    table = build_table(place, near, gathered)
    g, window = far_products(place, table, source, masses_out, target_out, g, near)
    part = sweep(table, window[0], kc, g)
    rest_out, rest_sib = outward(rest), sibling(rest)

    totals, g_other = folded(
        part, lambda message: other_products(message, other_source, rest, rest_sib, rest_out)
    )
    hh = window[1] - LAM * totals
    part = sweep(table, hh, kc, g)
    totals, table_other = folded(part, lambda message: build_table(place_other, message, gathered))
    hh = window[1] - LAM * totals
    couplings = (place, table, hh, g, table_other, mirrored(hh), g_other)
    late = late_fates(*couplings, rest, rest_sib, rest_out)
    late_out, late_sib = outward(late), sibling(late)
    weights, sums = early_weights(*couplings)
    total = early_near(weights, late, late_sib)
    early = early_fates(weights, sums, total, late_out)
    return early, late


def solution(mesh):
    in_specs = (
        P(None, "cells", None),
        P(None, "cells"),
        P("cells", None),
        P(None, None, ("cells", "tiles")),
    )
    out_specs = (P("cells", None), P("cells", None))
    return jax.shard_map(
        on_device, mesh=mesh, in_specs=in_specs, out_specs=out_specs, check_vma=False
    )
```

```python
import jax
import jax.numpy as jnp
from jax import lax
from jax.experimental import pallas as pl
from jax.experimental.pallas import tpu as pltpu
from jax.sharding import PartitionSpec as P

EMB = 256
BLOCK = 128
NBLK = 8
WIN = 3 * NBLK
CELLS = NBLK * BLOCK
EPS = 0.01
RHO = 1.0
LAM = RHO / (RHO + EPS)
BIG = 1e30

LOG2E = 1.4426950408889634
SCALE = LOG2E / (EMB * EPS)

QUAD = 4
STRIDE = WIN + QUAD
GROUPS = 384
TABLE = 512

FLOPS, BYTES, MIB = 3 * 10**9, 10**4, 4
VMEM = pl.BlockSpec(memory_space=pltpu.VMEM)
SMEM = pl.BlockSpec(memory_space=pltpu.SMEM)
ANY = pl.BlockSpec(memory_space=pl.ANY)
HBM = pl.BlockSpec(memory_space=pltpu.HBM)


def sibling(value):
    return lax.ppermute(value, "cells", [(c, c ^ 1) for c in range(lax.axis_size("cells"))])


def outward(value):
    count = lax.axis_size("cells")
    pairs = [(c, (c + 1 if c % 2 else c - 1) % count) for c in range(count)]
    return lax.ppermute(value, "cells", pairs)


def mirrored(value):
    count = lax.axis_size("tiles")
    return lax.ppermute(value, "tiles", [(t, count - 1 - t) for t in range(count)])


def call(kernel, outs, out_specs, in_specs, scratch=(), aliases=None, flops=FLOPS, mib=MIB):
    return pl.pallas_call(
        kernel,
        out_shape=outs,
        in_specs=in_specs,
        out_specs=out_specs,
        scratch_shapes=list(scratch),
        input_output_aliases=aliases or {},
        compiler_params=pltpu.CompilerParams(vmem_limit_bytes=mib << 20),
        cost_estimate=pl.CostEstimate(flops=flops, bytes_accessed=BYTES, transcendentals=0),
    )


def table_kernel(place_ref, behind_ref, *refs):
    del behind_ref
    *slot_refs, table_ref = refs
    owner, coupling = place_ref[0], place_ref[1]
    for s in range(NBLK + 1):
        table_ref[GROUPS + s] = 0

    @pl.loop(0, slot_refs[0].shape[2] // 2)
    def _(pair):
        for slot_ref in slot_refs:
            for half in range(2):
                source = slot_ref[coupling, 0, 2 * pair + half]
                target = slot_ref[coupling, 1, 2 * pair + half]
                away = target >> 3
                region = jnp.where(away == owner, 0, jnp.where(away == (owner ^ 1), NBLK, 2 * NBLK))
                s = jnp.where(source < 0, NBLK, source & 7)
                count = table_ref[GROUPS + s]
                table_ref[GROUPS + s] = count + 1
                table_ref[s * STRIDE + count] = region + (target & 7)

    for s in range(NBLK):
        count = table_ref[GROUPS + s]
        for extra in range(QUAD - 1):
            table_ref[s * STRIDE + count + extra] = WIN
        table_ref[GROUPS + s] = (count + QUAD - 1) >> 2


def products(source_ref, target_refs, g_ref, first):
    for region, target_ref in enumerate(target_refs, first):

        @pl.loop(0, NBLK // 2)
        def _(pair):
            rows = target_ref[pl.ds(pl.multiple_of(pair * 256, 256), 256), :]
            g = lax.dot_general(
                source_ref[...], rows, (((1,), (1,)), ((), ())), preferred_element_type=jnp.float32
            ) * (2.0 * SCALE)
            g_ref[region * NBLK + 2 * pair] = g[:, :BLOCK]
            g_ref[region * NBLK + 2 * pair + 1] = g[:, BLOCK:]


def block_masses(mass_ref, group, first):
    rows = []
    for block in range(NBLK):
        lanes = slice(block * BLOCK, (block + 1) * BLOCK)
        low, high = mass_ref[first : first + 1, lanes], mass_ref[first + 1 : first + 2, lanes]
        rows.append(jnp.where(group == 0, low, high))
    return jnp.concatenate(rows, axis=0)


def pack_kernel(place_ref, cells_hbm, mass_hbm, message_ref, mass_ref, sems):
    group = place_ref[1]
    cells = pltpu.make_async_copy(cells_hbm.at[group + 1], message_ref.at[:CELLS], sems.at[0])
    masses = pltpu.make_async_copy(mass_hbm, mass_ref, sems.at[1])
    cells.start()
    masses.start()
    masses.wait()
    left = block_masses(mass_ref, group, 1)
    parts = []
    for _ in range(3):
        part = left.astype(jnp.bfloat16).astype(jnp.float32)
        parts.append(part)
        left = left - part
    message_ref[CELLS:, :BLOCK] = jnp.concatenate(parts[:2], axis=0).astype(jnp.bfloat16)
    tail = jnp.concatenate([parts[2], jnp.zeros_like(parts[2])], axis=0)
    message_ref[CELLS:, BLOCK:] = tail.astype(jnp.bfloat16)
    cells.wait()


def target_constants(message_ref, window_ref, region):
    parts = message_ref[CELLS:, :].astype(jnp.float32)
    masses = (parts[:NBLK, :BLOCK] + parts[NBLK:, :BLOCK]) + parts[:NBLK, BLOCK:]
    ones = jnp.ones((8, EMB), jnp.bfloat16)
    for pair in range(NBLK // 2):
        y = message_ref[pair * 256 : (pair + 1) * 256, :].astype(jnp.float32)
        square = y * y
        high = square.astype(jnp.bfloat16)
        low = (square - high.astype(jnp.float32)).astype(jnp.bfloat16)
        norm = sum(
            lax.dot_general(ones, part, (((1,), (1,)), ((), ())), preferred_element_type=jnp.float32)
            for part in (high, low)
        )
        for half in range(2):
            block = 2 * pair + half
            scaled = norm[:1, half * BLOCK : (half + 1) * BLOCK] * SCALE
            mass = masses[block : block + 1, :] * LOG2E
            at = region * NBLK + block
            window_ref[0, at : at + 1, :] = mass - scaled
            window_ref[1, at : at + 1, :] = mass + (LAM - 1.0) * scaled


STRIPS = BLOCK // 8


def extended(hh_ref, terms_ref):
    for t in range(WIN):
        terms_ref[t] = jnp.broadcast_to(hh_ref[t : t + 1, :], (8, BLOCK))
    terms_ref[WIN] = jnp.full((8, BLOCK), -BIG, jnp.float32)


def source_rows(s):
    return pl.ds(pl.multiple_of(s * BLOCK, BLOCK), BLOCK)


def group_targets(table_ref, s, q):
    return [table_ref[s * STRIDE + q * QUAD + k] for k in range(QUAD)]


def strips(g_ref, t, s):
    return g_ref[jnp.minimum(t, WIN - 1), source_rows(s), :].reshape(STRIPS, 8, BLOCK)


def row_maxima(table_ref, terms_ref, g_ref, m_ref):
    @pl.loop(0, NBLK)
    def _(s):
        def step(q, highest):
            v = [strips(g_ref, t, s) + terms_ref[t] for t in group_targets(table_ref, s, q)]
            return jnp.maximum(highest, jnp.maximum(jnp.maximum(v[0], v[1]), jnp.maximum(v[2], v[3])))

        start = jnp.full((STRIPS, 8, BLOCK), -BIG, jnp.float32)
        highest = lax.fori_loop(0, table_ref[GROUPS + s], step, start)
        m_ref[source_rows(s), :] = highest.reshape(BLOCK, BLOCK)

    m_ref[...] = jnp.broadcast_to(jnp.max(m_ref[...], axis=1, keepdims=True), m_ref.shape)


def sweep_kernel(table_ref, hh_ref, kc_ref, g_ref, part_ref, terms_ref, top_ref, mass_ref, m_ref, acc_ref):
    extended(hh_ref, terms_ref)
    top_ref[...] = jnp.full(top_ref.shape, -BIG, jnp.float32)
    mass_ref[...] = jnp.zeros(mass_ref.shape, jnp.float32)
    row_maxima(table_ref, terms_ref, g_ref, m_ref)

    @pl.loop(0, NBLK)
    def _(s):
        m = m_ref[source_rows(s), :].reshape(STRIPS, 8, BLOCK)

        def step(q, acc):
            v = [
                jnp.exp2(strips(g_ref, t, s) + terms_ref[t] - m)
                for t in group_targets(table_ref, s, q)
            ]
            return acc + ((v[0] + v[1]) + (v[2] + v[3]))

        start = jnp.zeros((STRIPS, 8, BLOCK), jnp.float32)
        acc = lax.fori_loop(0, table_ref[GROUPS + s], step, start)
        acc_ref[source_rows(s), :] = acc.reshape(BLOCK, BLOCK)

    sums = jnp.broadcast_to(jnp.sum(acc_ref[...], axis=1, keepdims=True), acc_ref.shape)
    acc_ref[...] = kc_ref[...] - LAM * (m_ref[...] + LOG2E * jnp.log(sums))

    @pl.loop(0, NBLK)
    def _(s):
        uu = acc_ref[source_rows(s), :].reshape(STRIPS, 8, BLOCK)

        @pl.loop(0, table_ref[GROUPS + s])
        def _(q):
            ts = group_targets(table_ref, s, q)
            tops = [top_ref[t] for t in ts]
            masses = [mass_ref[t] for t in ts]
            made = []
            for t, top, mass in zip(ts, tops, masses):
                v = strips(g_ref, t, s) + uu
                high = jnp.maximum(top, jnp.max(v, axis=0))
                made.append((high, mass * jnp.exp2(top - high) + jnp.sum(jnp.exp2(v - high), axis=0)))
            for t, (high, mass) in zip(ts, made):
                top_ref[t] = high
                mass_ref[t] = mass

    top = top_ref[:WIN]
    high = jnp.max(top, axis=1, keepdims=True)
    part_ref[0] = high[:, 0, :]
    part_ref[1] = jnp.sum(mass_ref[:WIN] * jnp.exp2(top - high), axis=1)


def weigh(table_ref, hh_ref, g_ref, w_ref, sum_ref, terms_ref, m_ref):
    extended(hh_ref, terms_ref)
    row_maxima(table_ref, terms_ref, g_ref, m_ref)

    @pl.loop(0, NBLK)
    def _(s):
        rows = source_rows(s)
        m = m_ref[rows, :].reshape(STRIPS, 8, BLOCK)
        w_ref[rows, :] = jnp.zeros((BLOCK, (WIN + 1) * BLOCK), jnp.bfloat16)

        def step(q, acc):
            ts = group_targets(table_ref, s, q)
            v = [jnp.exp2(strips(g_ref, t, s) + terms_ref[t] - m) for t in ts]
            for t, e in zip(ts, v):
                lanes = pl.ds(pl.multiple_of(t * BLOCK, BLOCK), BLOCK)
                w_ref[rows, lanes] = e.reshape(BLOCK, BLOCK).astype(jnp.bfloat16)
            return acc + ((v[0] + v[1]) + (v[2] + v[3]))

        start = jnp.zeros((STRIPS, 8, BLOCK), jnp.float32)
        acc = lax.fori_loop(0, table_ref[GROUPS + s], step, start)
        sum_ref[rows, :] = acc.reshape(BLOCK, BLOCK)

    sum_ref[...] = jnp.broadcast_to(jnp.sum(sum_ref[...], axis=1, keepdims=True), sum_ref.shape)


def pulled(w_ref, rows, fate_refs, first):
    total = 0.0
    for region, fate_ref in enumerate(fate_refs, first):
        total += jnp.dot(
            w_ref[rows, region * CELLS : (region + 1) * CELLS],
            fate_ref[...],
            preferred_element_type=jnp.float32,
        )
    return total


def divided(total, sums):
    inverse = 1.0 / sums
    return (total * jnp.concatenate([inverse, inverse], axis=1)).astype(jnp.bfloat16)


def chunks(body):
    @pl.loop(0, 4)
    def _(chunk):
        body(pl.ds(pl.multiple_of(chunk * 256, 256), 256))


def near_kernel(place_ref, cells_hbm, mass_hbm, own_ref, sib_ref, g_ref, kc_ref, window_ref, source_ref, mass_ref, sems):
    group = place_ref[1]
    copies = (
        pltpu.make_async_copy(cells_hbm.at[group], source_ref, sems.at[0]),
        pltpu.make_async_copy(mass_hbm, mass_ref, sems.at[1]),
    )
    for copy in copies:
        copy.start()
    target_constants(own_ref, window_ref, 0)
    target_constants(sib_ref, window_ref, 1)
    copies[0].wait()
    products(source_ref, (own_ref, sib_ref), g_ref, 0)
    copies[1].wait()
    masses = block_masses(mass_ref, group, 0)
    for s in range(NBLK):
        x = source_ref[s * BLOCK : (s + 1) * BLOCK, :].astype(jnp.float32)
        norm = jnp.sum(x * x, axis=1, keepdims=True) * SCALE
        mass = jnp.broadcast_to(masses[s : s + 1, :], (BLOCK, BLOCK)).T
        kc_ref[s * BLOCK : (s + 1) * BLOCK, :] = mass * LOG2E + (LAM - 1.0) * norm


def far_kernel(table_ref, source_ref, out_ref, near_ref, near_window_ref, g_ref, window_ref):
    del table_ref, near_ref
    window_ref[:, : 2 * NBLK, :] = near_window_ref[...]
    products(source_ref, (out_ref,), g_ref, 2)
    target_constants(out_ref, window_ref, 2)


def other_kernel(behind_ref, source_ref, own_ref, sib_ref, out_ref, g_ref):
    del behind_ref
    products(source_ref, [ref.at[:CELLS] for ref in (own_ref, sib_ref, out_ref)], g_ref, 0)


def weigh_one(coupling, place_ref, mine, others, *outs):
    @pl.when(place_ref[1] == coupling)
    def _():
        weigh(*mine, *outs)

    @pl.when(place_ref[1] != coupling)
    def _():
        weigh(*others, *outs)


def late_kernel(place_ref, table_ref, hh_ref, g_ref, table2_ref, hh2_ref, g2_ref, own_ref, sib_ref, out_ref, late_ref, w_ref, sum_ref, terms_ref, m_ref):
    weigh_one(1, place_ref, (table_ref, hh_ref, g_ref), (table2_ref, hh2_ref, g2_ref), w_ref, sum_ref, terms_ref, m_ref)
    fates = [ref.at[CELLS:] for ref in (own_ref, sib_ref, out_ref)]

    @chunks
    def _(rows):
        late_ref[rows, :] = divided(pulled(w_ref, rows, fates, 0), sum_ref[rows, :])


def early_weights_kernel(place_ref, table_ref, hh_ref, g_ref, table2_ref, hh2_ref, g2_ref, w_ref, sum_ref, terms_ref, m_ref):
    weigh_one(0, place_ref, (table_ref, hh_ref, g_ref), (table2_ref, hh2_ref, g2_ref), w_ref, sum_ref, terms_ref, m_ref)


def early_near_kernel(w_ref, own_ref, sib_ref, total_ref):
    @chunks
    def _(rows):
        total_ref[rows, :] = pulled(w_ref, rows, (own_ref, sib_ref), 0)


def early_kernel(w_ref, sum_ref, total_ref, out_ref, early_ref):
    @chunks
    def _(rows):
        total = total_ref[rows, :] + pulled(w_ref, rows, (out_ref,), 2)
        early_ref[rows, :] = divided(total, sum_ref[rows, :])


G_SHAPE = pltpu.VMEM((WIN, CELLS, BLOCK), jnp.float32)
PART_SHAPE = jax.ShapeDtypeStruct((2, WIN, BLOCK), jnp.float32)
W_SHAPE = jax.ShapeDtypeStruct((CELLS, (WIN + 1) * BLOCK), jnp.bfloat16)
COLUMN_SHAPE = jax.ShapeDtypeStruct((CELLS, BLOCK), jnp.float32)
FATE_SHAPE = jax.ShapeDtypeStruct((CELLS, EMB), jnp.bfloat16)
TOTAL_SHAPE = jax.ShapeDtypeStruct((CELLS, EMB), jnp.float32)
TERMS = pltpu.VMEM((WIN + 1, 8, BLOCK), jnp.float32)
COLUMN = pltpu.VMEM(COLUMN_SHAPE.shape, COLUMN_SHAPE.dtype)
SWEEP_SCRATCH = [TERMS] * 3 + [COLUMN] * 2
HOLD = [pltpu.VMEM(W_SHAPE.shape, W_SHAPE.dtype), COLUMN]


WINDOW_SHAPE = jax.ShapeDtypeStruct((2, WIN, BLOCK), jnp.float32)
NEAR_SHAPE = jax.ShapeDtypeStruct((2, 2 * NBLK, BLOCK), jnp.float32)


def build_table(place, behind, slots):
    specs = [SMEM, ANY] + [SMEM] * len(slots)
    return call(table_kernel, jax.ShapeDtypeStruct((TABLE,), jnp.int32), SMEM, specs)(place, behind, *slots)


MESSAGE_SHAPE = jax.ShapeDtypeStruct((CELLS + 16, EMB), jnp.bfloat16)
MASSES = pltpu.VMEM((3, CELLS), jnp.float32)


def target_message(*args):
    scratch = [MASSES, pltpu.SemaphoreType.DMA((2,))]
    return call(pack_kernel, MESSAGE_SHAPE, VMEM, [SMEM, HBM, HBM], scratch)(*args)


def near_products(*args):
    outs = (G_SHAPE, COLUMN_SHAPE, NEAR_SHAPE, FATE_SHAPE)
    scratch = [MASSES, pltpu.SemaphoreType.DMA((2,))]
    return call(near_kernel, outs, (VMEM,) * 4, [SMEM, HBM, HBM, VMEM, VMEM], scratch)(*args)


def far_products(*args):
    return call(far_kernel, (G_SHAPE, WINDOW_SHAPE), (VMEM,) * 2, [SMEM] + [VMEM] * 4, aliases={3: 0})(*args)


def sweep(*args):
    return call(sweep_kernel, PART_SHAPE, VMEM, [SMEM] + [VMEM] * 3, SWEEP_SCRATCH)(*args)


def other_products(*args):
    return call(other_kernel, G_SHAPE, VMEM, [ANY] + [VMEM] * 4)(*args)


COUPLINGS = [SMEM, SMEM, VMEM, VMEM, SMEM, VMEM, VMEM]


def late_fates(*args):
    return call(late_kernel, FATE_SHAPE, VMEM, COUPLINGS + [VMEM] * 3, HOLD + [TERMS, COLUMN], mib=9)(*args)


def early_weights(*args):
    return call(early_weights_kernel, (W_SHAPE, COLUMN_SHAPE), (VMEM, VMEM), COUPLINGS, [TERMS, COLUMN])(*args)


def early_near(*args):
    return call(early_near_kernel, TOTAL_SHAPE, VMEM, [VMEM] * 3)(*args)


def early_fates(*args):
    return call(early_kernel, FATE_SHAPE, VMEM, [VMEM] * 4)(*args)


def merged(first, second):
    highest = jnp.maximum(first[0], second[0])
    return jnp.stack(
        [
            highest,
            first[1] * jnp.exp2(first[0] - highest) + second[1] * jnp.exp2(second[0] - highest),
        ]
    )


def folded(part, beside):
    own = merged(part[:, :NBLK], sibling(part[:, NBLK : 2 * NBLK]))
    beyond = part[:, 2 * NBLK :]
    message = jnp.concatenate([own, beyond], axis=1)
    arrived, made = lax.optimization_barrier((outward(message), beside(message)))
    own = merged(own, arrived[:, NBLK:])
    out = merged(arrived[:, :NBLK], beyond)
    own_total = own[0] + jnp.log2(own[1])
    out_total = out[0] + jnp.log2(out[1])
    return jnp.concatenate([own_total, sibling(own_total), out_total], axis=0), made


def shifted(value, steps):
    count = lax.axis_size("tiles")
    return lax.ppermute(value, "tiles", [(t, (t + steps) % count) for t in range(count)])


def on_device(embeddings, log_mass, signatures, tile_list):
    owner = lax.axis_index("cells").astype(jnp.int32)
    group = (lax.axis_index("tiles") >= 2).astype(jnp.int32)
    place, place_other = jnp.stack([owner, group]), jnp.stack([owner, 1 - group])

    def moment(array, index):
        return lax.dynamic_index_in_dim(array, index, 0, keepdims=False)

    cells, masses = (
        pltpu.with_memory_space_constraint(array, pltpu.HBM) for array in (embeddings, log_mass)
    )
    target = target_message(place, cells, masses)
    target_out, target_sib = outward(target), sibling(target)
    slots, target_sib = lax.optimization_barrier((tile_list, target_sib))
    gathered = [slots] + [shifted(slots, k) for k in range(1, lax.axis_size("tiles"))]
    g, kc, near, source = near_products(place, cells, masses, target, target_sib)
    table = build_table(place, near, gathered)
    later, fates, near = lax.optimization_barrier((embeddings, signatures, near))
    rest = jnp.concatenate([moment(later, 2 - group), fates])
    other_source = moment(later, 1 - group)
    g, window = far_products(table, source, target_out, g, near)
    part = sweep(table, window[0], kc, g)
    rest_out, rest_sib = outward(rest), sibling(rest)

    totals, g_other = folded(
        part, lambda message: other_products(message, other_source, rest, rest_sib, rest_out)
    )
    hh = window[1] - LAM * totals
    part = sweep(table, hh, kc, g)
    totals, table_other = folded(part, lambda message: build_table(place_other, message, gathered))
    hh = window[1] - LAM * totals
    couplings = (place, table, hh, g, table_other, mirrored(hh), g_other)
    late = late_fates(*couplings, rest, rest_sib, rest_out)
    late_out, late_sib = outward(late), sibling(late)
    weights, sums = early_weights(*couplings)
    total = early_near(weights, late, late_sib)
    early = early_fates(weights, sums, total, late_out)
    return early, late


def solution(mesh):
    in_specs = (
        P(None, "cells", None),
        P(None, "cells"),
        P("cells", None),
        P(None, None, ("cells", "tiles")),
    )
    out_specs = (P("cells", None), P("cells", None))
    return jax.shard_map(
        on_device, mesh=mesh, in_specs=in_specs, out_specs=out_specs, check_vma=False
    )
```

```python
import jax
import jax.numpy as jnp
from jax import lax
from jax.experimental import pallas as pl
from jax.experimental.pallas import tpu as pltpu
from jax.sharding import PartitionSpec as P

EMB = 256
BLOCK = 128
NBLK = 8
WIN = 3 * NBLK
CELLS = NBLK * BLOCK
EPS = 0.01
RHO = 1.0
LAM = RHO / (RHO + EPS)
BIG = 1e30

LOG2E = 1.4426950408889634
SCALE = LOG2E / (EMB * EPS)

QUAD = 4
STRIDE = WIN + QUAD
GROUPS = 384
TABLE = 512

FLOPS, BYTES, MIB = 3 * 10**9, 10**4, 4
VMEM = pl.BlockSpec(memory_space=pltpu.VMEM)
SMEM = pl.BlockSpec(memory_space=pltpu.SMEM)
ANY = pl.BlockSpec(memory_space=pl.ANY)
HBM = pl.BlockSpec(memory_space=pltpu.HBM)


def sibling(value):
    return lax.ppermute(value, "cells", [(c, c ^ 1) for c in range(lax.axis_size("cells"))])


def outward(value):
    count = lax.axis_size("cells")
    pairs = [(c, (c + 1 if c % 2 else c - 1) % count) for c in range(count)]
    return lax.ppermute(value, "cells", pairs)


def mirrored(value):
    count = lax.axis_size("tiles")
    return lax.ppermute(value, "tiles", [(t, count - 1 - t) for t in range(count)])


def call(kernel, outs, out_specs, in_specs, scratch=(), aliases=None, flops=FLOPS, mib=MIB):
    return pl.pallas_call(
        kernel,
        out_shape=outs,
        in_specs=in_specs,
        out_specs=out_specs,
        scratch_shapes=list(scratch),
        input_output_aliases=aliases or {},
        compiler_params=pltpu.CompilerParams(vmem_limit_bytes=mib << 20),
        cost_estimate=pl.CostEstimate(flops=flops, bytes_accessed=BYTES, transcendentals=0),
    )


def start_table(table_ref):
    for s in range(NBLK + 1):
        table_ref[GROUPS + s] = 0


def extend_table(place_ref, coupling, slot_refs, table_ref, step):
    owner = place_ref[0]
    share = slot_refs[0].shape[2] // 4
    for index in range(share):
        for slot_ref in slot_refs:
            source = slot_ref[coupling, 0, step * share + index]
            target = slot_ref[coupling, 1, step * share + index]
            away = target >> 3
            region = jnp.where(away == owner, 0, jnp.where(away == (owner ^ 1), NBLK, 2 * NBLK))
            s = jnp.where(source < 0, NBLK, source & 7)
            count = table_ref[GROUPS + s]
            table_ref[GROUPS + s] = count + 1
            table_ref[s * STRIDE + count] = region + (target & 7)


def close_table(table_ref):
    for s in range(NBLK):
        count = table_ref[GROUPS + s]
        for extra in range(QUAD - 1):
            table_ref[s * STRIDE + count + extra] = WIN
        table_ref[GROUPS + s] = (count + QUAD - 1) >> 2


def products(source_ref, target_refs, g_ref, first, beside=None):
    for region, target_ref in enumerate(target_refs, first):

        @pl.loop(0, NBLK // 2)
        def _(pair):
            if beside is not None and region == first:
                beside(pair)
            rows = target_ref[pl.ds(pl.multiple_of(pair * 256, 256), 256), :]
            g = lax.dot_general(
                source_ref[...], rows, (((1,), (1,)), ((), ())), preferred_element_type=jnp.float32
            ) * (2.0 * SCALE)
            g_ref[region * NBLK + 2 * pair] = g[:, :BLOCK]
            g_ref[region * NBLK + 2 * pair + 1] = g[:, BLOCK:]


def block_masses(mass_ref, group, first):
    rows = []
    for block in range(NBLK):
        lanes = slice(block * BLOCK, (block + 1) * BLOCK)
        low, high = mass_ref[first : first + 1, lanes], mass_ref[first + 1 : first + 2, lanes]
        rows.append(jnp.where(group == 0, low, high))
    return jnp.concatenate(rows, axis=0)


def pack_kernel(place_ref, cells_hbm, mass_hbm, message_ref, mass_ref, sems):
    group = place_ref[1]
    cells = pltpu.make_async_copy(cells_hbm.at[group + 1], message_ref.at[:CELLS], sems.at[0])
    fetched = pltpu.make_async_copy(mass_hbm, mass_ref, sems.at[1])
    cells.start()
    fetched.start()
    fetched.wait()
    masses = block_masses(mass_ref, group, 1) * LOG2E
    cells.wait()
    ones = jnp.ones((8, EMB), jnp.bfloat16)
    norms = []
    for pair in range(NBLK // 2):
        y = message_ref[pair * 256 : (pair + 1) * 256, :].astype(jnp.float32)
        square = y * y
        high = square.astype(jnp.bfloat16)
        low = (square - high.astype(jnp.float32)).astype(jnp.bfloat16)
        norm = sum(
            lax.dot_general(ones, part, (((1,), (1,)), ((), ())), preferred_element_type=jnp.float32)
            for part in (high, low)
        )
        norms += [norm[:1, :BLOCK], norm[:1, BLOCK:]]
    norms = jnp.concatenate(norms, axis=0) * SCALE
    for half, left in enumerate((masses - norms, masses + (LAM - 1.0) * norms)):
        parts = []
        for _ in range(3):
            part = left.astype(jnp.bfloat16).astype(jnp.float32)
            parts.append(part)
            left = left - part
        parts.append(jnp.zeros_like(left))
        packed = jnp.concatenate(parts, axis=0).astype(jnp.bfloat16)
        message_ref[CELLS:, half * BLOCK : (half + 1) * BLOCK] = packed


def unpack(message_ref, window_ref, region):
    parts = message_ref[CELLS:, :].astype(jnp.float32)
    for half in range(2):
        p = parts[:, half * BLOCK : (half + 1) * BLOCK]
        total = (p[:NBLK] + p[NBLK : 2 * NBLK]) + p[2 * NBLK : 3 * NBLK]
        window_ref[half, region * NBLK : (region + 1) * NBLK, :] = total


STRIPS = BLOCK // 8


def extended(hh_ref, terms_ref):
    for t in range(WIN):
        terms_ref[t] = jnp.broadcast_to(hh_ref[t : t + 1, :], (8, BLOCK))
    terms_ref[WIN] = jnp.full((8, BLOCK), -BIG, jnp.float32)


def source_rows(s):
    return pl.ds(pl.multiple_of(s * BLOCK, BLOCK), BLOCK)


def group_targets(table_ref, s, q):
    return [table_ref[s * STRIDE + q * QUAD + k] for k in range(QUAD)]


def strips(g_ref, t, s):
    return g_ref[jnp.minimum(t, WIN - 1), source_rows(s), :].reshape(STRIPS, 8, BLOCK)


def row_maxima(table_ref, terms_ref, g_ref, m_ref):
    @pl.loop(0, NBLK)
    def _(s):
        def step(q, highest):
            v = [strips(g_ref, t, s) + terms_ref[t] for t in group_targets(table_ref, s, q)]
            return jnp.maximum(highest, jnp.maximum(jnp.maximum(v[0], v[1]), jnp.maximum(v[2], v[3])))

        start = jnp.full((STRIPS, 8, BLOCK), -BIG, jnp.float32)
        highest = lax.fori_loop(0, table_ref[GROUPS + s], step, start)
        m_ref[source_rows(s), :] = highest.reshape(BLOCK, BLOCK)

    m_ref[...] = jnp.broadcast_to(jnp.max(m_ref[...], axis=1, keepdims=True), m_ref.shape)


def sweep_kernel(table_ref, hh_ref, kc_ref, g_ref, part_ref, terms_ref, top_ref, mass_ref, m_ref, acc_ref):
    extended(hh_ref, terms_ref)
    top_ref[...] = jnp.full(top_ref.shape, -BIG, jnp.float32)
    mass_ref[...] = jnp.zeros(mass_ref.shape, jnp.float32)
    row_maxima(table_ref, terms_ref, g_ref, m_ref)

    @pl.loop(0, NBLK)
    def _(s):
        m = m_ref[source_rows(s), :].reshape(STRIPS, 8, BLOCK)

        def step(q, acc):
            v = [
                jnp.exp2(strips(g_ref, t, s) + terms_ref[t] - m)
                for t in group_targets(table_ref, s, q)
            ]
            return acc + ((v[0] + v[1]) + (v[2] + v[3]))

        start = jnp.zeros((STRIPS, 8, BLOCK), jnp.float32)
        acc = lax.fori_loop(0, table_ref[GROUPS + s], step, start)
        acc_ref[source_rows(s), :] = acc.reshape(BLOCK, BLOCK)

    sums = jnp.broadcast_to(jnp.sum(acc_ref[...], axis=1, keepdims=True), acc_ref.shape)
    acc_ref[...] = kc_ref[...] - LAM * (m_ref[...] + LOG2E * jnp.log(sums))

    @pl.loop(0, NBLK)
    def _(s):
        uu = acc_ref[source_rows(s), :].reshape(STRIPS, 8, BLOCK)

        @pl.loop(0, table_ref[GROUPS + s])
        def _(q):
            ts = group_targets(table_ref, s, q)
            tops = [top_ref[t] for t in ts]
            masses = [mass_ref[t] for t in ts]
            made = []
            for t, top, mass in zip(ts, tops, masses):
                v = strips(g_ref, t, s) + uu
                high = jnp.maximum(top, jnp.max(v, axis=0))
                made.append((high, mass * jnp.exp2(top - high) + jnp.sum(jnp.exp2(v - high), axis=0)))
            for t, (high, mass) in zip(ts, made):
                top_ref[t] = high
                mass_ref[t] = mass

    top = top_ref[:WIN]
    high = jnp.max(top, axis=1, keepdims=True)
    part_ref[0] = high[:, 0, :]
    part_ref[1] = jnp.sum(mass_ref[:WIN] * jnp.exp2(top - high), axis=1)


def weigh(table_ref, hh_ref, g_ref, w_ref, sum_ref, terms_ref, m_ref):
    extended(hh_ref, terms_ref)
    row_maxima(table_ref, terms_ref, g_ref, m_ref)

    @pl.loop(0, NBLK)
    def _(s):
        rows = source_rows(s)
        m = m_ref[rows, :].reshape(STRIPS, 8, BLOCK)
        w_ref[rows, :] = jnp.zeros((BLOCK, (WIN + 1) * BLOCK), jnp.bfloat16)

        def step(q, acc):
            ts = group_targets(table_ref, s, q)
            v = [jnp.exp2(strips(g_ref, t, s) + terms_ref[t] - m) for t in ts]
            for t, e in zip(ts, v):
                lanes = pl.ds(pl.multiple_of(t * BLOCK, BLOCK), BLOCK)
                w_ref[rows, lanes] = e.reshape(BLOCK, BLOCK).astype(jnp.bfloat16)
            return acc + ((v[0] + v[1]) + (v[2] + v[3]))

        start = jnp.zeros((STRIPS, 8, BLOCK), jnp.float32)
        acc = lax.fori_loop(0, table_ref[GROUPS + s], step, start)
        sum_ref[rows, :] = acc.reshape(BLOCK, BLOCK)

    sum_ref[...] = jnp.broadcast_to(jnp.sum(sum_ref[...], axis=1, keepdims=True), sum_ref.shape)


def pulled(w_ref, rows, fate_refs, first):
    total = 0.0
    for region, fate_ref in enumerate(fate_refs, first):
        total += jnp.dot(
            w_ref[rows, region * CELLS : (region + 1) * CELLS],
            fate_ref[...],
            preferred_element_type=jnp.float32,
        )
    return total


def divided(total, sums):
    inverse = 1.0 / sums
    return (total * jnp.concatenate([inverse, inverse], axis=1)).astype(jnp.bfloat16)


def chunks(body):
    @pl.loop(0, 4)
    def _(chunk):
        body(pl.ds(pl.multiple_of(chunk * 256, 256), 256))


def near_kernel(place_ref, *refs):
    *slot_refs, cells_hbm, mass_hbm, own_ref, sib_ref = refs[: len(refs) - 7]
    g_ref, kc_ref, window_ref, source_ref, table_ref, mass_ref, sems = refs[len(refs) - 7 :]
    group = place_ref[1]
    copies = (
        pltpu.make_async_copy(cells_hbm.at[group], source_ref, sems.at[0]),
        pltpu.make_async_copy(mass_hbm, mass_ref, sems.at[1]),
    )
    for copy in copies:
        copy.start()
    unpack(own_ref, window_ref, 0)
    unpack(sib_ref, window_ref, 1)
    copies[0].wait()
    start_table(table_ref)
    products(
        source_ref,
        (own_ref, sib_ref),
        g_ref,
        0,
        lambda step: extend_table(place_ref, place_ref[1], slot_refs, table_ref, step),
    )
    close_table(table_ref)
    copies[1].wait()
    masses = block_masses(mass_ref, group, 0)
    for s in range(NBLK):
        x = source_ref[s * BLOCK : (s + 1) * BLOCK, :].astype(jnp.float32)
        norm = jnp.sum(x * x, axis=1, keepdims=True) * SCALE
        mass = jnp.broadcast_to(masses[s : s + 1, :], (BLOCK, BLOCK)).T
        kc_ref[s * BLOCK : (s + 1) * BLOCK, :] = mass * LOG2E + (LAM - 1.0) * norm


def far_kernel(table_ref, source_ref, out_ref, near_ref, near_window_ref, kc_ref, g_ref, window_ref, part_ref, *scratch):
    del near_ref
    window_ref[:, : 2 * NBLK, :] = near_window_ref[...]
    unpack(out_ref, window_ref, 2)
    products(source_ref, (out_ref,), g_ref, 2)
    sweep_kernel(table_ref, window_ref.at[0], kc_ref, g_ref, part_ref, *scratch)


def other_kernel(place_ref, behind_ref, *refs):
    *slot_refs, source_ref, own_ref, sib_ref, out_ref, g_ref, table_ref = refs
    del behind_ref
    start_table(table_ref)
    products(
        source_ref,
        [ref.at[:CELLS] for ref in (own_ref, sib_ref, out_ref)],
        g_ref,
        0,
        lambda step: extend_table(place_ref, 1 - place_ref[1], slot_refs, table_ref, step),
    )
    close_table(table_ref)


def weigh_one(coupling, place_ref, mine, others, *outs):
    @pl.when(place_ref[1] == coupling)
    def _():
        weigh(*mine, *outs)

    @pl.when(place_ref[1] != coupling)
    def _():
        weigh(*others, *outs)


def late_kernel(place_ref, table_ref, hh_ref, g_ref, table2_ref, hh2_ref, g2_ref, own_ref, sib_ref, out_ref, late_ref, w_ref, sum_ref, terms_ref, m_ref):
    weigh_one(1, place_ref, (table_ref, hh_ref, g_ref), (table2_ref, hh2_ref, g2_ref), w_ref, sum_ref, terms_ref, m_ref)
    fates = [ref.at[CELLS:] for ref in (own_ref, sib_ref, out_ref)]

    @chunks
    def _(rows):
        late_ref[rows, :] = divided(pulled(w_ref, rows, fates, 0), sum_ref[rows, :])


def early_weights_kernel(place_ref, table_ref, hh_ref, g_ref, table2_ref, hh2_ref, g2_ref, w_ref, sum_ref, terms_ref, m_ref):
    weigh_one(0, place_ref, (table_ref, hh_ref, g_ref), (table2_ref, hh2_ref, g2_ref), w_ref, sum_ref, terms_ref, m_ref)


def early_near_kernel(w_ref, own_ref, sib_ref, total_ref):
    @chunks
    def _(rows):
        total_ref[rows, :] = pulled(w_ref, rows, (own_ref, sib_ref), 0)


def early_kernel(w_ref, sum_ref, total_ref, out_ref, early_ref):
    @chunks
    def _(rows):
        total = total_ref[rows, :] + pulled(w_ref, rows, (out_ref,), 2)
        early_ref[rows, :] = divided(total, sum_ref[rows, :])


G_SHAPE = pltpu.VMEM((WIN, CELLS, BLOCK), jnp.float32)
PART_SHAPE = jax.ShapeDtypeStruct((2, WIN, BLOCK), jnp.float32)
W_SHAPE = jax.ShapeDtypeStruct((CELLS, (WIN + 1) * BLOCK), jnp.bfloat16)
COLUMN_SHAPE = jax.ShapeDtypeStruct((CELLS, BLOCK), jnp.float32)
FATE_SHAPE = jax.ShapeDtypeStruct((CELLS, EMB), jnp.bfloat16)
TOTAL_SHAPE = jax.ShapeDtypeStruct((CELLS, EMB), jnp.float32)
TERMS = pltpu.VMEM((WIN + 1, 8, BLOCK), jnp.float32)
COLUMN = pltpu.VMEM(COLUMN_SHAPE.shape, COLUMN_SHAPE.dtype)
SWEEP_SCRATCH = [TERMS] * 3 + [COLUMN] * 2
HOLD = [pltpu.VMEM(W_SHAPE.shape, W_SHAPE.dtype), COLUMN]


WINDOW_SHAPE = jax.ShapeDtypeStruct((2, WIN, BLOCK), jnp.float32)
NEAR_SHAPE = jax.ShapeDtypeStruct((2, 2 * NBLK, BLOCK), jnp.float32)


TABLE_SHAPE = jax.ShapeDtypeStruct((TABLE,), jnp.int32)
MESSAGE_SHAPE = jax.ShapeDtypeStruct((CELLS + 4 * NBLK, EMB), jnp.bfloat16)
MASSES = pltpu.VMEM((3, CELLS), jnp.float32)


def target_message(*args):
    scratch = [MASSES, pltpu.SemaphoreType.DMA((2,))]
    return call(pack_kernel, MESSAGE_SHAPE, VMEM, [SMEM, HBM, HBM], scratch)(*args)


def near_products(place, slots, *args):
    outs = (G_SHAPE, COLUMN_SHAPE, NEAR_SHAPE, FATE_SHAPE, TABLE_SHAPE)
    in_specs = [SMEM] * (1 + len(slots)) + [HBM, HBM, VMEM, VMEM]
    scratch = [MASSES, pltpu.SemaphoreType.DMA((2,))]
    return call(near_kernel, outs, (VMEM,) * 4 + (SMEM,), in_specs, scratch)(place, *slots, *args)


def far_products(*args):
    outs = (G_SHAPE, WINDOW_SHAPE, PART_SHAPE)
    return call(far_kernel, outs, (VMEM,) * 3, [SMEM] + [VMEM] * 5, SWEEP_SCRATCH, {3: 0})(*args)


def sweep(*args):
    return call(sweep_kernel, PART_SHAPE, VMEM, [SMEM] + [VMEM] * 3, SWEEP_SCRATCH)(*args)


def other_products(place, behind, slots, *args):
    in_specs = [SMEM, ANY] + [SMEM] * len(slots) + [VMEM] * 4
    return call(other_kernel, (G_SHAPE, TABLE_SHAPE), (VMEM, SMEM), in_specs)(place, behind, *slots, *args)


COUPLINGS = [SMEM, SMEM, VMEM, VMEM, SMEM, VMEM, VMEM]


def late_fates(*args):
    return call(late_kernel, FATE_SHAPE, VMEM, COUPLINGS + [VMEM] * 3, HOLD + [TERMS, COLUMN], mib=9)(*args)


def early_weights(*args):
    return call(early_weights_kernel, (W_SHAPE, COLUMN_SHAPE), (VMEM, VMEM), COUPLINGS, [TERMS, COLUMN])(*args)


def early_near(*args):
    return call(early_near_kernel, TOTAL_SHAPE, VMEM, [VMEM] * 3)(*args)


def early_fates(*args):
    return call(early_kernel, FATE_SHAPE, VMEM, [VMEM] * 4)(*args)


def merged(first, second):
    highest = jnp.maximum(first[0], second[0])
    return jnp.stack(
        [
            highest,
            first[1] * jnp.exp2(first[0] - highest) + second[1] * jnp.exp2(second[0] - highest),
        ]
    )


def folded(part, beside=lambda message: None):
    own = merged(part[:, :NBLK], sibling(part[:, NBLK : 2 * NBLK]))
    beyond = part[:, 2 * NBLK :]
    message = jnp.concatenate([own, beyond], axis=1)
    arrived, made = lax.optimization_barrier((outward(message), beside(message)))
    own = merged(own, arrived[:, NBLK:])
    out = merged(arrived[:, :NBLK], beyond)
    own_total = own[0] + jnp.log2(own[1])
    out_total = out[0] + jnp.log2(out[1])
    return jnp.concatenate([own_total, sibling(own_total), out_total], axis=0), made


def shifted(value, steps):
    count = lax.axis_size("tiles")
    return lax.ppermute(value, "tiles", [(t, (t + steps) % count) for t in range(count)])


def on_device(embeddings, log_mass, signatures, tile_list):
    owner = lax.axis_index("cells").astype(jnp.int32)
    group = (lax.axis_index("tiles") >= 2).astype(jnp.int32)
    place = jnp.stack([owner, group])

    def moment(array, index):
        return lax.dynamic_index_in_dim(array, index, 0, keepdims=False)

    cells, masses = (
        pltpu.with_memory_space_constraint(array, pltpu.HBM) for array in (embeddings, log_mass)
    )
    target = target_message(place, cells, masses)
    target_out, target_sib = outward(target), sibling(target)
    slots, target_sib = lax.optimization_barrier((tile_list, target_sib))
    gathered = [slots] + [shifted(slots, k) for k in range(1, lax.axis_size("tiles"))]
    g, kc, near, source, table = near_products(place, gathered, cells, masses, target, target_sib)
    later, fates, near = lax.optimization_barrier((embeddings, signatures, near))
    rest = jnp.concatenate([moment(later, 2 - group), fates])
    other_source = moment(later, 1 - group)
    g, window, part = far_products(table, source, target_out, g, near, kc)
    rest_out, rest_sib = outward(rest), sibling(rest)

    totals, (g_other, table_other) = folded(
        part,
        lambda message: other_products(
            place, message, gathered, other_source, rest, rest_sib, rest_out
        ),
    )
    hh = window[1] - LAM * totals
    part = sweep(table, hh, kc, g)
    hh = window[1] - LAM * folded(part)[0]
    couplings = (place, table, hh, g, table_other, mirrored(hh), g_other)
    late = late_fates(*couplings, rest, rest_sib, rest_out)
    late_out, late_sib = outward(late), sibling(late)
    weights, sums = early_weights(*couplings)
    total = early_near(weights, late, late_sib)
    early = early_fates(weights, sums, total, late_out)
    return early, late


def solution(mesh):
    in_specs = (
        P(None, "cells", None),
        P(None, "cells"),
        P("cells", None),
        P(None, None, ("cells", "tiles")),
    )
    out_specs = (P("cells", None), P("cells", None))
    return jax.shard_map(
        on_device, mesh=mesh, in_specs=in_specs, out_specs=out_specs, check_vma=False
    )
```

```python
import jax
import jax.numpy as jnp
from jax import lax
from jax.experimental import pallas as pl
from jax.experimental.pallas import tpu as pltpu
from jax.sharding import PartitionSpec as P

EMB = 256
BLOCK = 128
NBLK = 8
WIN = 3 * NBLK
CELLS = NBLK * BLOCK
EPS = 0.01
RHO = 1.0
LAM = RHO / (RHO + EPS)
BIG = 1e30

LOG2E = 1.4426950408889634
SCALE = LOG2E / (EMB * EPS)

QUAD = 4
STRIDE = 32
GROUPS = NBLK * STRIDE
UNREAD = GROUPS + NBLK
TABLE = 384

FLOPS, BYTES, MIB = 3 * 10**9, 10**4, 4
VMEM = pl.BlockSpec(memory_space=pltpu.VMEM)
SMEM = pl.BlockSpec(memory_space=pltpu.SMEM)
ANY = pl.BlockSpec(memory_space=pl.ANY)
HBM = pl.BlockSpec(memory_space=pltpu.HBM)


def sibling(value):
    return lax.ppermute(value, "cells", [(c, c ^ 1) for c in range(lax.axis_size("cells"))])


def outward(value):
    count = lax.axis_size("cells")
    pairs = [(c, (c + 1 if c % 2 else c - 1) % count) for c in range(count)]
    return lax.ppermute(value, "cells", pairs)


def mirrored(value):
    count = lax.axis_size("tiles")
    return lax.ppermute(value, "tiles", [(t, count - 1 - t) for t in range(count)])


def call(kernel, outs, out_specs, in_specs, scratch=(), aliases=None, flops=FLOPS, mib=MIB):
    return pl.pallas_call(
        kernel,
        out_shape=outs,
        in_specs=in_specs,
        out_specs=out_specs,
        scratch_shapes=list(scratch),
        input_output_aliases=aliases or {},
        compiler_params=pltpu.CompilerParams(vmem_limit_bytes=mib << 20),
        cost_estimate=pl.CostEstimate(flops=flops, bytes_accessed=BYTES, transcendentals=0),
    )


def build_table(place_ref, coupling, slot_refs, table_ref):
    owner = place_ref[0]
    unroll = 4

    def step(index, counts):
        low, high = counts
        for inner in range(unroll):
            for slot_ref in slot_refs:
                source = slot_ref[coupling, 0, index * unroll + inner]
                target = slot_ref[coupling, 1, index * unroll + inner]
                away = target >> 3
                region = jnp.where(away == owner, 0, jnp.where(away == (owner ^ 1), NBLK, 2 * NBLK))
                empty = source < 0
                s = source & 7
                shift = (s & 3) << 3
                lower = s < 4
                count = (jnp.where(lower, low, high) >> shift) & 255
                table_ref[jnp.where(empty, UNREAD, s * STRIDE + count)] = region + (target & 7)
                one = jnp.where(empty, 0, 1 << shift)
                low, high = low + jnp.where(lower, one, 0), high + jnp.where(lower, 0, one)
        return low, high

    zero = jnp.int32(0)
    counts = lax.fori_loop(0, slot_refs[0].shape[2] // unroll, step, (zero, zero))
    for s in range(NBLK):
        count = (counts[s // 4] >> (8 * (s % 4))) & 255
        for extra in range(QUAD - 1):
            table_ref[s * STRIDE + count + extra] = WIN
        table_ref[GROUPS + s] = (count + QUAD - 1) >> 2


def products(source_ref, target_refs, g_ref, first):
    for region, target_ref in enumerate(target_refs, first):

        @pl.loop(0, NBLK // 2)
        def _(pair):
            rows = target_ref[pl.ds(pl.multiple_of(pair * 256, 256), 256), :]
            g = lax.dot_general(
                source_ref[...], rows, (((1,), (1,)), ((), ())), preferred_element_type=jnp.float32
            ) * (2.0 * SCALE)
            g_ref[region * NBLK + 2 * pair] = g[:, :BLOCK]
            g_ref[region * NBLK + 2 * pair + 1] = g[:, BLOCK:]


def block_masses(mass_ref, group, first):
    rows = []
    for block in range(NBLK):
        lanes = slice(block * BLOCK, (block + 1) * BLOCK)
        low, high = mass_ref[first : first + 1, lanes], mass_ref[first + 1 : first + 2, lanes]
        rows.append(jnp.where(group == 0, low, high))
    return jnp.concatenate(rows, axis=0)


def pack_kernel(place_ref, cells_hbm, mass_hbm, message_ref, mass_ref, sems):
    group = place_ref[1]
    cells = pltpu.make_async_copy(cells_hbm.at[group + 1], message_ref.at[:CELLS], sems.at[0])
    fetched = pltpu.make_async_copy(mass_hbm, mass_ref, sems.at[1])
    cells.start()
    fetched.start()
    fetched.wait()
    masses = block_masses(mass_ref, group, 1) * LOG2E
    cells.wait()
    ones = jnp.ones((8, EMB), jnp.bfloat16)
    norms = []
    for pair in range(NBLK // 2):
        y = message_ref[pair * 256 : (pair + 1) * 256, :].astype(jnp.float32)
        square = y * y
        high = square.astype(jnp.bfloat16)
        low = (square - high.astype(jnp.float32)).astype(jnp.bfloat16)
        norm = sum(
            lax.dot_general(ones, part, (((1,), (1,)), ((), ())), preferred_element_type=jnp.float32)
            for part in (high, low)
        )
        norms += [norm[:1, :BLOCK], norm[:1, BLOCK:]]
    norms = jnp.concatenate(norms, axis=0) * SCALE
    for half, left in enumerate((masses - norms, masses + (LAM - 1.0) * norms)):
        parts = []
        for _ in range(3):
            part = left.astype(jnp.bfloat16).astype(jnp.float32)
            parts.append(part)
            left = left - part
        parts.append(jnp.zeros_like(left))
        packed = jnp.concatenate(parts, axis=0).astype(jnp.bfloat16)
        message_ref[CELLS:, half * BLOCK : (half + 1) * BLOCK] = packed


def unpack(message_ref, window_ref, region):
    parts = message_ref[CELLS:, :].astype(jnp.float32)
    for half in range(2):
        p = parts[:, half * BLOCK : (half + 1) * BLOCK]
        total = (p[:NBLK] + p[NBLK : 2 * NBLK]) + p[2 * NBLK : 3 * NBLK]
        window_ref[half, region * NBLK : (region + 1) * NBLK, :] = total


STRIPS = BLOCK // 8


def extended(hh_ref, terms_ref):
    for t in range(WIN):
        terms_ref[t] = jnp.broadcast_to(hh_ref[t : t + 1, :], (8, BLOCK))
    terms_ref[WIN] = jnp.full((8, BLOCK), -BIG, jnp.float32)


def source_rows(s):
    return pl.ds(pl.multiple_of(s * BLOCK, BLOCK), BLOCK)


def group_targets(table_ref, s, q):
    return [table_ref[s * STRIDE + q * QUAD + k] for k in range(QUAD)]


def strips(g_ref, t, s):
    return g_ref[jnp.minimum(t, WIN - 1), source_rows(s), :].reshape(STRIPS, 8, BLOCK)


def row_maxima(table_ref, terms_ref, g_ref, m_ref):
    @pl.loop(0, NBLK)
    def _(s):
        def step(q, highest):
            v = [strips(g_ref, t, s) + terms_ref[t] for t in group_targets(table_ref, s, q)]
            return jnp.maximum(highest, jnp.maximum(jnp.maximum(v[0], v[1]), jnp.maximum(v[2], v[3])))

        start = jnp.full((STRIPS, 8, BLOCK), -BIG, jnp.float32)
        highest = lax.fori_loop(0, table_ref[GROUPS + s], step, start)
        m_ref[source_rows(s), :] = highest.reshape(BLOCK, BLOCK)

    m_ref[...] = jnp.broadcast_to(jnp.max(m_ref[...], axis=1, keepdims=True), m_ref.shape)


def sweep_kernel(table_ref, hh_ref, kc_ref, g_ref, part_ref, terms_ref, top_ref, mass_ref, m_ref, acc_ref):
    extended(hh_ref, terms_ref)
    top_ref[...] = jnp.full(top_ref.shape, -BIG, jnp.float32)
    mass_ref[...] = jnp.zeros(mass_ref.shape, jnp.float32)
    row_maxima(table_ref, terms_ref, g_ref, m_ref)

    @pl.loop(0, NBLK)
    def _(s):
        m = m_ref[source_rows(s), :].reshape(STRIPS, 8, BLOCK)

        def step(q, acc):
            v = [
                jnp.exp2(strips(g_ref, t, s) + terms_ref[t] - m)
                for t in group_targets(table_ref, s, q)
            ]
            return acc + ((v[0] + v[1]) + (v[2] + v[3]))

        start = jnp.zeros((STRIPS, 8, BLOCK), jnp.float32)
        acc = lax.fori_loop(0, table_ref[GROUPS + s], step, start)
        acc_ref[source_rows(s), :] = acc.reshape(BLOCK, BLOCK)

    sums = jnp.broadcast_to(jnp.sum(acc_ref[...], axis=1, keepdims=True), acc_ref.shape)
    acc_ref[...] = kc_ref[...] - LAM * (m_ref[...] + LOG2E * jnp.log(sums))

    @pl.loop(0, NBLK)
    def _(s):
        uu = acc_ref[source_rows(s), :].reshape(STRIPS, 8, BLOCK)

        @pl.loop(0, table_ref[GROUPS + s])
        def _(q):
            ts = group_targets(table_ref, s, q)
            tops = [top_ref[t] for t in ts]
            masses = [mass_ref[t] for t in ts]
            made = []
            for t, top, mass in zip(ts, tops, masses):
                v = strips(g_ref, t, s) + uu
                high = jnp.maximum(top, jnp.max(v, axis=0))
                made.append((high, mass * jnp.exp2(top - high) + jnp.sum(jnp.exp2(v - high), axis=0)))
            for t, (high, mass) in zip(ts, made):
                top_ref[t] = high
                mass_ref[t] = mass

    top = top_ref[:WIN]
    high = jnp.max(top, axis=1, keepdims=True)
    part_ref[0] = high[:, 0, :]
    part_ref[1] = jnp.sum(mass_ref[:WIN] * jnp.exp2(top - high), axis=1)


def weigh(table_ref, hh_ref, g_ref, w_ref, sum_ref, terms_ref, m_ref):
    extended(hh_ref, terms_ref)
    row_maxima(table_ref, terms_ref, g_ref, m_ref)

    @pl.loop(0, NBLK)
    def _(s):
        rows = source_rows(s)
        m = m_ref[rows, :].reshape(STRIPS, 8, BLOCK)
        w_ref[rows, :] = jnp.zeros((BLOCK, (WIN + 1) * BLOCK), jnp.bfloat16)

        def step(q, acc):
            ts = group_targets(table_ref, s, q)
            v = [jnp.exp2(strips(g_ref, t, s) + terms_ref[t] - m) for t in ts]
            for t, e in zip(ts, v):
                lanes = pl.ds(pl.multiple_of(t * BLOCK, BLOCK), BLOCK)
                w_ref[rows, lanes] = e.reshape(BLOCK, BLOCK).astype(jnp.bfloat16)
            return acc + ((v[0] + v[1]) + (v[2] + v[3]))

        start = jnp.zeros((STRIPS, 8, BLOCK), jnp.float32)
        acc = lax.fori_loop(0, table_ref[GROUPS + s], step, start)
        sum_ref[rows, :] = acc.reshape(BLOCK, BLOCK)

    sum_ref[...] = jnp.broadcast_to(jnp.sum(sum_ref[...], axis=1, keepdims=True), sum_ref.shape)


def pulled(w_ref, rows, fate_refs, first):
    total = 0.0
    for region, fate_ref in enumerate(fate_refs, first):
        total += jnp.dot(
            w_ref[rows, region * CELLS : (region + 1) * CELLS],
            fate_ref[...],
            preferred_element_type=jnp.float32,
        )
    return total


def divided(total, sums):
    inverse = 1.0 / sums
    return (total * jnp.concatenate([inverse, inverse], axis=1)).astype(jnp.bfloat16)


def chunks(body):
    @pl.loop(0, 4)
    def _(chunk):
        body(pl.ds(pl.multiple_of(chunk * 256, 256), 256))


def near_kernel(place_ref, *refs):
    *slot_refs, cells_hbm, mass_hbm, own_ref, sib_ref = refs[: len(refs) - 7]
    g_ref, kc_ref, window_ref, source_ref, table_ref, mass_ref, sems = refs[len(refs) - 7 :]
    group = place_ref[1]
    copies = (
        pltpu.make_async_copy(cells_hbm.at[group], source_ref, sems.at[0]),
        pltpu.make_async_copy(mass_hbm, mass_ref, sems.at[1]),
    )
    for copy in copies:
        copy.start()
    unpack(own_ref, window_ref, 0)
    unpack(sib_ref, window_ref, 1)
    build_table(place_ref, place_ref[1], slot_refs, table_ref)
    copies[0].wait()
    products(source_ref, (own_ref, sib_ref), g_ref, 0)
    copies[1].wait()
    masses = block_masses(mass_ref, group, 0)
    for s in range(NBLK):
        x = source_ref[s * BLOCK : (s + 1) * BLOCK, :].astype(jnp.float32)
        norm = jnp.sum(x * x, axis=1, keepdims=True) * SCALE
        mass = jnp.broadcast_to(masses[s : s + 1, :], (BLOCK, BLOCK)).T
        kc_ref[s * BLOCK : (s + 1) * BLOCK, :] = mass * LOG2E + (LAM - 1.0) * norm


def far_kernel(table_ref, source_ref, out_ref, near_ref, near_window_ref, kc_ref, g_ref, window_ref, part_ref, *scratch):
    del near_ref
    window_ref[:, : 2 * NBLK, :] = near_window_ref[...]
    unpack(out_ref, window_ref, 2)
    products(source_ref, (out_ref,), g_ref, 2)
    sweep_kernel(table_ref, window_ref.at[0], kc_ref, g_ref, part_ref, *scratch)


def other_kernel(behind_ref, source_ref, own_ref, sib_ref, out_ref, g_ref):
    del behind_ref
    products(source_ref, (own_ref, sib_ref, out_ref), g_ref, 0)


def rest_kernel(place_ref, behind_ref, *refs):
    del behind_ref
    *slot_refs, cells_hbm, table_ref, source_ref, target_ref, sems = refs
    group = place_ref[1]
    copies = (
        pltpu.make_async_copy(cells_hbm.at[2 - group], target_ref, sems.at[0]),
        pltpu.make_async_copy(cells_hbm.at[1 - group], source_ref, sems.at[1]),
    )
    for copy in copies:
        copy.start()
    build_table(place_ref, 1 - group, slot_refs, table_ref)
    for copy in copies:
        copy.wait()


def weigh_one(coupling, place_ref, mine, others, *outs):
    @pl.when(place_ref[1] == coupling)
    def _():
        weigh(*mine, *outs)

    @pl.when(place_ref[1] != coupling)
    def _():
        weigh(*others, *outs)


def late_kernel(place_ref, table_ref, hh_ref, g_ref, table2_ref, hh2_ref, g2_ref, own_ref, sib_ref, out_ref, late_ref, w_ref, sum_ref, terms_ref, m_ref):
    weigh_one(1, place_ref, (table_ref, hh_ref, g_ref), (table2_ref, hh2_ref, g2_ref), w_ref, sum_ref, terms_ref, m_ref)
    fates = (own_ref, sib_ref, out_ref)

    @chunks
    def _(rows):
        late_ref[rows, :] = divided(pulled(w_ref, rows, fates, 0), sum_ref[rows, :])


def early_weights_kernel(place_ref, table_ref, hh_ref, g_ref, table2_ref, hh2_ref, g2_ref, w_ref, sum_ref, terms_ref, m_ref):
    weigh_one(0, place_ref, (table_ref, hh_ref, g_ref), (table2_ref, hh2_ref, g2_ref), w_ref, sum_ref, terms_ref, m_ref)


def early_near_kernel(w_ref, own_ref, sib_ref, total_ref):
    @chunks
    def _(rows):
        total_ref[rows, :] = pulled(w_ref, rows, (own_ref, sib_ref), 0)


def early_kernel(w_ref, sum_ref, total_ref, out_ref, early_ref):
    @chunks
    def _(rows):
        total = total_ref[rows, :] + pulled(w_ref, rows, (out_ref,), 2)
        early_ref[rows, :] = divided(total, sum_ref[rows, :])


G_SHAPE = pltpu.VMEM((WIN, CELLS, BLOCK), jnp.float32)
PART_SHAPE = jax.ShapeDtypeStruct((2, WIN, BLOCK), jnp.float32)
W_SHAPE = jax.ShapeDtypeStruct((CELLS, (WIN + 1) * BLOCK), jnp.bfloat16)
COLUMN_SHAPE = jax.ShapeDtypeStruct((CELLS, BLOCK), jnp.float32)
FATE_SHAPE = jax.ShapeDtypeStruct((CELLS, EMB), jnp.bfloat16)
TOTAL_SHAPE = jax.ShapeDtypeStruct((CELLS, EMB), jnp.float32)
TERMS = pltpu.VMEM((WIN + 1, 8, BLOCK), jnp.float32)
COLUMN = pltpu.VMEM(COLUMN_SHAPE.shape, COLUMN_SHAPE.dtype)
SWEEP_SCRATCH = [TERMS] * 3 + [COLUMN] * 2
HOLD = [pltpu.VMEM(W_SHAPE.shape, W_SHAPE.dtype), COLUMN]


WINDOW_SHAPE = jax.ShapeDtypeStruct((2, WIN, BLOCK), jnp.float32)
NEAR_SHAPE = jax.ShapeDtypeStruct((2, 2 * NBLK, BLOCK), jnp.float32)


TABLE_SHAPE = jax.ShapeDtypeStruct((TABLE,), jnp.int32)
MESSAGE_SHAPE = jax.ShapeDtypeStruct((CELLS + 4 * NBLK, EMB), jnp.bfloat16)
MASSES = pltpu.VMEM((3, CELLS), jnp.float32)


def target_message(*args):
    scratch = [MASSES, pltpu.SemaphoreType.DMA((2,))]
    return call(pack_kernel, MESSAGE_SHAPE, VMEM, [SMEM, HBM, HBM], scratch)(*args)


def near_products(place, slots, *args):
    outs = (G_SHAPE, COLUMN_SHAPE, NEAR_SHAPE, FATE_SHAPE, TABLE_SHAPE)
    in_specs = [SMEM] * (1 + len(slots)) + [HBM, HBM, VMEM, VMEM]
    scratch = [MASSES, pltpu.SemaphoreType.DMA((2,))]
    return call(near_kernel, outs, (VMEM,) * 4 + (SMEM,), in_specs, scratch)(place, *slots, *args)


def far_products(*args):
    outs = (G_SHAPE, WINDOW_SHAPE, PART_SHAPE)
    return call(far_kernel, outs, (VMEM,) * 3, [SMEM] + [VMEM] * 5, SWEEP_SCRATCH, {3: 0})(*args)


def sweep(*args):
    return call(sweep_kernel, PART_SHAPE, VMEM, [SMEM] + [VMEM] * 3, SWEEP_SCRATCH)(*args)


def other_products(*args):
    return call(other_kernel, G_SHAPE, VMEM, [ANY] + [VMEM] * 4)(*args)


def other_inputs(place, behind, slots, *args):
    outs = (TABLE_SHAPE, FATE_SHAPE, FATE_SHAPE)
    in_specs = [SMEM, ANY] + [SMEM] * len(slots) + [HBM]
    scratch = [pltpu.SemaphoreType.DMA((2,))]
    return call(rest_kernel, outs, (SMEM, VMEM, VMEM), in_specs, scratch)(place, behind, *slots, *args)


COUPLINGS = [SMEM, SMEM, VMEM, VMEM, SMEM, VMEM, VMEM]


def late_fates(*args):
    return call(late_kernel, FATE_SHAPE, VMEM, COUPLINGS + [VMEM] * 3, HOLD + [TERMS, COLUMN], mib=9)(*args)


def early_weights(*args):
    return call(early_weights_kernel, (W_SHAPE, COLUMN_SHAPE), (VMEM, VMEM), COUPLINGS, [TERMS, COLUMN])(*args)


def early_near(*args):
    return call(early_near_kernel, TOTAL_SHAPE, VMEM, [VMEM] * 3)(*args)


def early_fates(*args):
    return call(early_kernel, FATE_SHAPE, VMEM, [VMEM] * 4)(*args)


def merged(first, second):
    highest = jnp.maximum(first[0], second[0])
    return jnp.stack(
        [
            highest,
            first[1] * jnp.exp2(first[0] - highest) + second[1] * jnp.exp2(second[0] - highest),
        ]
    )


def folded(part, beside):
    own = merged(part[:, :NBLK], sibling(part[:, NBLK : 2 * NBLK]))
    beyond = part[:, 2 * NBLK :]
    message = jnp.concatenate([own, beyond], axis=1)
    arrived, made = lax.optimization_barrier((outward(message), beside(message)))
    own = merged(own, arrived[:, NBLK:])
    out = merged(arrived[:, :NBLK], beyond)
    own_total = own[0] + jnp.log2(own[1])
    out_total = out[0] + jnp.log2(out[1])
    return jnp.concatenate([own_total, sibling(own_total), out_total], axis=0), made


def shifted(value, steps):
    count = lax.axis_size("tiles")
    return lax.ppermute(value, "tiles", [(t, (t + steps) % count) for t in range(count)])


def on_device(embeddings, log_mass, signatures, tile_list):
    owner = lax.axis_index("cells").astype(jnp.int32)
    group = (lax.axis_index("tiles") >= 2).astype(jnp.int32)
    place = jnp.stack([owner, group])

    cells, masses = (
        pltpu.with_memory_space_constraint(array, pltpu.HBM) for array in (embeddings, log_mass)
    )
    target = target_message(place, cells, masses)
    target_out, target_sib = outward(target), sibling(target)
    slots, target_sib = lax.optimization_barrier((tile_list, target_sib))
    gathered = [slots] + [shifted(slots, k) for k in range(1, lax.axis_size("tiles"))]
    g, kc, near, source, table = near_products(place, gathered, cells, masses, target, target_sib)
    g, window, part = far_products(table, source, target_out, g, near, kc)

    totals, (table_other, other_source, other) = folded(
        part, lambda message: other_inputs(place, message, gathered, cells)
    )
    other_out, other_sib = outward(other), sibling(other)
    fates, other = lax.optimization_barrier((signatures, other))
    fates_out, fates_sib = outward(fates), sibling(fates)
    hh = window[1] - LAM * totals
    part = sweep(table, hh, kc, g)
    totals, g_other = folded(
        part, lambda message: other_products(message, other_source, other, other_sib, other_out)
    )
    hh = window[1] - LAM * totals
    couplings = (place, table, hh, g, table_other, mirrored(hh), g_other)
    late = late_fates(*couplings, signatures, fates_sib, fates_out)
    late_out, late_sib = outward(late), sibling(late)
    weights, sums = early_weights(*couplings)
    total = early_near(weights, late, late_sib)
    early = early_fates(weights, sums, total, late_out)
    return early, late


def solution(mesh):
    in_specs = (
        P(None, "cells", None),
        P(None, "cells"),
        P("cells", None),
        P(None, None, ("cells", "tiles")),
    )
    out_specs = (P("cells", None), P("cells", None))
    return jax.shard_map(
        on_device, mesh=mesh, in_specs=in_specs, out_specs=out_specs, check_vma=False
    )
```

```python
import jax
import jax.numpy as jnp
from jax import lax
from jax.experimental import pallas as pl
from jax.experimental.pallas import tpu as pltpu
from jax.sharding import PartitionSpec as P

EMB = 256
BLOCK = 128
NBLK = 8
WIN = 3 * NBLK
CELLS = NBLK * BLOCK
EPS = 0.01
RHO = 1.0
LAM = RHO / (RHO + EPS)
BIG = 1e30

LOG2E = 1.4426950408889634
SCALE = LOG2E / (EMB * EPS)

QUAD = 4
STRIDE = 32
GROUPS = NBLK * STRIDE
UNREAD = GROUPS + NBLK
TABLE = 384

FLOPS, BYTES, MIB = 3 * 10**9, 10**4, 4
VMEM = pl.BlockSpec(memory_space=pltpu.VMEM)
SMEM = pl.BlockSpec(memory_space=pltpu.SMEM)
ANY = pl.BlockSpec(memory_space=pl.ANY)
HBM = pl.BlockSpec(memory_space=pltpu.HBM)


def sibling(value):
    return lax.ppermute(value, "cells", [(c, c ^ 1) for c in range(lax.axis_size("cells"))])


def outward(value):
    count = lax.axis_size("cells")
    pairs = [(c, (c + 1 if c % 2 else c - 1) % count) for c in range(count)]
    return lax.ppermute(value, "cells", pairs)


def mirrored(value):
    count = lax.axis_size("tiles")
    return lax.ppermute(value, "tiles", [(t, count - 1 - t) for t in range(count)])


def call(kernel, outs, out_specs, in_specs, scratch=(), aliases=None, flops=FLOPS, mib=MIB):
    return pl.pallas_call(
        kernel,
        out_shape=outs,
        in_specs=in_specs,
        out_specs=out_specs,
        scratch_shapes=list(scratch),
        input_output_aliases=aliases or {},
        compiler_params=pltpu.CompilerParams(vmem_limit_bytes=mib << 20),
        cost_estimate=pl.CostEstimate(flops=flops, bytes_accessed=BYTES, transcendentals=0),
    )


def build_table(place_ref, coupling, slot_refs, table_ref):
    owner = place_ref[0]
    unroll = 4

    def step(index, counts):
        low, high = counts
        for inner in range(unroll):
            for slot_ref in slot_refs:
                source = slot_ref[coupling, 0, index * unroll + inner]
                target = slot_ref[coupling, 1, index * unroll + inner]
                away = target >> 3
                region = jnp.where(away == owner, 0, jnp.where(away == (owner ^ 1), NBLK, 2 * NBLK))
                empty = source < 0
                s = source & 7
                shift = (s & 3) << 3
                lower = s < 4
                count = (jnp.where(lower, low, high) >> shift) & 255
                table_ref[jnp.where(empty, UNREAD, s * STRIDE + count)] = region + (target & 7)
                one = jnp.where(empty, 0, 1 << shift)
                low, high = low + jnp.where(lower, one, 0), high + jnp.where(lower, 0, one)
        return low, high

    zero = jnp.int32(0)
    counts = lax.fori_loop(0, slot_refs[0].shape[2] // unroll, step, (zero, zero))
    for s in range(NBLK):
        count = (counts[s // 4] >> (8 * (s % 4))) & 255
        for extra in range(QUAD - 1):
            table_ref[s * STRIDE + count + extra] = WIN
        table_ref[GROUPS + s] = (count + QUAD - 1) >> 2


def products(source_ref, target_refs, g_ref, first):
    for region, target_ref in enumerate(target_refs, first):

        @pl.loop(0, NBLK // 2)
        def _(pair):
            rows = target_ref[pl.ds(pl.multiple_of(pair * 256, 256), 256), :]
            g = lax.dot_general(
                source_ref[...], rows, (((1,), (1,)), ((), ())), preferred_element_type=jnp.float32
            ) * (2.0 * SCALE)
            g_ref[region * NBLK + 2 * pair] = g[:, :BLOCK]
            g_ref[region * NBLK + 2 * pair + 1] = g[:, BLOCK:]


def block_masses(mass_ref, group, first):
    rows = []
    for block in range(NBLK):
        lanes = slice(block * BLOCK, (block + 1) * BLOCK)
        low, high = mass_ref[first : first + 1, lanes], mass_ref[first + 1 : first + 2, lanes]
        rows.append(jnp.where(group == 0, low, high))
    return jnp.concatenate(rows, axis=0)


def pack_kernel(place_ref, cells_hbm, mass_hbm, message_ref, mass_ref, sems):
    group = place_ref[1]
    cells = pltpu.make_async_copy(cells_hbm.at[group + 1], message_ref.at[:CELLS], sems.at[0])
    fetched = pltpu.make_async_copy(mass_hbm, mass_ref, sems.at[1])
    cells.start()
    fetched.start()
    fetched.wait()
    masses = block_masses(mass_ref, group, 1) * LOG2E
    cells.wait()
    ones = jnp.ones((8, EMB), jnp.bfloat16)
    norms = []
    for pair in range(NBLK // 2):
        y = message_ref[pair * 256 : (pair + 1) * 256, :].astype(jnp.float32)
        square = y * y
        high = square.astype(jnp.bfloat16)
        low = (square - high.astype(jnp.float32)).astype(jnp.bfloat16)
        norm = sum(
            lax.dot_general(ones, part, (((1,), (1,)), ((), ())), preferred_element_type=jnp.float32)
            for part in (high, low)
        )
        norms += [norm[:1, :BLOCK], norm[:1, BLOCK:]]
    norms = jnp.concatenate(norms, axis=0) * SCALE
    for half, left in enumerate((masses - norms, masses + (LAM - 1.0) * norms)):
        parts = []
        for _ in range(3):
            part = left.astype(jnp.bfloat16).astype(jnp.float32)
            parts.append(part)
            left = left - part
        parts.append(jnp.zeros_like(left))
        packed = jnp.concatenate(parts, axis=0).astype(jnp.bfloat16)
        message_ref[CELLS:, half * BLOCK : (half + 1) * BLOCK] = packed


def unpack(message_ref, window_ref, region):
    parts = message_ref[CELLS:, :].astype(jnp.float32)
    for half in range(2):
        p = parts[:, half * BLOCK : (half + 1) * BLOCK]
        total = (p[:NBLK] + p[NBLK : 2 * NBLK]) + p[2 * NBLK : 3 * NBLK]
        window_ref[half, region * NBLK : (region + 1) * NBLK, :] = total


STRIPS = BLOCK // 8


def extended(hh_ref, terms_ref):
    for t in range(WIN):
        terms_ref[t] = jnp.broadcast_to(hh_ref[t : t + 1, :], (8, BLOCK))
    terms_ref[WIN] = jnp.full((8, BLOCK), -BIG, jnp.float32)


def source_rows(s):
    return pl.ds(pl.multiple_of(s * BLOCK, BLOCK), BLOCK)


def group_targets(table_ref, s, q):
    return [table_ref[s * STRIDE + q * QUAD + k] for k in range(QUAD)]


def strips(g_ref, t, s):
    return g_ref[jnp.minimum(t, WIN - 1), source_rows(s), :].reshape(STRIPS, 8, BLOCK)


def row_maxima(table_ref, terms_ref, g_ref, m_ref):
    @pl.loop(0, NBLK)
    def _(s):
        def step(q, highest):
            v = [strips(g_ref, t, s) + terms_ref[t] for t in group_targets(table_ref, s, q)]
            return jnp.maximum(highest, jnp.maximum(jnp.maximum(v[0], v[1]), jnp.maximum(v[2], v[3])))

        start = jnp.full((STRIPS, 8, BLOCK), -BIG, jnp.float32)
        highest = lax.fori_loop(0, table_ref[GROUPS + s], step, start)
        m_ref[source_rows(s), :] = highest.reshape(BLOCK, BLOCK)

    m_ref[...] = jnp.broadcast_to(jnp.max(m_ref[...], axis=1, keepdims=True), m_ref.shape)


def sweep_kernel(table_ref, hh_ref, kc_ref, g_ref, part_ref, terms_ref, top_ref, mass_ref, m_ref, acc_ref):
    extended(hh_ref, terms_ref)
    top_ref[...] = jnp.full(top_ref.shape, -BIG, jnp.float32)
    mass_ref[...] = jnp.zeros(mass_ref.shape, jnp.float32)
    row_maxima(table_ref, terms_ref, g_ref, m_ref)

    @pl.loop(0, NBLK)
    def _(s):
        m = m_ref[source_rows(s), :].reshape(STRIPS, 8, BLOCK)

        def step(q, acc):
            v = [
                jnp.exp2(strips(g_ref, t, s) + terms_ref[t] - m)
                for t in group_targets(table_ref, s, q)
            ]
            return acc + ((v[0] + v[1]) + (v[2] + v[3]))

        start = jnp.zeros((STRIPS, 8, BLOCK), jnp.float32)
        acc = lax.fori_loop(0, table_ref[GROUPS + s], step, start)
        acc_ref[source_rows(s), :] = acc.reshape(BLOCK, BLOCK)

    sums = jnp.broadcast_to(jnp.sum(acc_ref[...], axis=1, keepdims=True), acc_ref.shape)
    acc_ref[...] = kc_ref[...] - LAM * (m_ref[...] + LOG2E * jnp.log(sums))

    @pl.loop(0, NBLK)
    def _(s):
        uu = acc_ref[source_rows(s), :].reshape(STRIPS, 8, BLOCK)

        @pl.loop(0, table_ref[GROUPS + s])
        def _(q):
            ts = group_targets(table_ref, s, q)
            tops = [top_ref[t] for t in ts]
            masses = [mass_ref[t] for t in ts]
            made = []
            for t, top, mass in zip(ts, tops, masses):
                v = strips(g_ref, t, s) + uu
                high = jnp.maximum(top, jnp.max(v, axis=0))
                made.append((high, mass * jnp.exp2(top - high) + jnp.sum(jnp.exp2(v - high), axis=0)))
            for t, (high, mass) in zip(ts, made):
                top_ref[t] = high
                mass_ref[t] = mass

    top = top_ref[:WIN]
    high = jnp.max(top, axis=1, keepdims=True)
    part_ref[0] = high[:, 0, :]
    part_ref[1] = jnp.sum(mass_ref[:WIN] * jnp.exp2(top - high), axis=1)


def weigh(table_ref, hh_ref, g_ref, w_ref, sum_ref, terms_ref, m_ref):
    extended(hh_ref, terms_ref)
    row_maxima(table_ref, terms_ref, g_ref, m_ref)

    @pl.loop(0, NBLK)
    def _(s):
        rows = source_rows(s)
        m = m_ref[rows, :].reshape(STRIPS, 8, BLOCK)
        w_ref[rows, :] = jnp.zeros((BLOCK, (WIN + 1) * BLOCK), jnp.bfloat16)

        def step(q, acc):
            ts = group_targets(table_ref, s, q)
            v = [jnp.exp2(strips(g_ref, t, s) + terms_ref[t] - m) for t in ts]
            for t, e in zip(ts, v):
                lanes = pl.ds(pl.multiple_of(t * BLOCK, BLOCK), BLOCK)
                w_ref[rows, lanes] = e.reshape(BLOCK, BLOCK).astype(jnp.bfloat16)
            return acc + ((v[0] + v[1]) + (v[2] + v[3]))

        start = jnp.zeros((STRIPS, 8, BLOCK), jnp.float32)
        acc = lax.fori_loop(0, table_ref[GROUPS + s], step, start)
        sum_ref[rows, :] = acc.reshape(BLOCK, BLOCK)

    sum_ref[...] = jnp.broadcast_to(jnp.sum(sum_ref[...], axis=1, keepdims=True), sum_ref.shape)


def pulled(w_ref, rows, fate_refs, first):
    total = 0.0
    for region, fate_ref in enumerate(fate_refs, first):
        total += jnp.dot(
            w_ref[rows, region * CELLS : (region + 1) * CELLS],
            fate_ref[...],
            preferred_element_type=jnp.float32,
        )
    return total


def divided(total, sums):
    inverse = 1.0 / sums
    return (total * jnp.concatenate([inverse, inverse], axis=1)).astype(jnp.bfloat16)


def chunks(body):
    @pl.loop(0, 4)
    def _(chunk):
        body(pl.ds(pl.multiple_of(chunk * 256, 256), 256))


def near_kernel(place_ref, *refs):
    *slot_refs, cells_hbm, mass_hbm, own_ref, sib_ref = refs[: len(refs) - 7]
    g_ref, kc_ref, window_ref, source_ref, table_ref, mass_ref, sems = refs[len(refs) - 7 :]
    group = place_ref[1]
    copies = (
        pltpu.make_async_copy(cells_hbm.at[group], source_ref, sems.at[0]),
        pltpu.make_async_copy(mass_hbm, mass_ref, sems.at[1]),
    )
    for copy in copies:
        copy.start()
    unpack(own_ref, window_ref, 0)
    unpack(sib_ref, window_ref, 1)
    build_table(place_ref, place_ref[1], slot_refs, table_ref)
    copies[0].wait()
    products(source_ref, (own_ref, sib_ref), g_ref, 0)
    copies[1].wait()
    masses = block_masses(mass_ref, group, 0)
    for s in range(NBLK):
        x = source_ref[s * BLOCK : (s + 1) * BLOCK, :].astype(jnp.float32)
        norm = jnp.sum(x * x, axis=1, keepdims=True) * SCALE
        mass = jnp.broadcast_to(masses[s : s + 1, :], (BLOCK, BLOCK)).T
        kc_ref[s * BLOCK : (s + 1) * BLOCK, :] = mass * LOG2E + (LAM - 1.0) * norm


def far_kernel(table_ref, source_ref, out_ref, near_ref, near_window_ref, kc_ref, g_ref, window_ref, part_ref, *scratch):
    del near_ref
    window_ref[:, : 2 * NBLK, :] = near_window_ref[...]
    unpack(out_ref, window_ref, 2)
    products(source_ref, (out_ref,), g_ref, 2)
    sweep_kernel(table_ref, window_ref.at[0], kc_ref, g_ref, part_ref, *scratch)


def other_kernel(behind_ref, source_ref, own_ref, sib_ref, out_ref, g_ref):
    del behind_ref
    products(source_ref, (own_ref, sib_ref, out_ref), g_ref, 0)


def rest_kernel(place_ref, behind_ref, arrived_ref, *refs):
    del behind_ref, arrived_ref
    *slot_refs, cells_hbm, table_ref, source_ref, target_ref, sems = refs
    group = place_ref[1]
    copies = (
        pltpu.make_async_copy(cells_hbm.at[2 - group], target_ref, sems.at[0]),
        pltpu.make_async_copy(cells_hbm.at[1 - group], source_ref, sems.at[1]),
    )
    for copy in copies:
        copy.start()
    build_table(place_ref, 1 - group, slot_refs, table_ref)
    for copy in copies:
        copy.wait()


def weigh_one(coupling, place_ref, mine, others, *outs):
    @pl.when(place_ref[1] == coupling)
    def _():
        weigh(*mine, *outs)

    @pl.when(place_ref[1] != coupling)
    def _():
        weigh(*others, *outs)


def late_kernel(place_ref, table_ref, hh_ref, g_ref, table2_ref, hh2_ref, g2_ref, own_ref, sib_ref, out_ref, late_ref, w_ref, sum_ref, terms_ref, m_ref):
    weigh_one(1, place_ref, (table_ref, hh_ref, g_ref), (table2_ref, hh2_ref, g2_ref), w_ref, sum_ref, terms_ref, m_ref)
    fates = (own_ref, sib_ref, out_ref)

    @chunks
    def _(rows):
        late_ref[rows, :] = divided(pulled(w_ref, rows, fates, 0), sum_ref[rows, :])


def early_weights_kernel(place_ref, table_ref, hh_ref, g_ref, table2_ref, hh2_ref, g2_ref, w_ref, sum_ref, terms_ref, m_ref):
    weigh_one(0, place_ref, (table_ref, hh_ref, g_ref), (table2_ref, hh2_ref, g2_ref), w_ref, sum_ref, terms_ref, m_ref)


def early_near_kernel(w_ref, own_ref, sib_ref, total_ref):
    @chunks
    def _(rows):
        total_ref[rows, :] = pulled(w_ref, rows, (own_ref, sib_ref), 0)


def early_kernel(w_ref, sum_ref, total_ref, out_ref, early_ref):
    @chunks
    def _(rows):
        total = total_ref[rows, :] + pulled(w_ref, rows, (out_ref,), 2)
        early_ref[rows, :] = divided(total, sum_ref[rows, :])


G_SHAPE = pltpu.VMEM((WIN, CELLS, BLOCK), jnp.float32)
PART_SHAPE = jax.ShapeDtypeStruct((2, WIN, BLOCK), jnp.float32)
W_SHAPE = jax.ShapeDtypeStruct((CELLS, (WIN + 1) * BLOCK), jnp.bfloat16)
COLUMN_SHAPE = jax.ShapeDtypeStruct((CELLS, BLOCK), jnp.float32)
FATE_SHAPE = jax.ShapeDtypeStruct((CELLS, EMB), jnp.bfloat16)
TOTAL_SHAPE = jax.ShapeDtypeStruct((CELLS, EMB), jnp.float32)
TERMS = pltpu.VMEM((WIN + 1, 8, BLOCK), jnp.float32)
COLUMN = pltpu.VMEM(COLUMN_SHAPE.shape, COLUMN_SHAPE.dtype)
SWEEP_SCRATCH = [TERMS] * 3 + [COLUMN] * 2
HOLD = [pltpu.VMEM(W_SHAPE.shape, W_SHAPE.dtype), COLUMN]


WINDOW_SHAPE = jax.ShapeDtypeStruct((2, WIN, BLOCK), jnp.float32)
NEAR_SHAPE = jax.ShapeDtypeStruct((2, 2 * NBLK, BLOCK), jnp.float32)


TABLE_SHAPE = jax.ShapeDtypeStruct((TABLE,), jnp.int32)
MESSAGE_SHAPE = jax.ShapeDtypeStruct((CELLS + 4 * NBLK, EMB), jnp.bfloat16)
MASSES = pltpu.VMEM((3, CELLS), jnp.float32)


def target_message(*args):
    scratch = [MASSES, pltpu.SemaphoreType.DMA((2,))]
    return call(pack_kernel, MESSAGE_SHAPE, VMEM, [SMEM, HBM, HBM], scratch)(*args)


def near_products(place, slots, *args):
    outs = (G_SHAPE, COLUMN_SHAPE, NEAR_SHAPE, FATE_SHAPE, TABLE_SHAPE)
    in_specs = [SMEM] * (1 + len(slots)) + [HBM, HBM, VMEM, VMEM]
    scratch = [MASSES, pltpu.SemaphoreType.DMA((2,))]
    return call(near_kernel, outs, (VMEM,) * 4 + (SMEM,), in_specs, scratch)(place, *slots, *args)


def far_products(*args):
    outs = (G_SHAPE, WINDOW_SHAPE, PART_SHAPE)
    return call(far_kernel, outs, (VMEM,) * 3, [SMEM] + [VMEM] * 5, SWEEP_SCRATCH, {3: 0})(*args)


def sweep(*args):
    return call(sweep_kernel, PART_SHAPE, VMEM, [SMEM] + [VMEM] * 3, SWEEP_SCRATCH)(*args)


def other_products(*args):
    return call(other_kernel, G_SHAPE, VMEM, [ANY] + [VMEM] * 4)(*args)


def other_inputs(place, behind, arrived, slots, *args):
    outs = (TABLE_SHAPE, FATE_SHAPE, FATE_SHAPE)
    in_specs = [SMEM, ANY, ANY] + [SMEM] * len(slots) + [HBM]
    scratch = [pltpu.SemaphoreType.DMA((2,))]
    return call(rest_kernel, outs, (SMEM, VMEM, VMEM), in_specs, scratch)(place, behind, arrived, *slots, *args)


COUPLINGS = [SMEM, SMEM, VMEM, VMEM, SMEM, VMEM, VMEM]


def late_fates(*args):
    return call(late_kernel, FATE_SHAPE, VMEM, COUPLINGS + [VMEM] * 3, HOLD + [TERMS, COLUMN], mib=9)(*args)


def early_weights(*args):
    return call(early_weights_kernel, (W_SHAPE, COLUMN_SHAPE), (VMEM, VMEM), COUPLINGS, [TERMS, COLUMN])(*args)


def early_near(*args):
    return call(early_near_kernel, TOTAL_SHAPE, VMEM, [VMEM] * 3)(*args)


def early_fates(*args):
    return call(early_kernel, FATE_SHAPE, VMEM, [VMEM] * 4)(*args)


def merged(first, second):
    highest = jnp.maximum(first[0], second[0])
    return jnp.stack(
        [
            highest,
            first[1] * jnp.exp2(first[0] - highest) + second[1] * jnp.exp2(second[0] - highest),
        ]
    )


def folded(part, beside):
    own = merged(part[:, :NBLK], sibling(part[:, NBLK : 2 * NBLK]))
    beyond = part[:, 2 * NBLK :]
    message = jnp.concatenate([own, beyond], axis=1)
    arrived, made = lax.optimization_barrier((outward(message), beside(message)))
    own = merged(own, arrived[:, NBLK:])
    out = merged(arrived[:, :NBLK], beyond)
    own_total = own[0] + jnp.log2(own[1])
    out_total = out[0] + jnp.log2(out[1])
    return jnp.concatenate([own_total, sibling(own_total), out_total], axis=0), made


def shifted(value, steps):
    count = lax.axis_size("tiles")
    return lax.ppermute(value, "tiles", [(t, (t + steps) % count) for t in range(count)])


def on_device(embeddings, log_mass, signatures, tile_list):
    owner = lax.axis_index("cells").astype(jnp.int32)
    group = (lax.axis_index("tiles") >= 2).astype(jnp.int32)
    place = jnp.stack([owner, group])

    cells, masses = (
        pltpu.with_memory_space_constraint(array, pltpu.HBM) for array in (embeddings, log_mass)
    )
    target = target_message(place, cells, masses)
    target_out, target_sib = outward(target), sibling(target)
    slots, fates, target_sib = lax.optimization_barrier((tile_list, signatures, target_sib))
    fates_out, fates_sib = outward(fates), sibling(fates)
    gathered = [pltpu.with_memory_space_constraint(tile_list, pltpu.HBM)] + [shifted(slots, k) for k in range(1, lax.axis_size("tiles"))]
    g, kc, near, source, table = near_products(place, gathered, cells, masses, target, target_sib)
    g, window, part = far_products(table, source, target_out, g, near, kc)

    totals, (table_other, other_source, other) = folded(
        part, lambda message: other_inputs(place, message, fates_out, gathered, cells)
    )
    other_out, other_sib = outward(other), sibling(other)
    hh = window[1] - LAM * totals
    part = sweep(table, hh, kc, g)
    totals, g_other = folded(
        part, lambda message: other_products(message, other_source, other, other_sib, other_out)
    )
    hh = window[1] - LAM * totals
    couplings = (place, table, hh, g, table_other, mirrored(hh), g_other)
    late = late_fates(*couplings, signatures, fates_sib, fates_out)
    late_out, late_sib = outward(late), sibling(late)
    weights, sums = early_weights(*couplings)
    total = early_near(weights, late, late_sib)
    early = early_fates(weights, sums, total, late_out)
    return early, late


def solution(mesh):
    in_specs = (
        P(None, "cells", None),
        P(None, "cells"),
        P("cells", None),
        P(None, None, ("cells", "tiles")),
    )
    out_specs = (P("cells", None), P("cells", None))
    return jax.shard_map(
        on_device, mesh=mesh, in_specs=in_specs, out_specs=out_specs, check_vma=False
    )
```

```python
import jax
import jax.numpy as jnp
from jax import lax
from jax.experimental import pallas as pl
from jax.experimental.pallas import tpu as pltpu
from jax.sharding import PartitionSpec as P

EMB = 256
BLOCK = 128
NBLK = 8
WIN = 3 * NBLK
CELLS = NBLK * BLOCK
EPS = 0.01
RHO = 1.0
LAM = RHO / (RHO + EPS)
BIG = 1e30

LOG2E = 1.4426950408889634
SCALE = LOG2E / (EMB * EPS)

QUAD = 4
STRIDE = 32
GROUPS = NBLK * STRIDE
UNREAD = GROUPS + NBLK
TABLE = 384

FLOPS, BYTES, MIB = 3 * 10**9, 10**4, 4
VMEM = pl.BlockSpec(memory_space=pltpu.VMEM)
SMEM = pl.BlockSpec(memory_space=pltpu.SMEM)
ANY = pl.BlockSpec(memory_space=pl.ANY)
HBM = pl.BlockSpec(memory_space=pltpu.HBM)


def sibling(value):
    return lax.ppermute(value, "cells", [(c, c ^ 1) for c in range(lax.axis_size("cells"))])


def outward(value):
    count = lax.axis_size("cells")
    pairs = [(c, (c + 1 if c % 2 else c - 1) % count) for c in range(count)]
    return lax.ppermute(value, "cells", pairs)


def mirrored(value):
    count = lax.axis_size("tiles")
    return lax.ppermute(value, "tiles", [(t, count - 1 - t) for t in range(count)])


def call(kernel, outs, out_specs, in_specs, scratch=(), aliases=None, flops=FLOPS, mib=MIB):
    return pl.pallas_call(
        kernel,
        out_shape=outs,
        in_specs=in_specs,
        out_specs=out_specs,
        scratch_shapes=list(scratch),
        input_output_aliases=aliases or {},
        compiler_params=pltpu.CompilerParams(vmem_limit_bytes=mib << 20),
        cost_estimate=pl.CostEstimate(flops=flops, bytes_accessed=BYTES, transcendentals=0),
    )


def enter_slots(place_ref, coupling, slot_refs, table_ref, quarter, counts):
    low, high = counts
    owner = place_ref[0]
    share = slot_refs[0].shape[2] // 4
    for index in range(share):
        for slot_ref in slot_refs:
            source = slot_ref[coupling, 0, quarter * share + index]
            target = slot_ref[coupling, 1, quarter * share + index]
            away = target >> 3
            region = jnp.where(away == owner, 0, jnp.where(away == (owner ^ 1), NBLK, 2 * NBLK))
            empty = source < 0
            s = source & 7
            shift = (s & 3) << 3
            lower = s < 4
            count = (jnp.where(lower, low, high) >> shift) & 255
            table_ref[jnp.where(empty, UNREAD, s * STRIDE + count)] = region + (target & 7)
            one = jnp.where(empty, 0, 1 << shift)
            low, high = low + jnp.where(lower, one, 0), high + jnp.where(lower, 0, one)
    return low, high


def close_table(table_ref, counts):
    for s in range(NBLK):
        count = (counts[s // 4] >> (8 * (s % 4))) & 255
        for extra in range(QUAD - 1):
            table_ref[s * STRIDE + count + extra] = WIN
        table_ref[GROUPS + s] = (count + QUAD - 1) >> 2


def product_pair(source_ref, target_ref, g_ref, region, pair):
    rows = target_ref[pl.ds(pl.multiple_of(pair * 256, 256), 256), :]
    g = lax.dot_general(
        source_ref[...], rows, (((1,), (1,)), ((), ())), preferred_element_type=jnp.float32
    ) * (2.0 * SCALE)
    g_ref[region * NBLK + 2 * pair] = g[:, :BLOCK]
    g_ref[region * NBLK + 2 * pair + 1] = g[:, BLOCK:]


def products(source_ref, target_refs, g_ref, first):
    for region, target_ref in enumerate(target_refs, first):

        @pl.loop(0, NBLK // 2)
        def _(pair):
            product_pair(source_ref, target_ref, g_ref, region, pair)


def block_masses(mass_ref, group, first):
    rows = []
    for block in range(NBLK):
        lanes = slice(block * BLOCK, (block + 1) * BLOCK)
        low, high = mass_ref[first : first + 1, lanes], mass_ref[first + 1 : first + 2, lanes]
        rows.append(jnp.where(group == 0, low, high))
    return jnp.concatenate(rows, axis=0)


def pack_kernel(place_ref, cells_hbm, mass_hbm, message_ref, mass_ref, sems):
    group = place_ref[1]
    cells = pltpu.make_async_copy(cells_hbm.at[group + 1], message_ref.at[:CELLS], sems.at[0])
    fetched = pltpu.make_async_copy(mass_hbm, mass_ref, sems.at[1])
    cells.start()
    fetched.start()
    fetched.wait()
    masses = block_masses(mass_ref, group, 1) * LOG2E
    cells.wait()
    ones = jnp.ones((8, EMB), jnp.bfloat16)
    norms = []
    for pair in range(NBLK // 2):
        y = message_ref[pair * 256 : (pair + 1) * 256, :].astype(jnp.float32)
        square = y * y
        high = square.astype(jnp.bfloat16)
        low = (square - high.astype(jnp.float32)).astype(jnp.bfloat16)
        norm = sum(
            lax.dot_general(ones, part, (((1,), (1,)), ((), ())), preferred_element_type=jnp.float32)
            for part in (high, low)
        )
        norms += [norm[:1, :BLOCK], norm[:1, BLOCK:]]
    norms = jnp.concatenate(norms, axis=0) * SCALE
    for half, left in enumerate((masses - norms, masses + (LAM - 1.0) * norms)):
        parts = []
        for _ in range(3):
            part = left.astype(jnp.bfloat16).astype(jnp.float32)
            parts.append(part)
            left = left - part
        parts.append(jnp.zeros_like(left))
        packed = jnp.concatenate(parts, axis=0).astype(jnp.bfloat16)
        message_ref[CELLS:, half * BLOCK : (half + 1) * BLOCK] = packed


def unpack(message_ref, window_ref, region):
    parts = message_ref[CELLS:, :].astype(jnp.float32)
    for half in range(2):
        p = parts[:, half * BLOCK : (half + 1) * BLOCK]
        total = (p[:NBLK] + p[NBLK : 2 * NBLK]) + p[2 * NBLK : 3 * NBLK]
        window_ref[half, region * NBLK : (region + 1) * NBLK, :] = total


STRIPS = BLOCK // 8


def extended(hh_ref, terms_ref):
    for t in range(WIN):
        terms_ref[t] = jnp.broadcast_to(hh_ref[t : t + 1, :], (8, BLOCK))
    terms_ref[WIN] = jnp.full((8, BLOCK), -BIG, jnp.float32)


def source_rows(s):
    return pl.ds(pl.multiple_of(s * BLOCK, BLOCK), BLOCK)


def group_targets(table_ref, s, q):
    return [table_ref[s * STRIDE + q * QUAD + k] for k in range(QUAD)]


def strips(g_ref, t, s):
    return g_ref[jnp.minimum(t, WIN - 1), source_rows(s), :].reshape(STRIPS, 8, BLOCK)


def row_maxima(table_ref, terms_ref, g_ref, m_ref):
    @pl.loop(0, NBLK)
    def _(s):
        def step(q, highest):
            v = [strips(g_ref, t, s) + terms_ref[t] for t in group_targets(table_ref, s, q)]
            return jnp.maximum(highest, jnp.maximum(jnp.maximum(v[0], v[1]), jnp.maximum(v[2], v[3])))

        start = jnp.full((STRIPS, 8, BLOCK), -BIG, jnp.float32)
        highest = lax.fori_loop(0, table_ref[GROUPS + s], step, start)
        m_ref[source_rows(s), :] = highest.reshape(BLOCK, BLOCK)

    m_ref[...] = jnp.broadcast_to(jnp.max(m_ref[...], axis=1, keepdims=True), m_ref.shape)


def sweep_kernel(table_ref, hh_ref, kc_ref, g_ref, part_ref, terms_ref, top_ref, mass_ref, m_ref, acc_ref):
    extended(hh_ref, terms_ref)
    top_ref[...] = jnp.full(top_ref.shape, -BIG, jnp.float32)
    mass_ref[...] = jnp.zeros(mass_ref.shape, jnp.float32)

    @pl.loop(0, NBLK)
    def _(s):
        def step(q, carried):
            top, acc = carried
            v = [strips(g_ref, t, s) + terms_ref[t] for t in group_targets(table_ref, s, q)]
            high = jnp.maximum(jnp.maximum(v[0], v[1]), jnp.maximum(v[2], v[3]))
            high = jnp.maximum(top, high)
            e = [jnp.exp2(part - high) for part in v]
            return high, acc * jnp.exp2(top - high) + ((e[0] + e[1]) + (e[2] + e[3]))

        shape = (STRIPS, 8, BLOCK)
        start = jnp.full(shape, -BIG, jnp.float32), jnp.zeros(shape, jnp.float32)
        top, acc = lax.fori_loop(0, table_ref[GROUPS + s], step, start)
        m_ref[source_rows(s), :] = top.reshape(BLOCK, BLOCK)
        acc_ref[source_rows(s), :] = acc.reshape(BLOCK, BLOCK)

    tops = m_ref[...]
    high = jnp.max(tops, axis=1, keepdims=True)
    sums = jnp.sum(acc_ref[...] * jnp.exp2(tops - high), axis=1, keepdims=True)
    acc_ref[...] = kc_ref[...] - LAM * (high + LOG2E * jnp.log(sums))

    @pl.loop(0, NBLK)
    def _(s):
        uu = acc_ref[source_rows(s), :].reshape(STRIPS, 8, BLOCK)
        groups = table_ref[GROUPS + s]

        def columns(ts):
            tops = [top_ref[t] for t in ts]
            masses = [mass_ref[t] for t in ts]
            made = []
            for t, top, mass in zip(ts, tops, masses):
                v = strips(g_ref, t, s) + uu
                high = jnp.maximum(top, jnp.max(v, axis=0))
                made.append((high, mass * jnp.exp2(top - high) + jnp.sum(jnp.exp2(v - high), axis=0)))
            for t, (high, mass) in zip(ts, made):
                top_ref[t] = high
                mass_ref[t] = mass

        @pl.loop(0, groups // 2)
        def _(double):
            columns(group_targets(table_ref, s, 2 * double) + group_targets(table_ref, s, 2 * double + 1))

        @pl.when(groups % 2 == 1)
        def _():
            columns(group_targets(table_ref, s, groups - 1))

    top = top_ref[:WIN]
    high = jnp.max(top, axis=1, keepdims=True)
    part_ref[0] = high[:, 0, :]
    part_ref[1] = jnp.sum(mass_ref[:WIN] * jnp.exp2(top - high), axis=1)


def weigh(table_ref, hh_ref, g_ref, w_ref, sum_ref, terms_ref, m_ref):
    extended(hh_ref, terms_ref)
    row_maxima(table_ref, terms_ref, g_ref, m_ref)

    @pl.loop(0, NBLK)
    def _(s):
        rows = source_rows(s)
        m = m_ref[rows, :].reshape(STRIPS, 8, BLOCK)

        def step(q, acc):
            ts = group_targets(table_ref, s, q)
            v = [jnp.exp2(strips(g_ref, t, s) + terms_ref[t] - m) for t in ts]
            for t, e in zip(ts, v):
                lanes = pl.ds(pl.multiple_of(t * BLOCK, BLOCK), BLOCK)
                w_ref[rows, lanes] = e.reshape(BLOCK, BLOCK).astype(jnp.bfloat16)
            return acc + ((v[0] + v[1]) + (v[2] + v[3]))

        start = jnp.zeros((STRIPS, 8, BLOCK), jnp.float32)
        acc = lax.fori_loop(0, table_ref[GROUPS + s], step, start)
        sum_ref[rows, :] = acc.reshape(BLOCK, BLOCK)

    sum_ref[...] = jnp.broadcast_to(jnp.sum(sum_ref[...], axis=1, keepdims=True), sum_ref.shape)


def pulled(w_ref, rows, fate_refs, first):
    total = 0.0
    for region, fate_ref in enumerate(fate_refs, first):
        total += jnp.dot(
            w_ref[rows, region * CELLS : (region + 1) * CELLS],
            fate_ref[...],
            preferred_element_type=jnp.float32,
        )
    return total


def divided(total, sums):
    inverse = 1.0 / sums
    return (total * jnp.concatenate([inverse, inverse], axis=1)).astype(jnp.bfloat16)


def chunks(body):
    @pl.loop(0, 4)
    def _(chunk):
        body(pl.ds(pl.multiple_of(chunk * 256, 256), 256))


def near_kernel(place_ref, *refs):
    *slot_refs, cells_hbm, mass_hbm, own_ref, sib_ref = refs[: len(refs) - 7]
    g_ref, kc_ref, window_ref, source_ref, table_ref, mass_ref, sems = refs[len(refs) - 7 :]
    group = place_ref[1]
    copies = (
        pltpu.make_async_copy(cells_hbm.at[group], source_ref, sems.at[0]),
        pltpu.make_async_copy(mass_hbm, mass_ref, sems.at[1]),
    )
    for copy in copies:
        copy.start()
    unpack(own_ref, window_ref, 0)
    unpack(sib_ref, window_ref, 1)
    copies[0].wait()

    def step(pair, counts):
        product_pair(source_ref, own_ref, g_ref, 0, pair)
        return enter_slots(place_ref, group, slot_refs, table_ref, pair, counts)

    zero = jnp.int32(0)
    close_table(table_ref, lax.fori_loop(0, NBLK // 2, step, (zero, zero)))
    products(source_ref, (sib_ref,), g_ref, 1)
    copies[1].wait()
    masses = block_masses(mass_ref, group, 0)
    for s in range(NBLK):
        x = source_ref[s * BLOCK : (s + 1) * BLOCK, :].astype(jnp.float32)
        norm = jnp.sum(x * x, axis=1, keepdims=True) * SCALE
        mass = jnp.broadcast_to(masses[s : s + 1, :], (BLOCK, BLOCK)).T
        kc_ref[s * BLOCK : (s + 1) * BLOCK, :] = mass * LOG2E + (LAM - 1.0) * norm


def far_kernel(table_ref, source_ref, out_ref, near_ref, near_window_ref, kc_ref, g_ref, window_ref, part_ref, *scratch):
    del near_ref
    window_ref[:, : 2 * NBLK, :] = near_window_ref[...]
    unpack(out_ref, window_ref, 2)
    products(source_ref, (out_ref,), g_ref, 2)
    sweep_kernel(table_ref, window_ref.at[0], kc_ref, g_ref, part_ref, *scratch)


def other_kernel(behind_ref, source_ref, own_ref, sib_ref, out_ref, g_ref):
    del behind_ref
    products(source_ref, (own_ref, sib_ref, out_ref), g_ref, 0)


def rest_kernel(place_ref, behind_ref, arrived_ref, *refs):
    del behind_ref, arrived_ref
    *slot_refs, cells_hbm, table_ref, source_ref, target_ref, sems = refs
    group = place_ref[1]
    copies = (
        pltpu.make_async_copy(cells_hbm.at[2 - group], target_ref, sems.at[0]),
        pltpu.make_async_copy(cells_hbm.at[1 - group], source_ref, sems.at[1]),
    )
    for copy in copies:
        copy.start()

    def step(quarter, counts):
        return enter_slots(place_ref, 1 - group, slot_refs, table_ref, quarter, counts)

    zero = jnp.int32(0)
    close_table(table_ref, lax.fori_loop(0, 4, step, (zero, zero)))
    for copy in copies:
        copy.wait()


def weigh_one(coupling, place_ref, mine, others, *outs):
    @pl.when(place_ref[1] == coupling)
    def _():
        weigh(*mine, *outs)

    @pl.when(place_ref[1] != coupling)
    def _():
        weigh(*others, *outs)


def blank_kernel(behind_ref, w_ref):
    del behind_ref

    @pl.loop(0, NBLK)
    def _(s):
        w_ref[source_rows(s), :] = jnp.zeros((BLOCK, (WIN + 1) * BLOCK), jnp.bfloat16)


def late_kernel(place_ref, table_ref, hh_ref, g_ref, table2_ref, hh2_ref, g2_ref, own_ref, sib_ref, out_ref, blank_ref, late_ref, w_ref, sum_ref, terms_ref, m_ref):
    del blank_ref
    weigh_one(1, place_ref, (table_ref, hh_ref, g_ref), (table2_ref, hh2_ref, g2_ref), w_ref, sum_ref, terms_ref, m_ref)
    fates = (own_ref, sib_ref, out_ref)

    @chunks
    def _(rows):
        late_ref[rows, :] = divided(pulled(w_ref, rows, fates, 0), sum_ref[rows, :])


def early_weights_kernel(place_ref, table_ref, hh_ref, g_ref, table2_ref, hh2_ref, g2_ref, w_ref, sum_ref, terms_ref, m_ref):
    blank_kernel(None, w_ref)
    weigh_one(0, place_ref, (table_ref, hh_ref, g_ref), (table2_ref, hh2_ref, g2_ref), w_ref, sum_ref, terms_ref, m_ref)


def early_near_kernel(w_ref, own_ref, sib_ref, total_ref):
    @chunks
    def _(rows):
        total_ref[rows, :] = pulled(w_ref, rows, (own_ref, sib_ref), 0)


def early_kernel(w_ref, sum_ref, total_ref, out_ref, early_ref):
    @chunks
    def _(rows):
        total = total_ref[rows, :] + pulled(w_ref, rows, (out_ref,), 2)
        early_ref[rows, :] = divided(total, sum_ref[rows, :])


G_SHAPE = pltpu.VMEM((WIN, CELLS, BLOCK), jnp.float32)
PART_SHAPE = jax.ShapeDtypeStruct((2, WIN, BLOCK), jnp.float32)
W_SHAPE = jax.ShapeDtypeStruct((CELLS, (WIN + 1) * BLOCK), jnp.bfloat16)
COLUMN_SHAPE = jax.ShapeDtypeStruct((CELLS, BLOCK), jnp.float32)
FATE_SHAPE = jax.ShapeDtypeStruct((CELLS, EMB), jnp.bfloat16)
TOTAL_SHAPE = jax.ShapeDtypeStruct((CELLS, EMB), jnp.float32)
TERMS = pltpu.VMEM((WIN + 1, 8, BLOCK), jnp.float32)
COLUMN = pltpu.VMEM(COLUMN_SHAPE.shape, COLUMN_SHAPE.dtype)
SWEEP_SCRATCH = [TERMS] * 3 + [COLUMN] * 2


WINDOW_SHAPE = jax.ShapeDtypeStruct((2, WIN, BLOCK), jnp.float32)
NEAR_SHAPE = jax.ShapeDtypeStruct((2, 2 * NBLK, BLOCK), jnp.float32)


TABLE_SHAPE = jax.ShapeDtypeStruct((TABLE,), jnp.int32)
MESSAGE_SHAPE = jax.ShapeDtypeStruct((CELLS + 4 * NBLK, EMB), jnp.bfloat16)
MASSES = pltpu.VMEM((3, CELLS), jnp.float32)


def target_message(*args):
    scratch = [MASSES, pltpu.SemaphoreType.DMA((2,))]
    return call(pack_kernel, MESSAGE_SHAPE, VMEM, [SMEM, HBM, HBM], scratch)(*args)


def near_products(place, slots, *args):
    outs = (G_SHAPE, COLUMN_SHAPE, NEAR_SHAPE, FATE_SHAPE, TABLE_SHAPE)
    in_specs = [SMEM] * (1 + len(slots)) + [HBM, HBM, VMEM, VMEM]
    scratch = [MASSES, pltpu.SemaphoreType.DMA((2,))]
    return call(near_kernel, outs, (VMEM,) * 4 + (SMEM,), in_specs, scratch)(place, *slots, *args)


def far_products(*args):
    outs = (G_SHAPE, WINDOW_SHAPE, PART_SHAPE)
    return call(far_kernel, outs, (VMEM,) * 3, [SMEM] + [VMEM] * 5, SWEEP_SCRATCH, {3: 0})(*args)


def sweep(*args):
    return call(sweep_kernel, PART_SHAPE, VMEM, [SMEM] + [VMEM] * 3, SWEEP_SCRATCH)(*args)


def other_products(*args):
    return call(other_kernel, G_SHAPE, VMEM, [ANY] + [VMEM] * 4)(*args)


def other_inputs(place, behind, arrived, slots, *args):
    outs = (TABLE_SHAPE, FATE_SHAPE, FATE_SHAPE)
    in_specs = [SMEM, ANY, ANY] + [SMEM] * len(slots) + [HBM]
    scratch = [pltpu.SemaphoreType.DMA((2,))]
    return call(rest_kernel, outs, (SMEM, VMEM, VMEM), in_specs, scratch)(place, behind, arrived, *slots, *args)


COUPLINGS = [SMEM, SMEM, VMEM, VMEM, SMEM, VMEM, VMEM]


def blank_weights(behind):
    return call(blank_kernel, W_SHAPE, VMEM, [ANY])(behind)


def late_fates(*args):
    outs, in_specs = (FATE_SHAPE, W_SHAPE), COUPLINGS + [VMEM] * 4
    return call(late_kernel, outs, (VMEM, VMEM), in_specs, [COLUMN, TERMS, COLUMN], {10: 1})(*args)[0]


def early_weights(*args):
    return call(early_weights_kernel, (W_SHAPE, COLUMN_SHAPE), (VMEM, VMEM), COUPLINGS, [TERMS, COLUMN])(*args)


def early_near(*args):
    return call(early_near_kernel, TOTAL_SHAPE, VMEM, [VMEM] * 3)(*args)


def early_fates(*args):
    return call(early_kernel, FATE_SHAPE, VMEM, [VMEM] * 4)(*args)


def merged(first, second):
    highest = jnp.maximum(first[0], second[0])
    return jnp.stack(
        [
            highest,
            first[1] * jnp.exp2(first[0] - highest) + second[1] * jnp.exp2(second[0] - highest),
        ]
    )


def folded(part, beside):
    own = merged(part[:, :NBLK], sibling(part[:, NBLK : 2 * NBLK]))
    beyond = part[:, 2 * NBLK :]
    message = jnp.concatenate([own, beyond], axis=1)
    arrived, made = lax.optimization_barrier((outward(message), beside(message)))
    own = merged(own, arrived[:, NBLK:])
    out = merged(arrived[:, :NBLK], beyond)
    own_total = own[0] + jnp.log2(own[1])
    out_total = out[0] + jnp.log2(out[1])
    return jnp.concatenate([own_total, sibling(own_total), out_total], axis=0), made


def shifted(value, steps):
    count = lax.axis_size("tiles")
    return lax.ppermute(value, "tiles", [(t, (t + steps) % count) for t in range(count)])


def on_device(embeddings, log_mass, signatures, tile_list):
    owner = lax.axis_index("cells").astype(jnp.int32)
    group = (lax.axis_index("tiles") >= 2).astype(jnp.int32)
    place = jnp.stack([owner, group])

    cells, masses = (
        pltpu.with_memory_space_constraint(array, pltpu.HBM) for array in (embeddings, log_mass)
    )
    target = target_message(place, cells, masses)
    target_out, target_sib = outward(target), sibling(target)
    slots, fates, target_sib = lax.optimization_barrier((tile_list, signatures, target_sib))
    fates_out, fates_sib = outward(fates), sibling(fates)
    gathered = [pltpu.with_memory_space_constraint(tile_list, pltpu.HBM)] + [shifted(slots, k) for k in range(1, lax.axis_size("tiles"))]
    g, kc, near, source, table = near_products(place, gathered, cells, masses, target, target_sib)
    g, window, part = far_products(table, source, target_out, g, near, kc)

    totals, (table_other, other_source, other) = folded(
        part, lambda message: other_inputs(place, message, fates_out, gathered, cells)
    )
    other_out, other_sib = outward(other), sibling(other)
    hh = window[1] - LAM * totals
    part = sweep(table, hh, kc, g)
    totals, g_other = folded(
        part, lambda message: other_products(message, other_source, other, other_sib, other_out)
    )
    hh = window[1] - LAM * totals
    couplings = (place, table, hh, g, table_other, mirrored(hh), g_other)
    late = late_fates(*couplings, signatures, fates_sib, fates_out, blank_weights(hh))
    late_out, late_sib = outward(late), sibling(late)
    weights, sums = early_weights(*couplings)
    total = early_near(weights, late, late_sib)
    early = early_fates(weights, sums, total, late_out)
    return early, late


def solution(mesh):
    in_specs = (
        P(None, "cells", None),
        P(None, "cells"),
        P("cells", None),
        P(None, None, ("cells", "tiles")),
    )
    out_specs = (P("cells", None), P("cells", None))
    return jax.shard_map(
        on_device, mesh=mesh, in_specs=in_specs, out_specs=out_specs, check_vma=False
    )
```

```python
import jax
import jax.numpy as jnp
from jax import lax
from jax.experimental import pallas as pl
from jax.experimental.pallas import tpu as pltpu
from jax.sharding import PartitionSpec as P

EMB = 256
BLOCK = 128
NBLK = 8
WIN = 3 * NBLK
CELLS = NBLK * BLOCK
EPS = 0.01
RHO = 1.0
LAM = RHO / (RHO + EPS)
BIG = 1e30

LOG2E = 1.4426950408889634
SCALE = LOG2E / (EMB * EPS)

QUAD = 4
STRIDE = 32
GROUPS = NBLK * STRIDE
UNREAD = GROUPS + NBLK
TABLE = 384

FLOPS, BYTES, MIB = 3 * 10**9, 10**4, 4
VMEM = pl.BlockSpec(memory_space=pltpu.VMEM)
SMEM = pl.BlockSpec(memory_space=pltpu.SMEM)
ANY = pl.BlockSpec(memory_space=pl.ANY)
HBM = pl.BlockSpec(memory_space=pltpu.HBM)


def sibling(value):
    return lax.ppermute(value, "cells", [(c, c ^ 1) for c in range(lax.axis_size("cells"))])


def outward(value):
    count = lax.axis_size("cells")
    pairs = [(c, (c + 1 if c % 2 else c - 1) % count) for c in range(count)]
    return lax.ppermute(value, "cells", pairs)


def mirrored(value):
    count = lax.axis_size("tiles")
    return lax.ppermute(value, "tiles", [(t, count - 1 - t) for t in range(count)])


def call(kernel, outs, out_specs, in_specs, scratch=(), aliases=None, flops=FLOPS, mib=MIB):
    return pl.pallas_call(
        kernel,
        out_shape=outs,
        in_specs=in_specs,
        out_specs=out_specs,
        scratch_shapes=list(scratch),
        input_output_aliases=aliases or {},
        compiler_params=pltpu.CompilerParams(vmem_limit_bytes=mib << 20),
        cost_estimate=pl.CostEstimate(flops=flops, bytes_accessed=BYTES, transcendentals=0),
    )


def enter_slots(place_ref, coupling, slot_refs, table_ref, quarter, counts):
    low, high = counts
    owner = place_ref[0]
    share = slot_refs[0].shape[2] // 4
    for index in range(share):
        for slot_ref in slot_refs:
            source = slot_ref[coupling, 0, quarter * share + index]
            target = slot_ref[coupling, 1, quarter * share + index]
            away = target >> 3
            region = jnp.where(away == owner, 0, jnp.where(away == (owner ^ 1), NBLK, 2 * NBLK))
            empty = source < 0
            s = source & 7
            shift = (s & 3) << 3
            lower = s < 4
            count = (jnp.where(lower, low, high) >> shift) & 255
            table_ref[jnp.where(empty, UNREAD, s * STRIDE + count)] = region + (target & 7)
            one = jnp.where(empty, 0, 1 << shift)
            low, high = low + jnp.where(lower, one, 0), high + jnp.where(lower, 0, one)
    return low, high


def close_table(table_ref, counts):
    for s in range(NBLK):
        count = (counts[s // 4] >> (8 * (s % 4))) & 255
        for extra in range(QUAD - 1):
            table_ref[s * STRIDE + count + extra] = WIN
        table_ref[GROUPS + s] = (count + QUAD - 1) >> 2


def products(source_ref, target_refs, g_ref, first):
    for region, target_ref in enumerate(target_refs, first):
        g = lax.dot_general(
            source_ref[...],
            target_ref[:CELLS, :],
            (((1,), (1,)), ((), ())),
            preferred_element_type=jnp.float32,
        ) * (2.0 * SCALE)
        for block in range(NBLK):
            g_ref[region * NBLK + block] = g[:, block * BLOCK : (block + 1) * BLOCK]


def block_masses(mass_ref, group, first):
    rows = []
    for block in range(NBLK):
        lanes = slice(block * BLOCK, (block + 1) * BLOCK)
        low, high = mass_ref[first : first + 1, lanes], mass_ref[first + 1 : first + 2, lanes]
        rows.append(jnp.where(group == 0, low, high))
    return jnp.concatenate(rows, axis=0)


def pack_kernel(place_ref, cells_hbm, mass_hbm, message_ref, source_ref, mass_ref, sems):
    group = place_ref[1]
    cells = pltpu.make_async_copy(cells_hbm.at[group + 1], message_ref.at[:CELLS], sems.at[0])
    fetched = pltpu.make_async_copy(mass_hbm, mass_ref, sems.at[1])
    source = pltpu.make_async_copy(cells_hbm.at[group], source_ref, sems.at[2])
    fetched.start()
    cells.start()
    source.start()
    fetched.wait()
    masses = block_masses(mass_ref, group, 1) * LOG2E
    cells.wait()
    ones = jnp.ones((8, EMB), jnp.bfloat16)
    norms = []
    for pair in range(NBLK // 2):
        y = message_ref[pair * 256 : (pair + 1) * 256, :].astype(jnp.float32)
        square = y * y
        high = square.astype(jnp.bfloat16)
        low = (square - high.astype(jnp.float32)).astype(jnp.bfloat16)
        norm = sum(
            lax.dot_general(ones, part, (((1,), (1,)), ((), ())), preferred_element_type=jnp.float32)
            for part in (high, low)
        )
        norms += [norm[:1, :BLOCK], norm[:1, BLOCK:]]
    norms = jnp.concatenate(norms, axis=0) * SCALE
    for half, left in enumerate((masses - norms, masses + (LAM - 1.0) * norms)):
        parts = []
        for _ in range(3):
            part = left.astype(jnp.bfloat16).astype(jnp.float32)
            parts.append(part)
            left = left - part
        parts.append(jnp.zeros_like(left))
        packed = jnp.concatenate(parts, axis=0).astype(jnp.bfloat16)
        message_ref[CELLS:, half * BLOCK : (half + 1) * BLOCK] = packed
    source.wait()


def unpack(message_ref, window_ref, region):
    parts = message_ref[CELLS:, :].astype(jnp.float32)
    for half in range(2):
        p = parts[:, half * BLOCK : (half + 1) * BLOCK]
        total = (p[:NBLK] + p[NBLK : 2 * NBLK]) + p[2 * NBLK : 3 * NBLK]
        window_ref[half, region * NBLK : (region + 1) * NBLK, :] = total


STRIPS = BLOCK // 8


def extended(hh_ref, terms_ref):
    for t in range(WIN):
        terms_ref[t] = jnp.broadcast_to(hh_ref[t : t + 1, :], (8, BLOCK))
    terms_ref[WIN] = jnp.full((8, BLOCK), -BIG, jnp.float32)


def source_rows(s):
    return pl.ds(pl.multiple_of(s * BLOCK, BLOCK), BLOCK)


def group_targets(table_ref, s, q):
    return [table_ref[s * STRIDE + q * QUAD + k] for k in range(QUAD)]


def strips(g_ref, t, s):
    return g_ref[jnp.minimum(t, WIN - 1), source_rows(s), :].reshape(STRIPS, 8, BLOCK)


def row_maxima(table_ref, terms_ref, g_ref, m_ref):
    @pl.loop(0, NBLK)
    def _(s):
        def step(q, highest):
            v = [strips(g_ref, t, s) + terms_ref[t] for t in group_targets(table_ref, s, q)]
            return jnp.maximum(highest, jnp.maximum(jnp.maximum(v[0], v[1]), jnp.maximum(v[2], v[3])))

        start = jnp.full((STRIPS, 8, BLOCK), -BIG, jnp.float32)
        highest = lax.fori_loop(0, table_ref[GROUPS + s], step, start)
        m_ref[source_rows(s), :] = highest.reshape(BLOCK, BLOCK)

    m_ref[...] = jnp.broadcast_to(jnp.max(m_ref[...], axis=1, keepdims=True), m_ref.shape)


def sweep_kernel(table_ref, hh_ref, kc_ref, g_ref, part_ref, terms_ref, top_ref, mass_ref, m_ref, acc_ref):
    extended(hh_ref, terms_ref)
    top_ref[...] = jnp.full(top_ref.shape, -BIG, jnp.float32)
    mass_ref[...] = jnp.zeros(mass_ref.shape, jnp.float32)

    @pl.loop(0, NBLK)
    def _(s):
        def step(q, carried):
            top, acc = carried
            v = [strips(g_ref, t, s) + terms_ref[t] for t in group_targets(table_ref, s, q)]
            high = jnp.maximum(jnp.maximum(v[0], v[1]), jnp.maximum(v[2], v[3]))
            high = jnp.maximum(top, high)
            e = [jnp.exp2(part - high) for part in v]
            return high, acc * jnp.exp2(top - high) + ((e[0] + e[1]) + (e[2] + e[3]))

        shape = (STRIPS, 8, BLOCK)
        start = jnp.full(shape, -BIG, jnp.float32), jnp.zeros(shape, jnp.float32)
        top, acc = lax.fori_loop(0, table_ref[GROUPS + s], step, start)
        m_ref[source_rows(s), :] = top.reshape(BLOCK, BLOCK)
        acc_ref[source_rows(s), :] = acc.reshape(BLOCK, BLOCK)

    tops = m_ref[...]
    high = jnp.max(tops, axis=1, keepdims=True)
    sums = jnp.sum(acc_ref[...] * jnp.exp2(tops - high), axis=1, keepdims=True)
    acc_ref[...] = kc_ref[...] - LAM * (high + LOG2E * jnp.log(sums))

    @pl.loop(0, NBLK)
    def _(s):
        uu = acc_ref[source_rows(s), :].reshape(STRIPS, 8, BLOCK)
        groups = table_ref[GROUPS + s]

        def columns(ts):
            tops = [top_ref[t] for t in ts]
            masses = [mass_ref[t] for t in ts]
            made = []
            for t, top, mass in zip(ts, tops, masses):
                v = strips(g_ref, t, s) + uu
                high = jnp.maximum(top, jnp.max(v, axis=0))
                made.append((high, mass * jnp.exp2(top - high) + jnp.sum(jnp.exp2(v - high), axis=0)))
            for t, (high, mass) in zip(ts, made):
                top_ref[t] = high
                mass_ref[t] = mass

        @pl.loop(0, groups // 2)
        def _(double):
            columns(group_targets(table_ref, s, 2 * double) + group_targets(table_ref, s, 2 * double + 1))

        @pl.when(groups % 2 == 1)
        def _():
            columns(group_targets(table_ref, s, groups - 1))

    top = top_ref[:WIN]
    high = jnp.max(top, axis=1, keepdims=True)
    part_ref[0] = high[:, 0, :]
    part_ref[1] = jnp.sum(mass_ref[:WIN] * jnp.exp2(top - high), axis=1)


def weigh(table_ref, hh_ref, g_ref, w_ref, sum_ref, terms_ref, m_ref):
    extended(hh_ref, terms_ref)
    row_maxima(table_ref, terms_ref, g_ref, m_ref)

    @pl.loop(0, NBLK)
    def _(s):
        rows = source_rows(s)
        m = m_ref[rows, :].reshape(STRIPS, 8, BLOCK)

        def step(q, acc):
            ts = group_targets(table_ref, s, q)
            v = [jnp.exp2(strips(g_ref, t, s) + terms_ref[t] - m) for t in ts]
            for t, e in zip(ts, v):
                lanes = pl.ds(pl.multiple_of(t * BLOCK, BLOCK), BLOCK)
                w_ref[rows, lanes] = e.reshape(BLOCK, BLOCK).astype(jnp.bfloat16)
            return acc + ((v[0] + v[1]) + (v[2] + v[3]))

        start = jnp.zeros((STRIPS, 8, BLOCK), jnp.float32)
        acc = lax.fori_loop(0, table_ref[GROUPS + s], step, start)
        sum_ref[rows, :] = acc.reshape(BLOCK, BLOCK)

    sum_ref[...] = jnp.broadcast_to(jnp.sum(sum_ref[...], axis=1, keepdims=True), sum_ref.shape)


def pulled(w_ref, rows, fate_refs, first):
    total = 0.0
    for region, fate_ref in enumerate(fate_refs, first):
        total += jnp.dot(
            w_ref[rows, region * CELLS : (region + 1) * CELLS],
            fate_ref[...],
            preferred_element_type=jnp.float32,
        )
    return total


def divided(total, sums):
    inverse = 1.0 / sums
    return (total * jnp.concatenate([inverse, inverse], axis=1)).astype(jnp.bfloat16)


def chunks(body):
    for chunk in range(2):
        body(slice(chunk * 512, (chunk + 1) * 512))


def near_kernel(place_ref, *refs):
    *slot_refs, mass_hbm, source_ref, own_ref, sib_ref = refs[: len(refs) - 6]
    g_ref, kc_ref, window_ref, table_ref, mass_ref, sem = refs[len(refs) - 6 :]
    group = place_ref[1]
    fetched = pltpu.make_async_copy(mass_hbm, mass_ref, sem)
    fetched.start()
    unpack(own_ref, window_ref, 0)
    unpack(sib_ref, window_ref, 1)

    def step(quarter, counts):
        return enter_slots(place_ref, group, slot_refs, table_ref, quarter, counts)

    zero = jnp.int32(0)
    counts = (zero, zero)
    for quarter in range(4):
        counts = step(quarter, counts)
    products(source_ref, (own_ref, sib_ref), g_ref, 0)
    close_table(table_ref, counts)
    fetched.wait()
    masses = block_masses(mass_ref, group, 0)
    for s in range(NBLK):
        x = source_ref[s * BLOCK : (s + 1) * BLOCK, :].astype(jnp.float32)
        norm = jnp.sum(x * x, axis=1, keepdims=True) * SCALE
        mass = jnp.broadcast_to(masses[s : s + 1, :], (BLOCK, BLOCK)).T
        kc_ref[s * BLOCK : (s + 1) * BLOCK, :] = mass * LOG2E + (LAM - 1.0) * norm


def far_kernel(table_ref, source_ref, out_ref, near_ref, near_window_ref, kc_ref, g_ref, window_ref, part_ref, *scratch):
    del near_ref
    window_ref[:, : 2 * NBLK, :] = near_window_ref[...]
    unpack(out_ref, window_ref, 2)
    products(source_ref, (out_ref,), g_ref, 2)
    sweep_kernel(table_ref, window_ref.at[0], kc_ref, g_ref, part_ref, *scratch)


def other_kernel(behind_ref, source_ref, own_ref, sib_ref, out_ref, g_ref):
    del behind_ref
    products(source_ref, (own_ref, sib_ref, out_ref), g_ref, 0)


def rest_kernel(place_ref, behind_ref, arrived_ref, *refs):
    del behind_ref, arrived_ref
    *slot_refs, cells_hbm, table_ref, source_ref, target_ref, sems = refs
    group = place_ref[1]
    copies = (
        pltpu.make_async_copy(cells_hbm.at[2 - group], target_ref, sems.at[0]),
        pltpu.make_async_copy(cells_hbm.at[1 - group], source_ref, sems.at[1]),
    )
    for copy in copies:
        copy.start()

    def step(quarter, counts):
        return enter_slots(place_ref, 1 - group, slot_refs, table_ref, quarter, counts)

    zero = jnp.int32(0)
    close_table(table_ref, lax.fori_loop(0, 4, step, (zero, zero)))
    for copy in copies:
        copy.wait()


def weigh_one(coupling, place_ref, mine, others, *outs):
    @pl.when(place_ref[1] == coupling)
    def _():
        weigh(*mine, *outs)

    @pl.when(place_ref[1] != coupling)
    def _():
        weigh(*others, *outs)


def blank_kernel(behind_ref, w_ref):
    del behind_ref

    @pl.loop(0, NBLK)
    def _(s):
        w_ref[source_rows(s), :] = jnp.zeros((BLOCK, (WIN + 1) * BLOCK), jnp.bfloat16)


def late_kernel(place_ref, table_ref, hh_ref, g_ref, table2_ref, hh2_ref, g2_ref, own_ref, sib_ref, out_ref, blank_ref, late_ref, w_ref, sum_ref, terms_ref, m_ref):
    del blank_ref
    weigh_one(1, place_ref, (table_ref, hh_ref, g_ref), (table2_ref, hh2_ref, g2_ref), w_ref, sum_ref, terms_ref, m_ref)
    fates = (own_ref, sib_ref, out_ref)

    @chunks
    def _(rows):
        late_ref[rows, :] = divided(pulled(w_ref, rows, fates, 0), sum_ref[rows, :])


def early_weights_kernel(place_ref, table_ref, hh_ref, g_ref, table2_ref, hh2_ref, g2_ref, w_ref, sum_ref, terms_ref, m_ref):
    blank_kernel(None, w_ref)
    weigh_one(0, place_ref, (table_ref, hh_ref, g_ref), (table2_ref, hh2_ref, g2_ref), w_ref, sum_ref, terms_ref, m_ref)


def early_near_kernel(w_ref, own_ref, sib_ref, total_ref):
    @chunks
    def _(rows):
        total_ref[rows, :] = pulled(w_ref, rows, (own_ref, sib_ref), 0)


def early_kernel(w_ref, sum_ref, total_ref, out_ref, early_ref):
    @chunks
    def _(rows):
        total = total_ref[rows, :] + pulled(w_ref, rows, (out_ref,), 2)
        early_ref[rows, :] = divided(total, sum_ref[rows, :])


G_SHAPE = pltpu.VMEM((WIN, CELLS, BLOCK), jnp.float32)
PART_SHAPE = jax.ShapeDtypeStruct((2, WIN, BLOCK), jnp.float32)
W_SHAPE = jax.ShapeDtypeStruct((CELLS, (WIN + 1) * BLOCK), jnp.bfloat16)
COLUMN_SHAPE = jax.ShapeDtypeStruct((CELLS, BLOCK), jnp.float32)
FATE_SHAPE = jax.ShapeDtypeStruct((CELLS, EMB), jnp.bfloat16)
TOTAL_SHAPE = jax.ShapeDtypeStruct((CELLS, EMB), jnp.float32)
TERMS = pltpu.VMEM((WIN + 1, 8, BLOCK), jnp.float32)
COLUMN = pltpu.VMEM(COLUMN_SHAPE.shape, COLUMN_SHAPE.dtype)
SWEEP_SCRATCH = [TERMS] * 3 + [COLUMN] * 2


WINDOW_SHAPE = jax.ShapeDtypeStruct((2, WIN, BLOCK), jnp.float32)
NEAR_SHAPE = jax.ShapeDtypeStruct((2, 2 * NBLK, BLOCK), jnp.float32)


TABLE_SHAPE = jax.ShapeDtypeStruct((TABLE,), jnp.int32)
MESSAGE_SHAPE = jax.ShapeDtypeStruct((CELLS + 4 * NBLK, EMB), jnp.bfloat16)
MASSES = pltpu.VMEM((3, CELLS), jnp.float32)


def target_message(*args):
    scratch = [MASSES, pltpu.SemaphoreType.DMA((3,))]
    return call(pack_kernel, (MESSAGE_SHAPE, FATE_SHAPE), (VMEM, VMEM), [SMEM, HBM, HBM], scratch)(*args)


def near_products(place, slots, *args):
    outs = (G_SHAPE, COLUMN_SHAPE, NEAR_SHAPE, TABLE_SHAPE)
    in_specs = [SMEM] * (1 + len(slots)) + [HBM, VMEM, VMEM, VMEM]
    scratch = [MASSES, pltpu.SemaphoreType.DMA]
    return call(near_kernel, outs, (VMEM,) * 3 + (SMEM,), in_specs, scratch)(place, *slots, *args)


def far_products(*args):
    outs = (G_SHAPE, WINDOW_SHAPE, PART_SHAPE)
    return call(far_kernel, outs, (VMEM,) * 3, [SMEM] + [VMEM] * 5, SWEEP_SCRATCH, {3: 0})(*args)


def sweep(*args):
    return call(sweep_kernel, PART_SHAPE, VMEM, [SMEM] + [VMEM] * 3, SWEEP_SCRATCH)(*args)


def other_products(*args):
    return call(other_kernel, G_SHAPE, VMEM, [ANY] + [VMEM] * 4)(*args)


def other_inputs(place, behind, arrived, slots, *args):
    outs = (TABLE_SHAPE, FATE_SHAPE, FATE_SHAPE)
    in_specs = [SMEM, ANY, ANY] + [SMEM] * len(slots) + [HBM]
    scratch = [pltpu.SemaphoreType.DMA((2,))]
    return call(rest_kernel, outs, (SMEM, VMEM, VMEM), in_specs, scratch)(place, behind, arrived, *slots, *args)


COUPLINGS = [SMEM, SMEM, VMEM, VMEM, SMEM, VMEM, VMEM]


def blank_weights(behind):
    return call(blank_kernel, W_SHAPE, VMEM, [ANY])(behind)


def late_fates(*args):
    outs, in_specs = (FATE_SHAPE, W_SHAPE), COUPLINGS + [VMEM] * 4
    return call(late_kernel, outs, (VMEM, VMEM), in_specs, [COLUMN, TERMS, COLUMN], {10: 1})(*args)[0]


def early_weights(*args):
    return call(early_weights_kernel, (W_SHAPE, COLUMN_SHAPE), (VMEM, VMEM), COUPLINGS, [TERMS, COLUMN])(*args)


def early_near(*args):
    return call(early_near_kernel, TOTAL_SHAPE, VMEM, [VMEM] * 3)(*args)


def early_fates(*args):
    return call(early_kernel, FATE_SHAPE, VMEM, [VMEM] * 4)(*args)


def merged(first, second):
    highest = jnp.maximum(first[0], second[0])
    return jnp.stack(
        [
            highest,
            first[1] * jnp.exp2(first[0] - highest) + second[1] * jnp.exp2(second[0] - highest),
        ]
    )


def folded(part, beside):
    own = merged(part[:, :NBLK], sibling(part[:, NBLK : 2 * NBLK]))
    beyond = part[:, 2 * NBLK :]
    message = jnp.concatenate([own, beyond], axis=1)
    arrived, made = lax.optimization_barrier((outward(message), beside(message)))
    own = merged(own, arrived[:, NBLK:])
    out = merged(arrived[:, :NBLK], beyond)
    own_total = own[0] + jnp.log2(own[1])
    out_total = out[0] + jnp.log2(out[1])
    return jnp.concatenate([own_total, sibling(own_total), out_total], axis=0), made


def shifted(value, steps):
    count = lax.axis_size("tiles")
    return lax.ppermute(value, "tiles", [(t, (t + steps) % count) for t in range(count)])


def on_device(embeddings, log_mass, signatures, tile_list):
    owner = lax.axis_index("cells").astype(jnp.int32)
    group = (lax.axis_index("tiles") >= 2).astype(jnp.int32)
    place = jnp.stack([owner, group])

    cells, masses = (
        pltpu.with_memory_space_constraint(array, pltpu.HBM) for array in (embeddings, log_mass)
    )
    target, source = target_message(place, cells, masses)
    target_out, target_sib = outward(target), sibling(target)
    slots, fates, target_sib = lax.optimization_barrier((tile_list, signatures, target_sib))
    fates_out, fates_sib = outward(fates), sibling(fates)
    gathered = [pltpu.with_memory_space_constraint(tile_list, pltpu.HBM)] + [shifted(slots, k) for k in range(1, lax.axis_size("tiles"))]
    g, kc, near, table = near_products(place, gathered, masses, source, target, target_sib)
    g, window, part = far_products(table, source, target_out, g, near, kc)

    totals, (table_other, other_source, other) = folded(
        part, lambda message: other_inputs(place, message, fates_out, gathered, cells)
    )
    other_out, other_sib = outward(other), sibling(other)
    hh = window[1] - LAM * totals
    part = sweep(table, hh, kc, g)
    totals, g_other = folded(
        part, lambda message: other_products(message, other_source, other, other_sib, other_out)
    )
    hh = window[1] - LAM * totals
    couplings = (place, table, hh, g, table_other, mirrored(hh), g_other)
    late = late_fates(*couplings, signatures, fates_sib, fates_out, blank_weights(hh))
    late_out, late_sib = outward(late), sibling(late)
    weights, sums = early_weights(*couplings)
    total = early_near(weights, late, late_sib)
    early = early_fates(weights, sums, total, late_out)
    return early, late


def solution(mesh):
    in_specs = (
        P(None, "cells", None),
        P(None, "cells"),
        P("cells", None),
        P(None, None, ("cells", "tiles")),
    )
    out_specs = (P("cells", None), P("cells", None))
    return jax.shard_map(
        on_device, mesh=mesh, in_specs=in_specs, out_specs=out_specs, check_vma=False
    )
```

```python
import jax
import jax.numpy as jnp
from jax import lax
from jax.experimental import pallas as pl
from jax.experimental.pallas import tpu as pltpu
from jax.sharding import PartitionSpec as P

EMB = 256
BLOCK = 128
NBLK = 8
WIN = 3 * NBLK
CELLS = NBLK * BLOCK
EPS = 0.01
RHO = 1.0
LAM = RHO / (RHO + EPS)
BIG = 1e30

LOG2E = 1.4426950408889634
SCALE = LOG2E / (EMB * EPS)

QUAD = 4
STRIDE = 32
GROUPS = NBLK * STRIDE
UNREAD = GROUPS + NBLK
TABLE = 384

FLOPS, BYTES, MIB = 3 * 10**9, 10**4, 4
VMEM = pl.BlockSpec(memory_space=pltpu.VMEM)
SMEM = pl.BlockSpec(memory_space=pltpu.SMEM)
ANY = pl.BlockSpec(memory_space=pl.ANY)
HBM = pl.BlockSpec(memory_space=pltpu.HBM)


def sibling(value):
    return lax.ppermute(value, "cells", [(c, c ^ 1) for c in range(lax.axis_size("cells"))])


def outward(value):
    count = lax.axis_size("cells")
    pairs = [(c, (c + 1 if c % 2 else c - 1) % count) for c in range(count)]
    return lax.ppermute(value, "cells", pairs)


def mirrored(value):
    count = lax.axis_size("tiles")
    return lax.ppermute(value, "tiles", [(t, count - 1 - t) for t in range(count)])


def call(kernel, outs, out_specs, in_specs, scratch=(), aliases=None, flops=FLOPS, mib=MIB):
    return pl.pallas_call(
        kernel,
        out_shape=outs,
        in_specs=in_specs,
        out_specs=out_specs,
        scratch_shapes=list(scratch),
        input_output_aliases=aliases or {},
        compiler_params=pltpu.CompilerParams(vmem_limit_bytes=mib << 20),
        cost_estimate=pl.CostEstimate(flops=flops, bytes_accessed=BYTES, transcendentals=0),
    )


def enter_slots(place_ref, coupling, slot_refs, table_ref, quarter, counts):
    low, high = counts
    owner = place_ref[0]
    share = slot_refs[0].shape[2] // 4
    for index in range(share):
        for slot_ref in slot_refs:
            source = slot_ref[coupling, 0, quarter * share + index]
            target = slot_ref[coupling, 1, quarter * share + index]
            away = target >> 3
            region = jnp.where(away == owner, 0, jnp.where(away == (owner ^ 1), NBLK, 2 * NBLK))
            empty = source < 0
            s = source & 7
            shift = (s & 3) << 3
            lower = s < 4
            count = (jnp.where(lower, low, high) >> shift) & 255
            table_ref[jnp.where(empty, UNREAD, s * STRIDE + count)] = region + (target & 7)
            one = jnp.where(empty, 0, 1 << shift)
            low, high = low + jnp.where(lower, one, 0), high + jnp.where(lower, 0, one)
    return low, high


def close_table(table_ref, counts):
    for s in range(NBLK):
        count = (counts[s // 4] >> (8 * (s % 4))) & 255
        for extra in range(QUAD - 1):
            table_ref[s * STRIDE + count + extra] = WIN
        table_ref[GROUPS + s] = (count + QUAD - 1) >> 2


def products(source_ref, target_refs, g_ref, first):
    for region, target_ref in enumerate(target_refs, first):
        g = lax.dot_general(
            source_ref[...],
            target_ref[:CELLS, :],
            (((1,), (1,)), ((), ())),
            preferred_element_type=jnp.float32,
        ) * (2.0 * SCALE)
        for block in range(NBLK):
            g_ref[region * NBLK + block] = g[:, block * BLOCK : (block + 1) * BLOCK]


def block_masses(mass_ref, group, first):
    rows = []
    for block in range(NBLK):
        lanes = slice(block * BLOCK, (block + 1) * BLOCK)
        low, high = mass_ref[first : first + 1, lanes], mass_ref[first + 1 : first + 2, lanes]
        rows.append(jnp.where(group == 0, low, high))
    return jnp.concatenate(rows, axis=0)


def pack_kernel(place_ref, cells_hbm, mass_hbm, message_ref, source_ref, mass_ref, sems):
    group = place_ref[1]
    cells = pltpu.make_async_copy(cells_hbm.at[group + 1], message_ref.at[:CELLS], sems.at[0])
    fetched = pltpu.make_async_copy(mass_hbm, mass_ref, sems.at[1])
    source = pltpu.make_async_copy(cells_hbm.at[group], source_ref, sems.at[2])
    fetched.start()
    cells.start()
    source.start()
    fetched.wait()
    masses = block_masses(mass_ref, group, 1) * LOG2E
    cells.wait()
    ones = jnp.ones((8, EMB), jnp.bfloat16)
    norms = []
    for pair in range(NBLK // 2):
        y = message_ref[pair * 256 : (pair + 1) * 256, :].astype(jnp.float32)
        square = y * y
        high = square.astype(jnp.bfloat16)
        low = (square - high.astype(jnp.float32)).astype(jnp.bfloat16)
        norm = sum(
            lax.dot_general(ones, part, (((1,), (1,)), ((), ())), preferred_element_type=jnp.float32)
            for part in (high, low)
        )
        norms += [norm[:1, :BLOCK], norm[:1, BLOCK:]]
    norms = jnp.concatenate(norms, axis=0) * SCALE
    for half, left in enumerate((masses - norms, masses + (LAM - 1.0) * norms)):
        parts = []
        for _ in range(3):
            part = left.astype(jnp.bfloat16).astype(jnp.float32)
            parts.append(part)
            left = left - part
        parts.append(jnp.zeros_like(left))
        packed = jnp.concatenate(parts, axis=0).astype(jnp.bfloat16)
        message_ref[CELLS:, half * BLOCK : (half + 1) * BLOCK] = packed
    source.wait()


def unpack(message_ref, window_ref, region):
    parts = message_ref[CELLS:, :].astype(jnp.float32)
    for half in range(2):
        p = parts[:, half * BLOCK : (half + 1) * BLOCK]
        total = (p[:NBLK] + p[NBLK : 2 * NBLK]) + p[2 * NBLK : 3 * NBLK]
        window_ref[half, region * NBLK : (region + 1) * NBLK, :] = total


STRIPS = BLOCK // 8


def extended(hh_ref, terms_ref):
    for t in range(WIN):
        terms_ref[t] = jnp.broadcast_to(hh_ref[t : t + 1, :], (8, BLOCK))
    terms_ref[WIN] = jnp.full((8, BLOCK), -BIG, jnp.float32)


def source_rows(s):
    if isinstance(s, int):
        return slice(s * BLOCK, (s + 1) * BLOCK)
    return pl.ds(pl.multiple_of(s * BLOCK, BLOCK), BLOCK)


def over_groups(table_ref, s, step, start):
    groups = table_ref[GROUPS + s]
    carried = lax.fori_loop(
        0, groups // 2, lambda double, so_far: step(2 * double + 1, step(2 * double, so_far)), start
    )
    return lax.cond(
        groups % 2 == 1, lambda so_far: step(groups - 1, so_far), lambda so_far: so_far, carried
    )


def group_targets(table_ref, s, q):
    return [table_ref[s * STRIDE + q * QUAD + k] for k in range(QUAD)]


def strips(g_ref, t, s):
    return g_ref[jnp.minimum(t, WIN - 1), source_rows(s), :].reshape(STRIPS, 8, BLOCK)


def over_sources(body):
    for s in range(NBLK):
        body(s)


def row_maxima(table_ref, terms_ref, g_ref, m_ref):
    @pl.loop(0, NBLK)
    def _(s):
        def step(q, highest):
            v = [strips(g_ref, t, s) + terms_ref[t] for t in group_targets(table_ref, s, q)]
            return jnp.maximum(highest, jnp.maximum(jnp.maximum(v[0], v[1]), jnp.maximum(v[2], v[3])))

        start = jnp.full((STRIPS, 8, BLOCK), -BIG, jnp.float32)
        highest = lax.fori_loop(0, table_ref[GROUPS + s], step, start)
        m_ref[source_rows(s), :] = highest.reshape(BLOCK, BLOCK)

    m_ref[...] = jnp.broadcast_to(jnp.max(m_ref[...], axis=1, keepdims=True), m_ref.shape)


def sweep_kernel(table_ref, hh_ref, kc_ref, g_ref, part_ref, terms_ref, top_ref, mass_ref, m_ref, acc_ref):
    extended(hh_ref, terms_ref)
    top_ref[...] = jnp.full(top_ref.shape, -BIG, jnp.float32)
    mass_ref[...] = jnp.zeros(mass_ref.shape, jnp.float32)

    @over_sources
    def _(s):
        def step(q, carried):
            top, acc = carried
            v = [strips(g_ref, t, s) + terms_ref[t] for t in group_targets(table_ref, s, q)]
            high = jnp.maximum(jnp.maximum(v[0], v[1]), jnp.maximum(v[2], v[3]))
            high = jnp.maximum(top, high)
            e = [jnp.exp2(part - high) for part in v]
            return high, acc * jnp.exp2(top - high) + ((e[0] + e[1]) + (e[2] + e[3]))

        shape = (STRIPS, 8, BLOCK)
        start = jnp.full(shape, -BIG, jnp.float32), jnp.zeros(shape, jnp.float32)
        top, acc = over_groups(table_ref, s, step, start)
        m_ref[source_rows(s), :] = top.reshape(BLOCK, BLOCK)
        acc_ref[source_rows(s), :] = acc.reshape(BLOCK, BLOCK)

    tops = m_ref[...]
    high = jnp.max(tops, axis=1, keepdims=True)
    sums = jnp.sum(acc_ref[...] * jnp.exp2(tops - high), axis=1, keepdims=True)
    acc_ref[...] = kc_ref[...] - LAM * (high + LOG2E * jnp.log(sums))

    @over_sources
    def _(s):
        uu = acc_ref[source_rows(s), :].reshape(STRIPS, 8, BLOCK)
        groups = table_ref[GROUPS + s]

        def columns(ts):
            tops = [top_ref[t] for t in ts]
            masses = [mass_ref[t] for t in ts]
            made = []
            for t, top, mass in zip(ts, tops, masses):
                v = strips(g_ref, t, s) + uu
                high = jnp.maximum(top, jnp.max(v, axis=0))
                made.append((high, mass * jnp.exp2(top - high) + jnp.sum(jnp.exp2(v - high), axis=0)))
            for t, (high, mass) in zip(ts, made):
                top_ref[t] = high
                mass_ref[t] = mass

        @pl.loop(0, groups // 2)
        def _(double):
            columns(group_targets(table_ref, s, 2 * double) + group_targets(table_ref, s, 2 * double + 1))

        @pl.when(groups % 2 == 1)
        def _():
            columns(group_targets(table_ref, s, groups - 1))

    top = top_ref[:WIN]
    high = jnp.max(top, axis=1, keepdims=True)
    part_ref[0] = high[:, 0, :]
    part_ref[1] = jnp.sum(mass_ref[:WIN] * jnp.exp2(top - high), axis=1)


def weigh(table_ref, hh_ref, g_ref, w_ref, sum_ref, terms_ref, m_ref):
    extended(hh_ref, terms_ref)
    row_maxima(table_ref, terms_ref, g_ref, m_ref)

    @pl.loop(0, NBLK)
    def _(s):
        rows = source_rows(s)
        m = m_ref[rows, :].reshape(STRIPS, 8, BLOCK)

        def step(q, acc):
            ts = group_targets(table_ref, s, q)
            v = [jnp.exp2(strips(g_ref, t, s) + terms_ref[t] - m) for t in ts]
            for t, e in zip(ts, v):
                lanes = pl.ds(pl.multiple_of(t * BLOCK, BLOCK), BLOCK)
                w_ref[rows, lanes] = e.reshape(BLOCK, BLOCK).astype(jnp.bfloat16)
            return acc + ((v[0] + v[1]) + (v[2] + v[3]))

        start = jnp.zeros((STRIPS, 8, BLOCK), jnp.float32)
        acc = lax.fori_loop(0, table_ref[GROUPS + s], step, start)
        sum_ref[rows, :] = acc.reshape(BLOCK, BLOCK)

    sum_ref[...] = jnp.broadcast_to(jnp.sum(sum_ref[...], axis=1, keepdims=True), sum_ref.shape)


def pulled(w_ref, rows, fate_refs, first):
    total = 0.0
    for region, fate_ref in enumerate(fate_refs, first):
        total += jnp.dot(
            w_ref[rows, region * CELLS : (region + 1) * CELLS],
            fate_ref[...],
            preferred_element_type=jnp.float32,
        )
    return total


def divided(total, sums):
    inverse = 1.0 / sums
    return (total * jnp.concatenate([inverse, inverse], axis=1)).astype(jnp.bfloat16)


def chunks(body):
    for chunk in range(2):
        body(slice(chunk * 512, (chunk + 1) * 512))


def near_kernel(place_ref, *refs):
    *slot_refs, mass_hbm, source_ref, own_ref, sib_ref = refs[: len(refs) - 6]
    g_ref, kc_ref, window_ref, table_ref, mass_ref, sem = refs[len(refs) - 6 :]
    group = place_ref[1]
    fetched = pltpu.make_async_copy(mass_hbm, mass_ref, sem)
    fetched.start()
    unpack(own_ref, window_ref, 0)
    unpack(sib_ref, window_ref, 1)

    def step(quarter, counts):
        return enter_slots(place_ref, group, slot_refs, table_ref, quarter, counts)

    zero = jnp.int32(0)
    counts = (zero, zero)
    for quarter in range(4):
        counts = step(quarter, counts)
    products(source_ref, (own_ref, sib_ref), g_ref, 0)
    close_table(table_ref, counts)
    fetched.wait()
    masses = block_masses(mass_ref, group, 0)
    for s in range(NBLK):
        x = source_ref[s * BLOCK : (s + 1) * BLOCK, :].astype(jnp.float32)
        norm = jnp.sum(x * x, axis=1, keepdims=True) * SCALE
        mass = jnp.broadcast_to(masses[s : s + 1, :], (BLOCK, BLOCK)).T
        kc_ref[s * BLOCK : (s + 1) * BLOCK, :] = mass * LOG2E + (LAM - 1.0) * norm


def far_kernel(table_ref, source_ref, out_ref, near_ref, near_window_ref, kc_ref, g_ref, window_ref, part_ref, *scratch):
    del near_ref
    window_ref[:, : 2 * NBLK, :] = near_window_ref[...]
    unpack(out_ref, window_ref, 2)
    products(source_ref, (out_ref,), g_ref, 2)
    sweep_kernel(table_ref, window_ref.at[0], kc_ref, g_ref, part_ref, *scratch)


def other_kernel(behind_ref, source_ref, own_ref, sib_ref, out_ref, g_ref):
    del behind_ref
    products(source_ref, (own_ref, sib_ref, out_ref), g_ref, 0)


def rest_kernel(place_ref, behind_ref, arrived_ref, *refs):
    del behind_ref, arrived_ref
    *slot_refs, cells_hbm, table_ref, source_ref, target_ref, sems = refs
    group = place_ref[1]
    copies = (
        pltpu.make_async_copy(cells_hbm.at[2 - group], target_ref, sems.at[0]),
        pltpu.make_async_copy(cells_hbm.at[1 - group], source_ref, sems.at[1]),
    )
    for copy in copies:
        copy.start()

    def step(quarter, counts):
        return enter_slots(place_ref, 1 - group, slot_refs, table_ref, quarter, counts)

    zero = jnp.int32(0)
    close_table(table_ref, lax.fori_loop(0, 4, step, (zero, zero)))
    for copy in copies:
        copy.wait()


def weigh_one(coupling, place_ref, mine, others, *outs):
    @pl.when(place_ref[1] == coupling)
    def _():
        weigh(*mine, *outs)

    @pl.when(place_ref[1] != coupling)
    def _():
        weigh(*others, *outs)


def blank_kernel(behind_ref, w_ref):
    del behind_ref

    @over_sources
    def _(s):
        w_ref[source_rows(s), :] = jnp.zeros((BLOCK, (WIN + 1) * BLOCK), jnp.bfloat16)


def late_kernel(place_ref, table_ref, hh_ref, g_ref, table2_ref, hh2_ref, g2_ref, own_ref, sib_ref, out_ref, blank_ref, late_ref, w_ref, sum_ref, terms_ref, m_ref):
    del blank_ref
    weigh_one(1, place_ref, (table_ref, hh_ref, g_ref), (table2_ref, hh2_ref, g2_ref), w_ref, sum_ref, terms_ref, m_ref)
    fates = (own_ref, sib_ref, out_ref)

    @chunks
    def _(rows):
        late_ref[rows, :] = divided(pulled(w_ref, rows, fates, 0), sum_ref[rows, :])


def early_weights_kernel(place_ref, table_ref, hh_ref, g_ref, table2_ref, hh2_ref, g2_ref, w_ref, sum_ref, terms_ref, m_ref):
    blank_kernel(None, w_ref)
    weigh_one(0, place_ref, (table_ref, hh_ref, g_ref), (table2_ref, hh2_ref, g2_ref), w_ref, sum_ref, terms_ref, m_ref)


def early_near_kernel(w_ref, own_ref, sib_ref, total_ref):
    @chunks
    def _(rows):
        total_ref[rows, :] = pulled(w_ref, rows, (own_ref, sib_ref), 0)


def early_kernel(w_ref, sum_ref, total_ref, out_ref, early_ref):
    @chunks
    def _(rows):
        total = total_ref[rows, :] + pulled(w_ref, rows, (out_ref,), 2)
        early_ref[rows, :] = divided(total, sum_ref[rows, :])


G_SHAPE = pltpu.VMEM((WIN, CELLS, BLOCK), jnp.float32)
PART_SHAPE = jax.ShapeDtypeStruct((2, WIN, BLOCK), jnp.float32)
W_SHAPE = jax.ShapeDtypeStruct((CELLS, (WIN + 1) * BLOCK), jnp.bfloat16)
COLUMN_SHAPE = jax.ShapeDtypeStruct((CELLS, BLOCK), jnp.float32)
FATE_SHAPE = jax.ShapeDtypeStruct((CELLS, EMB), jnp.bfloat16)
TOTAL_SHAPE = jax.ShapeDtypeStruct((CELLS, EMB), jnp.float32)
TERMS = pltpu.VMEM((WIN + 1, 8, BLOCK), jnp.float32)
COLUMN = pltpu.VMEM(COLUMN_SHAPE.shape, COLUMN_SHAPE.dtype)
SWEEP_SCRATCH = [TERMS] * 3 + [COLUMN] * 2


WINDOW_SHAPE = jax.ShapeDtypeStruct((2, WIN, BLOCK), jnp.float32)
NEAR_SHAPE = jax.ShapeDtypeStruct((2, 2 * NBLK, BLOCK), jnp.float32)


TABLE_SHAPE = jax.ShapeDtypeStruct((TABLE,), jnp.int32)
MESSAGE_SHAPE = jax.ShapeDtypeStruct((CELLS + 4 * NBLK, EMB), jnp.bfloat16)
MASSES = pltpu.VMEM((3, CELLS), jnp.float32)


def target_message(*args):
    scratch = [MASSES, pltpu.SemaphoreType.DMA((3,))]
    return call(pack_kernel, (MESSAGE_SHAPE, FATE_SHAPE), (VMEM, VMEM), [SMEM, HBM, HBM], scratch)(*args)


def near_products(place, slots, *args):
    outs = (G_SHAPE, COLUMN_SHAPE, NEAR_SHAPE, TABLE_SHAPE)
    in_specs = [SMEM] * (1 + len(slots)) + [HBM, VMEM, VMEM, VMEM]
    scratch = [MASSES, pltpu.SemaphoreType.DMA]
    return call(near_kernel, outs, (VMEM,) * 3 + (SMEM,), in_specs, scratch)(place, *slots, *args)


def far_products(*args):
    outs = (G_SHAPE, WINDOW_SHAPE, PART_SHAPE)
    return call(far_kernel, outs, (VMEM,) * 3, [SMEM] + [VMEM] * 5, SWEEP_SCRATCH, {3: 0})(*args)


def sweep(*args):
    return call(sweep_kernel, PART_SHAPE, VMEM, [SMEM] + [VMEM] * 3, SWEEP_SCRATCH)(*args)


def other_products(*args):
    return call(other_kernel, G_SHAPE, VMEM, [ANY] + [VMEM] * 4)(*args)


def other_inputs(place, behind, arrived, slots, *args):
    outs = (TABLE_SHAPE, FATE_SHAPE, FATE_SHAPE)
    in_specs = [SMEM, ANY, ANY] + [SMEM] * len(slots) + [HBM]
    scratch = [pltpu.SemaphoreType.DMA((2,))]
    return call(rest_kernel, outs, (SMEM, VMEM, VMEM), in_specs, scratch)(place, behind, arrived, *slots, *args)


COUPLINGS = [SMEM, SMEM, VMEM, VMEM, SMEM, VMEM, VMEM]


def blank_weights(behind):
    return call(blank_kernel, W_SHAPE, VMEM, [ANY])(behind)


def late_fates(*args):
    outs, in_specs = (FATE_SHAPE, W_SHAPE), COUPLINGS + [VMEM] * 4
    return call(late_kernel, outs, (VMEM, VMEM), in_specs, [COLUMN, TERMS, COLUMN], {10: 1})(*args)[0]


def early_weights(*args):
    return call(early_weights_kernel, (W_SHAPE, COLUMN_SHAPE), (VMEM, VMEM), COUPLINGS, [TERMS, COLUMN])(*args)


def early_near(*args):
    return call(early_near_kernel, TOTAL_SHAPE, VMEM, [VMEM] * 3)(*args)


def early_fates(*args):
    return call(early_kernel, FATE_SHAPE, VMEM, [VMEM] * 4)(*args)


def merged(first, second):
    highest = jnp.maximum(first[0], second[0])
    return jnp.stack(
        [
            highest,
            first[1] * jnp.exp2(first[0] - highest) + second[1] * jnp.exp2(second[0] - highest),
        ]
    )


def folded(part, beside):
    own = merged(part[:, :NBLK], sibling(part[:, NBLK : 2 * NBLK]))
    beyond = part[:, 2 * NBLK :]
    message = jnp.concatenate([own, beyond], axis=1)
    arrived, made = lax.optimization_barrier((outward(message), beside(message)))
    own = merged(own, arrived[:, NBLK:])
    out = merged(arrived[:, :NBLK], beyond)
    own_total = own[0] + jnp.log2(own[1])
    out_total = out[0] + jnp.log2(out[1])
    return jnp.concatenate([own_total, sibling(own_total), out_total], axis=0), made


def shifted(value, steps):
    count = lax.axis_size("tiles")
    return lax.ppermute(value, "tiles", [(t, (t + steps) % count) for t in range(count)])


def on_device(embeddings, log_mass, signatures, tile_list):
    owner = lax.axis_index("cells").astype(jnp.int32)
    group = (lax.axis_index("tiles") >= 2).astype(jnp.int32)
    place = jnp.stack([owner, group])

    cells, masses = (
        pltpu.with_memory_space_constraint(array, pltpu.HBM) for array in (embeddings, log_mass)
    )
    target, source = target_message(place, cells, masses)
    target_out, target_sib = outward(target), sibling(target)
    slots, fates, target_sib = lax.optimization_barrier((tile_list, signatures, target_sib))
    fates_out, fates_sib = outward(fates), sibling(fates)
    gathered = [pltpu.with_memory_space_constraint(tile_list, pltpu.HBM)] + [shifted(slots, k) for k in range(1, lax.axis_size("tiles"))]
    g, kc, near, table = near_products(place, gathered, masses, source, target, target_sib)
    g, window, part = far_products(table, source, target_out, g, near, kc)

    totals, (table_other, other_source, other) = folded(
        part, lambda message: other_inputs(place, message, fates_out, gathered, cells)
    )
    other_out, other_sib = outward(other), sibling(other)
    hh = window[1] - LAM * totals
    part = sweep(table, hh, kc, g)
    totals, g_other = folded(
        part, lambda message: other_products(message, other_source, other, other_sib, other_out)
    )
    hh = window[1] - LAM * totals
    couplings = (place, table, hh, g, table_other, mirrored(hh), g_other)
    late = late_fates(*couplings, signatures, fates_sib, fates_out, blank_weights(hh))
    late_out, late_sib = outward(late), sibling(late)
    weights, sums = early_weights(*couplings)
    total = early_near(weights, late, late_sib)
    early = early_fates(weights, sums, total, late_out)
    return early, late


def solution(mesh):
    in_specs = (
        P(None, "cells", None),
        P(None, "cells"),
        P("cells", None),
        P(None, None, ("cells", "tiles")),
    )
    out_specs = (P("cells", None), P("cells", None))
    return jax.shard_map(
        on_device, mesh=mesh, in_specs=in_specs, out_specs=out_specs, check_vma=False
    )
```

```python
import jax
import jax.numpy as jnp
from jax import lax
from jax.experimental import pallas as pl
from jax.experimental.pallas import tpu as pltpu
from jax.sharding import PartitionSpec as P

EMB = 256
BLOCK = 128
NBLK = 8
WIN = 3 * NBLK
CELLS = NBLK * BLOCK
EPS = 0.01
RHO = 1.0
LAM = RHO / (RHO + EPS)
BIG = 1e30

LOG2E = 1.4426950408889634
SCALE = LOG2E / (EMB * EPS)

STRIDE = 32
PAIRS = NBLK * STRIDE
UNREAD = PAIRS + NBLK
TABLE = 384

FLOPS, BYTES, MIB = 3 * 10**9, 10**4, 4
VMEM = pl.BlockSpec(memory_space=pltpu.VMEM)
SMEM = pl.BlockSpec(memory_space=pltpu.SMEM)
ANY = pl.BlockSpec(memory_space=pl.ANY)
HBM = pl.BlockSpec(memory_space=pltpu.HBM)


def sibling(value):
    return lax.ppermute(value, "cells", [(c, c ^ 1) for c in range(lax.axis_size("cells"))])


def outward(value):
    count = lax.axis_size("cells")
    pairs = [(c, (c + 1 if c % 2 else c - 1) % count) for c in range(count)]
    return lax.ppermute(value, "cells", pairs)


def mirrored(value):
    count = lax.axis_size("tiles")
    return lax.ppermute(value, "tiles", [(t, count - 1 - t) for t in range(count)])


def call(kernel, outs, out_specs, in_specs, scratch=(), aliases=None, flops=FLOPS, mib=MIB):
    return pl.pallas_call(
        kernel,
        out_shape=outs,
        in_specs=in_specs,
        out_specs=out_specs,
        scratch_shapes=list(scratch),
        input_output_aliases=aliases or {},
        compiler_params=pltpu.CompilerParams(vmem_limit_bytes=mib << 20),
        cost_estimate=pl.CostEstimate(flops=flops, bytes_accessed=BYTES, transcendentals=0),
    )


def enter_slots(place_ref, coupling, slot_refs, table_ref, quarter, counts):
    low, high = counts
    owner = place_ref[0]
    share = slot_refs[0].shape[2] // 4
    for index in range(share):
        for slot_ref in slot_refs:
            source = slot_ref[coupling, 0, quarter * share + index]
            target = slot_ref[coupling, 1, quarter * share + index]
            away = target >> 3
            region = jnp.where(away == owner, 0, jnp.where(away == (owner ^ 1), NBLK, 2 * NBLK))
            empty = source < 0
            s = source & 7
            shift = (s & 3) << 3
            lower = s < 4
            count = (jnp.where(lower, low, high) >> shift) & 255
            table_ref[jnp.where(empty, UNREAD, s * STRIDE + count)] = region + (target & 7)
            one = jnp.where(empty, 0, 1 << shift)
            low, high = low + jnp.where(lower, one, 0), high + jnp.where(lower, 0, one)
    return low, high


def close_table(table_ref, counts):
    for s in range(NBLK):
        count = (counts[s // 4] >> (8 * (s % 4))) & 255
        table_ref[s * STRIDE + count] = WIN
        table_ref[PAIRS + s] = (count + 1) >> 1


def products(source_ref, target_refs, g_ref, first):
    for region, target_ref in enumerate(target_refs, first):
        g = lax.dot_general(
            source_ref[...],
            target_ref[:CELLS, :],
            (((1,), (1,)), ((), ())),
            preferred_element_type=jnp.float32,
        ) * (2.0 * SCALE)
        for block in range(NBLK):
            g_ref[region * NBLK + block] = g[:, block * BLOCK : (block + 1) * BLOCK]


def block_masses(mass_ref, group, first):
    rows = []
    for block in range(NBLK):
        lanes = slice(block * BLOCK, (block + 1) * BLOCK)
        low, high = mass_ref[first : first + 1, lanes], mass_ref[first + 1 : first + 2, lanes]
        rows.append(jnp.where(group == 0, low, high))
    return jnp.concatenate(rows, axis=0)


def pack_kernel(place_ref, cells_hbm, mass_hbm, message_ref, source_ref, mass_ref, sems):
    group = place_ref[1]
    cells = pltpu.make_async_copy(cells_hbm.at[group + 1], message_ref.at[:CELLS], sems.at[0])
    fetched = pltpu.make_async_copy(mass_hbm, mass_ref, sems.at[1])
    source = pltpu.make_async_copy(cells_hbm.at[group], source_ref, sems.at[2])
    fetched.start()
    cells.start()
    source.start()
    fetched.wait()
    masses = block_masses(mass_ref, group, 1) * LOG2E
    cells.wait()
    ones = jnp.ones((8, EMB), jnp.bfloat16)
    norms = []
    for pair in range(NBLK // 2):
        y = message_ref[pair * 256 : (pair + 1) * 256, :].astype(jnp.float32)
        square = y * y
        high = square.astype(jnp.bfloat16)
        low = (square - high.astype(jnp.float32)).astype(jnp.bfloat16)
        norm = sum(
            lax.dot_general(ones, part, (((1,), (1,)), ((), ())), preferred_element_type=jnp.float32)
            for part in (high, low)
        )
        norms += [norm[:1, :BLOCK], norm[:1, BLOCK:]]
    norms = jnp.concatenate(norms, axis=0) * SCALE
    for half, left in enumerate((masses - norms, masses + (LAM - 1.0) * norms)):
        parts = []
        for _ in range(3):
            part = left.astype(jnp.bfloat16).astype(jnp.float32)
            parts.append(part)
            left = left - part
        parts.append(jnp.zeros_like(left))
        packed = jnp.concatenate(parts, axis=0).astype(jnp.bfloat16)
        message_ref[CELLS:, half * BLOCK : (half + 1) * BLOCK] = packed
    source.wait()


def unpack(message_ref, window_ref, region):
    parts = message_ref[CELLS:, :].astype(jnp.float32)
    for half in range(2):
        p = parts[:, half * BLOCK : (half + 1) * BLOCK]
        total = (p[:NBLK] + p[NBLK : 2 * NBLK]) + p[2 * NBLK : 3 * NBLK]
        window_ref[half, region * NBLK : (region + 1) * NBLK, :] = total


STRIPS = BLOCK // 8


def extended(hh_ref, terms_ref):
    for t in range(WIN):
        terms_ref[t] = jnp.broadcast_to(hh_ref[t : t + 1, :], (8, BLOCK))
    terms_ref[WIN] = jnp.full((8, BLOCK), -BIG, jnp.float32)


def source_rows(s):
    if isinstance(s, int):
        return slice(s * BLOCK, (s + 1) * BLOCK)
    return pl.ds(pl.multiple_of(s * BLOCK, BLOCK), BLOCK)


def targets_at(table_ref, s, pair, count):
    return [table_ref[s * STRIDE + pair * 2 + k] for k in range(count)]


def over_targets(table_ref, s, step, start, eight):
    pairs = table_ref[PAIRS + s]

    def four(pair, so_far):
        return step(targets_at(table_ref, s, pair, 4), so_far)

    def keep(so_far):
        return so_far

    if eight:
        carried = lax.fori_loop(0, pairs >> 2, lambda i, c: four(4 * i + 2, four(4 * i, c)), start)
        carried = lax.cond((pairs & 2) != 0, lambda c: four((pairs >> 2) << 2, c), keep, carried)
    else:
        carried = lax.fori_loop(0, pairs >> 1, lambda i, c: four(2 * i, c), start)

    def two(so_far):
        return step(targets_at(table_ref, s, pairs - 1, 2), so_far)

    return lax.cond((pairs & 1) != 0, two, keep, carried)


def joined(combine, items):
    while len(items) > 1:
        items = [combine(a, b) for a, b in zip(items[::2], items[1::2])]
    return items[0]


def strips(g_ref, t, s):
    return g_ref[jnp.minimum(t, WIN - 1), source_rows(s), :].reshape(STRIPS, 8, BLOCK)


def over_sources(body):
    for s in range(NBLK):
        body(s)


def row_maxima(table_ref, terms_ref, g_ref, m_ref):
    @pl.loop(0, NBLK)
    def _(s):
        def step(ts, highest):
            v = [strips(g_ref, t, s) + terms_ref[t] for t in ts]
            return jnp.maximum(highest, joined(jnp.maximum, v))

        start = jnp.full((STRIPS, 8, BLOCK), -BIG, jnp.float32)
        highest = over_targets(table_ref, s, step, start, False)
        m_ref[source_rows(s), :] = highest.reshape(BLOCK, BLOCK)

    m_ref[...] = jnp.broadcast_to(jnp.max(m_ref[...], axis=1, keepdims=True), m_ref.shape)


def sweep_kernel(table_ref, hh_ref, kc_ref, g_ref, part_ref, terms_ref, top_ref, mass_ref, m_ref, acc_ref):
    extended(hh_ref, terms_ref)
    top_ref[...] = jnp.full(top_ref.shape, -BIG, jnp.float32)
    mass_ref[...] = jnp.zeros(mass_ref.shape, jnp.float32)

    @over_sources
    def _(s):
        def step(ts, carried):
            top, acc = carried
            v = [strips(g_ref, t, s) + terms_ref[t] for t in ts]
            high = jnp.maximum(top, joined(jnp.maximum, v))
            e = [jnp.exp2(part - high) for part in v]
            return high, acc * jnp.exp2(top - high) + joined(jnp.add, e)

        shape = (STRIPS, 8, BLOCK)
        start = jnp.full(shape, -BIG, jnp.float32), jnp.zeros(shape, jnp.float32)
        top, acc = over_targets(table_ref, s, step, start, True)
        m_ref[source_rows(s), :] = top.reshape(BLOCK, BLOCK)
        acc_ref[source_rows(s), :] = acc.reshape(BLOCK, BLOCK)

    tops = m_ref[...]
    high = jnp.max(tops, axis=1, keepdims=True)
    sums = jnp.sum(acc_ref[...] * jnp.exp2(tops - high), axis=1, keepdims=True)
    acc_ref[...] = kc_ref[...] - LAM * (high + LOG2E * jnp.log(sums))

    @over_sources
    def _(s):
        uu = acc_ref[source_rows(s), :].reshape(STRIPS, 8, BLOCK)
        pairs = table_ref[PAIRS + s]

        def columns(ts):
            tops = [top_ref[t] for t in ts]
            masses = [mass_ref[t] for t in ts]
            made = []
            for t, top, mass in zip(ts, tops, masses):
                v = strips(g_ref, t, s) + uu
                high = jnp.maximum(top, jnp.max(v, axis=0))
                made.append((high, mass * jnp.exp2(top - high) + jnp.sum(jnp.exp2(v - high), axis=0)))
            for t, (high, mass) in zip(ts, made):
                top_ref[t] = high
                mass_ref[t] = mass

        @pl.loop(0, pairs >> 2)
        def _(turn):
            columns(targets_at(table_ref, s, 4 * turn, 8))

        @pl.when((pairs & 2) != 0)
        def _():
            columns(targets_at(table_ref, s, (pairs >> 2) << 2, 4))

        @pl.when((pairs & 1) != 0)
        def _():
            columns(targets_at(table_ref, s, pairs - 1, 2))

    top = top_ref[:WIN]
    high = jnp.max(top, axis=1, keepdims=True)
    part_ref[0] = high[:, 0, :]
    part_ref[1] = jnp.sum(mass_ref[:WIN] * jnp.exp2(top - high), axis=1)


def weigh(table_ref, hh_ref, g_ref, w_ref, sum_ref, terms_ref, m_ref):
    extended(hh_ref, terms_ref)
    row_maxima(table_ref, terms_ref, g_ref, m_ref)

    @pl.loop(0, NBLK)
    def _(s):
        rows = source_rows(s)
        m = m_ref[rows, :].reshape(STRIPS, 8, BLOCK)

        def step(ts, acc):
            v = [jnp.exp2(strips(g_ref, t, s) + terms_ref[t] - m) for t in ts]
            for t, e in zip(ts, v):
                lanes = pl.ds(pl.multiple_of(t * BLOCK, BLOCK), BLOCK)
                w_ref[rows, lanes] = e.reshape(BLOCK, BLOCK).astype(jnp.bfloat16)
            return acc + joined(jnp.add, v)

        start = jnp.zeros((STRIPS, 8, BLOCK), jnp.float32)
        acc = over_targets(table_ref, s, step, start, False)
        sum_ref[rows, :] = acc.reshape(BLOCK, BLOCK)

    sum_ref[...] = jnp.broadcast_to(jnp.sum(sum_ref[...], axis=1, keepdims=True), sum_ref.shape)


def pulled(w_ref, rows, fate_refs, first):
    total = 0.0
    for region, fate_ref in enumerate(fate_refs, first):
        total += jnp.dot(
            w_ref[rows, region * CELLS : (region + 1) * CELLS],
            fate_ref[...],
            preferred_element_type=jnp.float32,
        )
    return total


def divided(total, sums):
    inverse = 1.0 / sums
    return (total * jnp.concatenate([inverse, inverse], axis=1)).astype(jnp.bfloat16)


def chunks(body):
    for chunk in range(2):
        body(slice(chunk * 512, (chunk + 1) * 512))


def near_kernel(place_ref, *refs):
    *slot_refs, mass_hbm, source_ref, own_ref, sib_ref = refs[: len(refs) - 6]
    g_ref, kc_ref, window_ref, table_ref, mass_ref, sem = refs[len(refs) - 6 :]
    group = place_ref[1]
    fetched = pltpu.make_async_copy(mass_hbm, mass_ref, sem)
    fetched.start()
    unpack(own_ref, window_ref, 0)
    unpack(sib_ref, window_ref, 1)

    def step(quarter, counts):
        return enter_slots(place_ref, group, slot_refs, table_ref, quarter, counts)

    zero = jnp.int32(0)
    counts = (zero, zero)
    for quarter in range(4):
        counts = step(quarter, counts)
    products(source_ref, (own_ref, sib_ref), g_ref, 0)
    close_table(table_ref, counts)
    fetched.wait()
    masses = block_masses(mass_ref, group, 0)
    for s in range(NBLK):
        x = source_ref[s * BLOCK : (s + 1) * BLOCK, :].astype(jnp.float32)
        norm = jnp.sum(x * x, axis=1, keepdims=True) * SCALE
        mass = jnp.broadcast_to(masses[s : s + 1, :], (BLOCK, BLOCK)).T
        kc_ref[s * BLOCK : (s + 1) * BLOCK, :] = mass * LOG2E + (LAM - 1.0) * norm


def far_kernel(table_ref, source_ref, out_ref, near_ref, near_window_ref, kc_ref, g_ref, window_ref, part_ref, *scratch):
    del near_ref
    window_ref[:, : 2 * NBLK, :] = near_window_ref[...]
    unpack(out_ref, window_ref, 2)
    products(source_ref, (out_ref,), g_ref, 2)
    sweep_kernel(table_ref, window_ref.at[0], kc_ref, g_ref, part_ref, *scratch)


def other_kernel(behind_ref, source_ref, own_ref, sib_ref, out_ref, g_ref):
    del behind_ref
    products(source_ref, (own_ref, sib_ref, out_ref), g_ref, 0)


def rest_kernel(place_ref, behind_ref, arrived_ref, *refs):
    del behind_ref, arrived_ref
    *slot_refs, cells_hbm, table_ref, source_ref, target_ref, sems = refs
    group = place_ref[1]
    copies = (
        pltpu.make_async_copy(cells_hbm.at[2 - group], target_ref, sems.at[0]),
        pltpu.make_async_copy(cells_hbm.at[1 - group], source_ref, sems.at[1]),
    )
    for copy in copies:
        copy.start()

    def step(quarter, counts):
        return enter_slots(place_ref, 1 - group, slot_refs, table_ref, quarter, counts)

    zero = jnp.int32(0)
    close_table(table_ref, lax.fori_loop(0, 4, step, (zero, zero)))
    for copy in copies:
        copy.wait()


def weigh_one(coupling, place_ref, mine, others, *outs):
    @pl.when(place_ref[1] == coupling)
    def _():
        weigh(*mine, *outs)

    @pl.when(place_ref[1] != coupling)
    def _():
        weigh(*others, *outs)


def blank_kernel(behind_ref, w_ref):
    del behind_ref

    @over_sources
    def _(s):
        w_ref[source_rows(s), :] = jnp.zeros((BLOCK, (WIN + 1) * BLOCK), jnp.bfloat16)


def late_kernel(place_ref, table_ref, hh_ref, g_ref, table2_ref, hh2_ref, g2_ref, own_ref, sib_ref, out_ref, blank_ref, late_ref, w_ref, sum_ref, terms_ref, m_ref):
    del blank_ref
    weigh_one(1, place_ref, (table_ref, hh_ref, g_ref), (table2_ref, hh2_ref, g2_ref), w_ref, sum_ref, terms_ref, m_ref)
    fates = (own_ref, sib_ref, out_ref)

    @chunks
    def _(rows):
        late_ref[rows, :] = divided(pulled(w_ref, rows, fates, 0), sum_ref[rows, :])


def early_weights_kernel(place_ref, table_ref, hh_ref, g_ref, table2_ref, hh2_ref, g2_ref, w_ref, sum_ref, terms_ref, m_ref):
    blank_kernel(None, w_ref)
    weigh_one(0, place_ref, (table_ref, hh_ref, g_ref), (table2_ref, hh2_ref, g2_ref), w_ref, sum_ref, terms_ref, m_ref)


def early_near_kernel(w_ref, own_ref, sib_ref, total_ref):
    @chunks
    def _(rows):
        total_ref[rows, :] = pulled(w_ref, rows, (own_ref, sib_ref), 0)


def early_kernel(w_ref, sum_ref, total_ref, out_ref, early_ref):
    @chunks
    def _(rows):
        total = total_ref[rows, :] + pulled(w_ref, rows, (out_ref,), 2)
        early_ref[rows, :] = divided(total, sum_ref[rows, :])


G_SHAPE = pltpu.VMEM((WIN, CELLS, BLOCK), jnp.float32)
PART_SHAPE = jax.ShapeDtypeStruct((2, WIN, BLOCK), jnp.float32)
W_SHAPE = jax.ShapeDtypeStruct((CELLS, (WIN + 1) * BLOCK), jnp.bfloat16)
COLUMN_SHAPE = jax.ShapeDtypeStruct((CELLS, BLOCK), jnp.float32)
FATE_SHAPE = jax.ShapeDtypeStruct((CELLS, EMB), jnp.bfloat16)
TOTAL_SHAPE = jax.ShapeDtypeStruct((CELLS, EMB), jnp.float32)
TERMS = pltpu.VMEM((WIN + 1, 8, BLOCK), jnp.float32)
COLUMN = pltpu.VMEM(COLUMN_SHAPE.shape, COLUMN_SHAPE.dtype)
SWEEP_SCRATCH = [TERMS] * 3 + [COLUMN] * 2


WINDOW_SHAPE = jax.ShapeDtypeStruct((2, WIN, BLOCK), jnp.float32)
NEAR_SHAPE = jax.ShapeDtypeStruct((2, 2 * NBLK, BLOCK), jnp.float32)


TABLE_SHAPE = jax.ShapeDtypeStruct((TABLE,), jnp.int32)
MESSAGE_SHAPE = jax.ShapeDtypeStruct((CELLS + 4 * NBLK, EMB), jnp.bfloat16)
MASSES = pltpu.VMEM((3, CELLS), jnp.float32)


def target_message(*args):
    scratch = [MASSES, pltpu.SemaphoreType.DMA((3,))]
    return call(pack_kernel, (MESSAGE_SHAPE, FATE_SHAPE), (VMEM, VMEM), [SMEM, HBM, HBM], scratch)(*args)


def near_products(place, slots, *args):
    outs = (G_SHAPE, COLUMN_SHAPE, NEAR_SHAPE, TABLE_SHAPE)
    in_specs = [SMEM] * (1 + len(slots)) + [HBM, VMEM, VMEM, VMEM]
    scratch = [MASSES, pltpu.SemaphoreType.DMA]
    return call(near_kernel, outs, (VMEM,) * 3 + (SMEM,), in_specs, scratch)(place, *slots, *args)


def far_products(*args):
    outs = (G_SHAPE, WINDOW_SHAPE, PART_SHAPE)
    return call(far_kernel, outs, (VMEM,) * 3, [SMEM] + [VMEM] * 5, SWEEP_SCRATCH, {3: 0})(*args)


def sweep(*args):
    return call(sweep_kernel, PART_SHAPE, VMEM, [SMEM] + [VMEM] * 3, SWEEP_SCRATCH)(*args)


def other_products(*args):
    return call(other_kernel, G_SHAPE, VMEM, [ANY] + [VMEM] * 4)(*args)


def other_inputs(place, behind, arrived, slots, *args):
    outs = (TABLE_SHAPE, FATE_SHAPE, FATE_SHAPE)
    in_specs = [SMEM, ANY, ANY] + [SMEM] * len(slots) + [HBM]
    scratch = [pltpu.SemaphoreType.DMA((2,))]
    return call(rest_kernel, outs, (SMEM, VMEM, VMEM), in_specs, scratch)(place, behind, arrived, *slots, *args)


COUPLINGS = [SMEM, SMEM, VMEM, VMEM, SMEM, VMEM, VMEM]


def blank_weights(behind):
    return call(blank_kernel, W_SHAPE, VMEM, [ANY])(behind)


def late_fates(*args):
    outs, in_specs = (FATE_SHAPE, W_SHAPE), COUPLINGS + [VMEM] * 4
    return call(late_kernel, outs, (VMEM, VMEM), in_specs, [COLUMN, TERMS, COLUMN], {10: 1})(*args)[0]


def early_weights(*args):
    return call(early_weights_kernel, (W_SHAPE, COLUMN_SHAPE), (VMEM, VMEM), COUPLINGS, [TERMS, COLUMN])(*args)


def early_near(*args):
    return call(early_near_kernel, TOTAL_SHAPE, VMEM, [VMEM] * 3)(*args)


def early_fates(*args):
    return call(early_kernel, FATE_SHAPE, VMEM, [VMEM] * 4)(*args)


def merged(first, second):
    highest = jnp.maximum(first[0], second[0])
    return jnp.stack(
        [
            highest,
            first[1] * jnp.exp2(first[0] - highest) + second[1] * jnp.exp2(second[0] - highest),
        ]
    )


def folded(part, beside):
    own = merged(part[:, :NBLK], sibling(part[:, NBLK : 2 * NBLK]))
    beyond = part[:, 2 * NBLK :]
    message = jnp.concatenate([own, beyond], axis=1)
    arrived, made = lax.optimization_barrier((outward(message), beside(message)))
    own = merged(own, arrived[:, NBLK:])
    out = merged(arrived[:, :NBLK], beyond)
    own_total = own[0] + jnp.log2(own[1])
    out_total = out[0] + jnp.log2(out[1])
    return jnp.concatenate([own_total, sibling(own_total), out_total], axis=0), made


def shifted(value, steps):
    count = lax.axis_size("tiles")
    return lax.ppermute(value, "tiles", [(t, (t + steps) % count) for t in range(count)])


def on_device(embeddings, log_mass, signatures, tile_list):
    owner = lax.axis_index("cells").astype(jnp.int32)
    group = (lax.axis_index("tiles") >= 2).astype(jnp.int32)
    place = jnp.stack([owner, group])

    cells, masses = (
        pltpu.with_memory_space_constraint(array, pltpu.HBM) for array in (embeddings, log_mass)
    )
    target, source = target_message(place, cells, masses)
    target_out, target_sib = outward(target), sibling(target)
    slots, fates, target_sib = lax.optimization_barrier((tile_list, signatures, target_sib))
    fates_out, fates_sib = outward(fates), sibling(fates)
    gathered = [pltpu.with_memory_space_constraint(tile_list, pltpu.HBM)] + [shifted(slots, k) for k in range(1, lax.axis_size("tiles"))]
    g, kc, near, table = near_products(place, gathered, masses, source, target, target_sib)
    g, window, part = far_products(table, source, target_out, g, near, kc)

    totals, (table_other, other_source, other) = folded(
        part, lambda message: other_inputs(place, message, fates_out, gathered, cells)
    )
    other_out, other_sib = outward(other), sibling(other)
    hh = window[1] - LAM * totals
    part = sweep(table, hh, kc, g)
    totals, g_other = folded(
        part, lambda message: other_products(message, other_source, other, other_sib, other_out)
    )
    hh = window[1] - LAM * totals
    couplings = (place, table, hh, g, table_other, mirrored(hh), g_other)
    late = late_fates(*couplings, signatures, fates_sib, fates_out, blank_weights(hh))
    late_out, late_sib = outward(late), sibling(late)
    weights, sums = early_weights(*couplings)
    total = early_near(weights, late, late_sib)
    early = early_fates(weights, sums, total, late_out)
    return early, late


def solution(mesh):
    in_specs = (
        P(None, "cells", None),
        P(None, "cells"),
        P("cells", None),
        P(None, None, ("cells", "tiles")),
    )
    out_specs = (P("cells", None), P("cells", None))
    return jax.shard_map(
        on_device, mesh=mesh, in_specs=in_specs, out_specs=out_specs, check_vma=False
    )
```
